128 devices in a mesh: ccd: 8 (over y, core), strip: 16 (over z, x).
Axes of the slice: x: 4, y: 4, z: 4, core: 2. Of those that a mesh axis runs over, the one named last changes fastest.
Arguments:
- tile_store: float32 [2304, 16, 128], P(('ccd', 'strip')), may hold values from -13 to 13
- tile_source: int32 [128, 18], replicated, may hold values from 0 to 127, as said below
- tile_slot: int32 [128, 18], replicated, may hold values from 0 to 17, as said below
- shift_cols: int32 [8], P('ccd'), may hold values from -117 to 117
- spatial_order: int32 [8], P('ccd'), may hold values from 0 to 2
- science: float32 [2048, 2048], P(('ccd', 'strip')), may hold values from -16 to 16
Outputs:
- difference: float32 [2048, 2048], P(('ccd', 'strip'))
The draws below stay inside these ranges and needn't reach their ends.
Inputs may be any that keep to these rules, and one draw needn't show every extreme that they name: `tile_source`: every device holds exactly 18 tiles over all strips, one device holds at most 1 tiles of one strip, and some device holds exactly 1 tiles of some strip. `tile_slot`: each position of each store is named by exactly one pair of strip and tile.
All inputs are finite; a program needn't handle non-finite values.
Results may differ from the reference program's by a relative error of at most 0.005.
Values sent between devices are 32-bit elements; how exact they have to be, the bound alone decides.
A program may use at most 64 MiB of HBM per device.

```python
import jax
import jax.numpy as jnp
from jax import lax

ROWS = 16
COLS = 2048
H = 11
CM = 128
TR = 16
TC = 128
RB = 4
NB = 27
NSP = 6
TW = 2304
TILES = 18
N_CCD = 8
N_STRIP = 16
DEVICES = 128


def gaussian_smooth(window, sigma_value, out_rows, out_cols):
    offsets = jnp.arange(-H, H + 1).astype(jnp.float32)
    weights = jnp.exp(-offsets * offsets / (2.0 * sigma_value * sigma_value))
    weights = weights / jnp.sum(weights)
    vertical = jnp.zeros((out_rows, window.shape[1]), jnp.float32)
    for tap_id in range(2 * H + 1):
        vertical = vertical + weights[tap_id] * window[tap_id:tap_id + out_rows, :]
    result = jnp.zeros((out_rows, out_cols), jnp.float32)
    for tap_id in range(2 * H + 1):
        result = result + weights[tap_id] * vertical[:, tap_id:tap_id + out_cols]
    return result


def shared_draw(key):
    key_perm = jax.random.fold_in(key, 11)
    key_devices = jax.random.fold_in(key, 12)
    key_order = jax.random.fold_in(key, 13)
    key_image = jax.random.fold_in(key, 14)
    key_shift = jax.random.fold_in(key, 15)
    key_noise = jax.random.fold_in(key, 16)
    per_dest = jax.vmap(lambda sub_key: jax.random.permutation(sub_key, TILES))(jax.random.split(key_perm, DEVICES))
    device_perm = jax.random.permutation(key_devices, DEVICES).astype(jnp.int32)
    residue = (per_dest.astype(jnp.int32) + jnp.arange(DEVICES, dtype=jnp.int32)[:, None]) % DEVICES
    owners = device_perm[residue].astype(jnp.int32)
    ranking = jax.random.permutation(key_order, DEVICES * TILES).astype(jnp.int32)
    composite = owners.reshape(-1) * (DEVICES * TILES) + ranking
    position = jnp.argsort(jnp.argsort(composite)).astype(jnp.int32)
    slots = (position - owners.reshape(-1) * TILES).reshape(DEVICES, TILES).astype(jnp.int32)
    images = 3.0 * jax.random.truncated_normal(key_image, -4.0, 4.0, (DEVICES, ROWS, TW), jnp.float32)
    random_shifts = jax.random.randint(key_shift, (N_CCD,), H - CM, CM - H + 1).astype(jnp.int32)
    ccd_ids = jnp.arange(N_CCD, dtype=jnp.int32)
    shifts = jnp.where(ccd_ids == 0, CM - H, jnp.where(ccd_ids == 1, H - CM, random_shifts)).astype(jnp.int32)
    tile_view = images.reshape(DEVICES, ROWS // TR, TR, TW // TC, TC).transpose(0, 1, 3, 2, 4).reshape(DEVICES * TILES, TR, TC)
    destination = (owners * TILES + slots).reshape(-1).astype(jnp.int32)
    inverse = jnp.argsort(destination, stable=True).astype(jnp.int32)
    store = jnp.take(tile_view, inverse, axis=0)
    total_rows = N_STRIP * ROWS
    ccd_images = images.reshape(N_CCD, total_rows, TW)
    padded = jnp.pad(ccd_images, ((0, 0), (H, H), (0, 0)))

    def one_ccd(padded_one, shift_one):
        window = lax.dynamic_slice_in_dim(padded_one, CM + shift_one - H, COLS + 2 * H, 1)
        return (gaussian_smooth(window, 1.3, total_rows, COLS), gaussian_smooth(window, 2.4, total_rows, COLS))
    sharp, broad = jax.vmap(one_ccd)(padded, shifts)
    horizontal_pos = 2.0 * (jnp.arange(COLS).astype(jnp.float32) + 0.5) / COLS - 1.0
    vertical_pos = 2.0 * (jnp.arange(total_rows).astype(jnp.float32) + 0.5) / total_rows - 1.0
    horizontal_grid = horizontal_pos[None, None, :]
    vertical_grid = vertical_pos[None, :, None]
    mixing = 0.5 + 0.3 * horizontal_grid + 0.3 * vertical_grid
    background = 0.4 + 0.3 * horizontal_grid - 0.2 * vertical_grid + 0.2 * horizontal_grid * vertical_grid
    noise = jax.random.truncated_normal(key_noise, -4.0, 4.0, (N_CCD, total_rows, COLS), jnp.float32)
    science = mixing * sharp + (1.0 - mixing) * broad + background + 0.3 * noise
    return (store, owners, slots, shifts, science.reshape(DEVICES * ROWS, COLS))


def draw_tile_store(key, part):
    return shared_draw(key)[0]


def draw_tile_source(key, part):
    return shared_draw(key)[1]


def draw_tile_slot(key, part):
    return shared_draw(key)[2]


def draw_shift_cols(key, part):
    return shared_draw(key)[3]


def draw_science(key, part):
    return shared_draw(key)[4]


def set_ends(drawn, stream_key, low, top_value):
    longest = drawn.shape.index(max(drawn.shape))
    spots = []
    for shift in (0, 1):
        where = [jax.random.randint(jax.random.fold_in(stream_key, axis), (), 0, length) for axis, length in enumerate(drawn.shape)]
        where[longest] = (where[longest] + shift) % drawn.shape[longest]
        spots.append(tuple(where))
    return drawn.at[spots[0]].set(low).at[spots[1]].set(top_value)


def setup_inputs(seed: int = 0) -> dict:
    streams_of = jax.random.split(jax.random.key(seed), 7)
    tile_store = draw_tile_store(jax.random.fold_in(streams_of[6], 71), 0)
    tile_source = draw_tile_source(jax.random.fold_in(streams_of[6], 71), 0)
    tile_slot = draw_tile_slot(jax.random.fold_in(streams_of[6], 71), 0)
    shift_cols = draw_shift_cols(jax.random.fold_in(streams_of[6], 71), 0)
    spatial_order = set_ends(jax.random.randint(streams_of[4], (N_CCD,), 0, 3), jax.random.fold_in(streams_of[4], 1), 0, 2).astype(jnp.int32)
    science = draw_science(jax.random.fold_in(streams_of[6], 71), 0)
    return dict(tile_store=tile_store, tile_source=tile_source, tile_slot=tile_slot, shift_cols=shift_cols, spatial_order=spatial_order, science=science)


gauss_sigmas = (0.7, 1.5, 3.0)
poly_degrees = (4, 2, 2)
mono_degrees = (0, 1, 1, 2, 2, 2)
ridge_weight = 0.05

def tap_table(half_width):
    offsets = jnp.arange(-half_width, half_width + 1).astype(jnp.float32)
    table_rows = []
    for sigma_value, top_degree in zip(gauss_sigmas, poly_degrees):
        envelope = jnp.exp(-offsets * offsets / (2.0 * sigma_value * sigma_value))
        envelope_sum = jnp.sum(envelope)
        for power_of in range(top_degree + 1):
            table_rows.append(envelope * (offsets / sigma_value) ** power_of / envelope_sum)
    return jnp.stack(table_rows)

def band_tables(tap_rows, half_width, block_rows):
    tap_count = 2 * half_width + 1
    out_pos = jnp.arange(block_rows)[:, None]
    in_pos = jnp.arange(block_rows + 2 * half_width)[None, :]
    onehot = ((in_pos - out_pos)[:, :, None] == jnp.arange(tap_count)[None, None, :]).astype(jnp.float32)
    band_rows = []
    first_row = 0
    for top_degree in poly_degrees:
        group_taps = tap_rows[first_row:first_row + top_degree + 1]
        band_rows.append(jnp.einsum('rka,ja->jrk', onehot, group_taps, precision=lax.Precision.HIGHEST).astype(jnp.bfloat16))
        first_row += top_degree + 1
    return band_rows

def horizontal_pass(window, tap_rows, out_cols):
    outputs = []
    tap_count = tap_rows.shape[1]
    for filter_id in range(tap_rows.shape[0]):
        taps_now = tap_rows[filter_id]

        def add_tap(tap_id, running, taps_now=taps_now):
            return running + taps_now[tap_id] * lax.dynamic_slice_in_dim(window, tap_id, out_cols, 1)
        summed = lax.fori_loop(0, tap_count, add_tap, jnp.zeros((window.shape[0], out_cols), jnp.float32))
        outputs.append(summed.astype(jnp.bfloat16))
    groups = []
    first_row = 0
    for top_degree in poly_degrees:
        groups.append(jnp.stack(outputs[first_row:first_row + top_degree + 1]))
        first_row += top_degree + 1
    return groups

def block_basis(groups, band_rows, start_row, block_rows, half_width):
    pieces = []
    for group_id, top_degree in enumerate(poly_degrees):
        rows_in = lax.dynamic_slice_in_dim(groups[group_id], start_row, block_rows + 2 * half_width, 1)
        mixed = jnp.einsum('jrk,ikx->ijrx', band_rows[group_id].astype(jnp.float32), rows_in.astype(jnp.float32), precision=lax.Precision.HIGHEST).astype(jnp.bfloat16)
        for horiz_degree in range(top_degree + 1):
            pieces.append(mixed[horiz_degree, :top_degree + 1 - horiz_degree])
    return jnp.concatenate(pieces, axis=0)

def monomials(first_row, block_rows, total_rows, col_count):
    row_pos = (first_row + jnp.arange(block_rows)).astype(jnp.float32)
    vertical_pos = 2.0 * (row_pos + 0.5) / total_rows - 1.0
    horizontal_pos = 2.0 * (jnp.arange(col_count).astype(jnp.float32) + 0.5) / col_count - 1.0
    vertical_grid = jnp.broadcast_to(vertical_pos[:, None], (block_rows, col_count))
    horizontal_grid = jnp.broadcast_to(horizontal_pos[None, :], (block_rows, col_count))
    ones_grid = jnp.ones((block_rows, col_count), jnp.float32)
    return jnp.stack([ones_grid, horizontal_grid, vertical_grid, horizontal_grid * horizontal_grid, horizontal_grid * vertical_grid, vertical_grid * vertical_grid])

def design_rows(basis_block, mono_grid):
    kernel_part = (basis_block.astype(jnp.float32)[:, None] * mono_grid[None]).astype(jnp.bfloat16)
    kernel_part = kernel_part.reshape(basis_block.shape[0] * mono_grid.shape[0], -1)
    back_part = mono_grid.astype(jnp.bfloat16).reshape(mono_grid.shape[0], -1)
    return jnp.concatenate([kernel_part, back_part], axis=0)

def solve_kernel(gram_total, rhs_total, order_value, basis_count):
    degree_list = jnp.array(mono_degrees, dtype=jnp.int32)
    kernel_on = (degree_list <= order_value.astype(jnp.int32)).astype(jnp.float32)
    active = jnp.concatenate([jnp.tile(kernel_on, basis_count), jnp.ones((len(mono_degrees),), jnp.float32)])
    masked = gram_total * active[:, None] * active[None, :] + jnp.diag(1.0 - active)
    system = masked + ridge_weight * jnp.diag(jnp.diag(masked))
    lower = jnp.linalg.cholesky(system)
    middle = jax.scipy.linalg.solve_triangular(lower, rhs_total * active, lower=True)
    return jax.scipy.linalg.solve_triangular(lower.T, middle, lower=False)

def block_difference(basis_block, mono_grid, coeffs, science_block, basis_count):
    spatial_count = mono_grid.shape[0]
    kernel_coef = coeffs[:basis_count * spatial_count].reshape(basis_count, spatial_count)
    back_coef = coeffs[basis_count * spatial_count:]
    weights = jnp.zeros((basis_count,) + mono_grid.shape[1:], jnp.float32)
    background = jnp.zeros(mono_grid.shape[1:], jnp.float32)
    for mono_id in range(spatial_count):
        weights = weights + kernel_coef[:, mono_id, None, None] * mono_grid[mono_id][None]
        background = background + back_coef[mono_id] * mono_grid[mono_id]
    model_image = jnp.sum(basis_block.astype(jnp.float32) * weights, axis=0) + background
    return science_block - model_image

def reference(tile_store, tile_source, tile_slot, shift_cols, spatial_order, science):
    device_count = tile_source.shape[0]
    tile_count = tile_source.shape[1]
    flat_pick = (tile_source.astype(jnp.int32) * tile_count + tile_slot.astype(jnp.int32)).reshape(-1)
    gathered = jnp.take(tile_store, flat_pick, axis=0)
    images = gathered.reshape(device_count, ROWS // TR, TW // TC, TR, TC).transpose(0, 1, 3, 2, 4)
    images = images.reshape(N_CCD, N_STRIP * ROWS, TW)
    total_rows = N_STRIP * ROWS
    science_ccd = science.reshape(N_CCD, total_rows, COLS)
    tap_rows = tap_table(H)
    band_rows = band_tables(tap_rows, H, RB)
    block_count = total_rows // RB
    param_count = NB * NSP + NSP

    def per_ccd(inputs):
        image_rows, science_rows, shift_value, order_value = inputs
        padded = jnp.pad(image_rows, ((H, H), (0, 0)))
        start_col = (CM + shift_value.astype(jnp.int32) - H).astype(jnp.int32)
        window = lax.dynamic_slice_in_dim(padded, start_col, COLS + 2 * H, 1)
        groups = horizontal_pass(window, tap_rows, COLS)

        def gram_step(carry_pair, block_id):
            start_row = (block_id * RB).astype(jnp.int32)
            basis_block = block_basis(groups, band_rows, start_row, RB, H)
            mono_grid = monomials(start_row, RB, total_rows, COLS)
            design = design_rows(basis_block, mono_grid).astype(jnp.float32)
            target = lax.dynamic_slice_in_dim(science_rows, start_row, RB, 0).astype(jnp.bfloat16).astype(jnp.float32).reshape(-1)
            gram_part = jnp.dot(design, design.T, precision=lax.Precision.HIGHEST)
            rhs_part = jnp.dot(design, target, precision=lax.Precision.HIGHEST)
            return ((carry_pair[0] + gram_part, carry_pair[1] + rhs_part), None)
        start_pair = (jnp.zeros((param_count, param_count), jnp.float32), jnp.zeros((param_count,), jnp.float32))
        (gram_total, rhs_total), _ = lax.scan(gram_step, start_pair, jnp.arange(block_count).astype(jnp.int32))
        coeffs = solve_kernel(gram_total, rhs_total, order_value, NB)

        def diff_block(block_id):
            start_row = (block_id * RB).astype(jnp.int32)
            basis_block = block_basis(groups, band_rows, start_row, RB, H)
            mono_grid = monomials(start_row, RB, total_rows, COLS)
            science_block = lax.dynamic_slice_in_dim(science_rows, start_row, RB, 0)
            return block_difference(basis_block, mono_grid, coeffs, science_block, NB)
        return lax.map(diff_block, jnp.arange(block_count).astype(jnp.int32)).reshape(total_rows, COLS)
    result = lax.map(per_ccd, (images, science_ccd, shift_cols, spatial_order))
    return result.reshape(N_CCD * total_rows, COLS)
```

```python
import jax
import jax.numpy as jnp
import numpy as np
from jax import lax
from jax.experimental import pallas as pl
from jax.experimental.pallas import tpu as pltpu
from jax.sharding import PartitionSpec as P

H = 11
CM = 128
ROWS = 16
COLS = 2048
TC = 128
SLOTS = 40
TARGET = 28
ONES = 15

sigmas = (0.7, 1.5, 3.0)
tops = (4, 2, 2)
mono = ((0, 0), (1, 0), (0, 1), (2, 0), (1, 1), (0, 2))
ridge = 0.05
F32 = jnp.float32
BF16 = jnp.bfloat16


def tap_table():
    a = np.arange(-H, H + 1).astype(np.float64)
    rows = []
    for s, top in zip(sigmas, tops):
        e = np.exp(-a * a / (2.0 * s * s))
        for n in range(top + 1):
            rows.append(e * (a / s) ** n / e.sum())
    return np.stack(rows).astype(np.float32)


def to_bf16(x):
    return x.astype(jnp.bfloat16.dtype)


def band_matrix():
    taps = tap_table()
    hi = to_bf16(taps).astype(np.float32)
    lo = to_bf16(taps - hi).astype(np.float32)
    full = []
    for part in (hi, lo):
        m = np.zeros((160, 11, TC), np.float32)
        for f in range(11):
            for x in range(TC):
                m[x : x + 23, f, x] = part[f]
        full.append(m.reshape(160, 11 * TC))
    h, l = full
    tail = np.zeros((TC, 11 * TC), np.float32)
    tail[0:32], tail[32:64], tail[64:96] = h[128:], h[128:], l[128:]
    return to_bf16(np.concatenate([h[:128], h[:128], l[:128], tail]))


def slot_of(row):
    return 16 + row if row < H else (row - H if row < H + ROWS else row)


def vertical_matrices():
    taps = to_bf16(tap_table()).astype(np.float32)
    first = np.zeros((ROWS, 16, 208), np.float32)
    second = np.zeros((ROWS, 16, 240), np.float32)
    slot = 0
    for i in range(5):
        for j in range(5 - i):
            for r in range(ROWS):
                for a in range(23):
                    first[r, slot, i * SLOTS + slot_of(r + a)] = taps[j, a]
            slot += 1
    first[:, ONES, 38] = 1.0
    slot = 0
    for g in range(2):
        for i in range(3):
            for j in range(3 - i):
                for r in range(ROWS):
                    for a in range(23):
                        second[r, slot, (3 * g + i) * SLOTS + slot_of(r + a)] = taps[5 + 3 * g + j, a]
                slot += 1
    return to_bf16(first.reshape(256, 208)), to_bf16(second.reshape(256, 240))


def column_powers():
    u = 2.0 * (np.arange(COLS).astype(np.float32) + np.float32(0.5)) / np.float32(COLS) - np.float32(1.0)
    u = u.astype(np.float32)
    return np.stack([u, u * u] + [np.zeros_like(u)] * 6)


def fit_kernel(scal, own, above, below, sci, band, va, vb, upow, e_out, mom_out, rolled, hs, acc):
    shift = scal[0]
    first_row = scal[1]
    start = CM + shift - H
    tile = lax.shift_right_logical(start, 7)
    rem = lax.bitwise_and(start, 127)
    count = own.shape[0]
    row16 = lax.broadcasted_iota(jnp.int32, (1, 16, TC), 1)
    row8 = lax.broadcasted_iota(jnp.int32, (1, 8, TC), 1)
    a = pltpu.roll(above[...], H, 1)
    b = pltpu.roll(below[...], H, 1)
    mid = jnp.where(row16 < H, a, b)
    end = jnp.where(row8 < 6, b[:, :8], jnp.where(row8 == 6, 1.0, 0.0))
    x = jnp.concatenate([own[...], mid, end], axis=1)
    rolled[0:count] = pltpu.roll(x, lax.bitwise_and(128 - rem, 127), 2)
    rolled[count : count + 1] = jnp.zeros((1, SLOTS, TC), F32)
    lane3 = lax.broadcasted_iota(jnp.int32, (1, SLOTS, TC), 2)
    w = jnp.where(
        lane3 < 128 - rem, rolled[pl.ds(tile, 17)], rolled[pl.ds(tile + 1, 17)]
    ).reshape(17 * SLOTS, TC)
    main = w[: 16 * SLOTS]
    nxt = w[SLOTS:]
    hi = main.astype(BF16)
    lo = (main - hi.astype(F32)).astype(BF16)
    nhi = nxt.astype(BF16).astype(F32)
    nlo = nxt - nhi
    lane = lax.broadcasted_iota(jnp.int32, (1, TC), 1)
    tail = jnp.where(
        lane < 32,
        nhi,
        jnp.where(lane < 64, pltpu.roll(nlo, 32, 1), jnp.where(lane < 96, pltpu.roll(nhi, 64, 1), 0.0)),
    ).astype(BF16)
    lhs = jnp.concatenate([hi, lo, hi, tail], axis=1)
    for c in range(6):
        n = 256 if c < 5 else 128
        res = jnp.dot(lhs, band[:, 256 * c : 256 * c + n], preferred_element_type=F32)
        for f in range(2 * c, 2 * c + n // TC):
            o = (f - 2 * c) * TC
            for j in range(16):
                hs[f * SLOTS : (f + 1) * SLOTS, j * TC : (j + 1) * TC] = res[
                    j * SLOTS : (j + 1) * SLOTS, o : o + TC
                ]
    for c in range(8):
        cols = slice(256 * c, 256 * c + 256)
        oa = jnp.dot(va[...], hs[0:208, cols].astype(BF16), preferred_element_type=F32)
        ob = jnp.dot(vb[...], hs[200:440, cols].astype(BF16), preferred_element_type=F32)
        e = jnp.concatenate([oa.reshape(ROWS, 16, 256), ob.reshape(ROWS, 16, 256)], axis=1)
        e_out[:, cols] = e.reshape(ROWS * 32, 256).astype(BF16)
    acc[...] = jnp.zeros_like(acc)
    u1 = upow[0:1, :]
    u2 = upow[1:2, :]
    brow = lax.broadcasted_iota(jnp.int32, (32, 1), 0)

    def row_step(r, carry):
        e = e_out[pl.ds(pl.multiple_of(r * 32, 32), 32), :].astype(F32)
        e = jnp.where(brow == TARGET, sci[pl.ds(r, 1), :], e)
        e16 = e.astype(BF16)
        e = e16.astype(F32)
        f1 = (e * u1).astype(BF16)
        f2 = (e * u2).astype(BF16)
        g = lax.dot_general(
            jnp.concatenate([e16, f2], axis=0),
            jnp.concatenate([e16, f1, f2], axis=0),
            (((1,), (1,)), ((), ())),
            preferred_element_type=F32,
        )
        v = (first_row + r).astype(F32) * (2.0 / 256.0) + (1.0 / 256.0 - 1.0)
        scale = 1.0
        for m in range(5):
            n = 64 if m < 2 else 32
            acc[m, 0:n, 0:96] += g[0:n] * scale
            scale = scale * v
        return carry

    lax.fori_loop(0, ROWS, row_step, 0)
    units = (
        jnp.where(lane < 96, acc[0, 0:32], pltpu.roll(acc[0, 32:64], 64, 1)),
        jnp.where(lane < 96, acc[1, 0:32], pltpu.roll(acc[1, 32:64], 64, 1)),
        jnp.where(lane < 96, acc[2, 0:32], pltpu.roll(acc[0, 32:64], 32, 1)),
        jnp.where(lane < 64, acc[3, 0:32], pltpu.roll(acc[4, 0:32], 64, 1)),
    )
    for i, unit in enumerate(units):
        mom_out[32 * i : 32 * i + 32] = unit


def unit_of(k, m):
    if m < 2 and k < 4:
        return m, k
    if m == 2:
        return 2, k
    return {(4, 0): (2, 3), (0, 3): (3, 0), (1, 3): (3, 1), (0, 4): (3, 2)}[(k, m)]


def apply_kernel(scal, moms, e_ref, sci, upow, out, mat, fx):
    order = scal[2]
    first_row = scal[1]
    total = moms[0]
    for i in range(1, moms.shape[0]):
        total = total + moms[i]
    units = [total[32 * i : 32 * i + 32] for i in range(4)]
    lane = lax.broadcasted_iota(jnp.int32, (1, TC), 1)
    row = lax.broadcasted_iota(jnp.int32, (32, 1), 0)
    degree = lambda q: 0 if q == 0 else (1 if q < 3 else 2)

    def col_active(t):
        q = lax.shift_right_logical(lane, 5) + 4 * t
        deg = jnp.where(q >= 1, 1, 0) + jnp.where(q >= 3, 1, 0)
        return (deg <= order) | (lax.bitwise_and(lane, 31) == ONES)

    for q in range(6):
        row_on = (degree(q) <= order) | (row == ONES)
        for t in range(2):
            block = jnp.zeros((32, TC), F32)
            for s in range(4 if t == 0 else 2):
                p = 4 * t + s
                i, k = unit_of(mono[q][0] + mono[p][0], mono[q][1] + mono[p][1])
                piece = units[i]
                if s != k:
                    piece = pltpu.roll(piece, (32 * (s - k)) % 128, 1)
                block = jnp.where(lax.shift_right_logical(lane, 5) == s, piece, block)
            both = row_on & col_active(t)
            block = jnp.where(both, block, 0.0)
            if t == q // 4:
                diag = lane == row + 32 * (q % 4)
                block = jnp.where(diag, jnp.where(both, block, 1.0) * (1.0 + ridge), block)
            mat[32 * q : 32 * q + 32, TC * t : TC * t + TC] = block
            if q == 0:
                mat[192:200, TC * t : TC * t + TC] = jnp.where(col_active(t), block[24:32], 0.0)
    wide = lax.broadcasted_iota(jnp.int32, (1, 2 * TC), 1)
    for q in range(6):
        t = q // 4
        top = 32 * q
        base = 32 * (q % 4)

        def sweep(b, carry, t=t, top=top, base=base):
            panel = mat[top : top + 32, :]
            prow = mat[pl.ds(top + b, 1), :]
            at = lane == base + b
            col = jnp.sum(
                jnp.where(at, panel[:, TC * t : TC * t + TC], 0.0), axis=1, keepdims=True
            )
            d = jnp.sum(jnp.where(at, prow[:, TC * t : TC * t + TC], 0.0), axis=1, keepdims=True)
            inv = 1.0 / d
            here = row == b
            g = jnp.where(here, -1.0, col) * inv
            atw = wide == TC * t + base + b
            mat[top : top + 32, :] = jnp.where(atw | here, 0.0, panel) - g * jnp.where(atw, 1.0, prow)
            return carry

        lax.fori_loop(0, 28, sweep, 0)
        panel = mat[top : top + 32, :]
        local = wide - (TC * t + base)
        inside = (local >= 0) & (local < 28)
        f = jnp.where(row < 28, jnp.where(inside, -panel, panel), 0.0)
        fx[...] = jnp.zeros_like(fx)
        fx[base : base + 32, :] = f
        rest = mat[top + 32 : 200, :]
        mat[top + 32 : 200, :] = jnp.where(inside, 0.0, rest) - jnp.dot(
            rest[:, TC * t : TC * t + TC],
            fx[...],
            preferred_element_type=F32,
            precision=lax.Precision.HIGHEST,
        )
    coef = []
    for q in range(6):
        z = mat[192:200, TC * (q // 4) : TC * (q // 4) + TC]
        z = jnp.broadcast_to(z[TARGET - 24 : TARGET - 23], (8, TC))
        if q % 4:
            z = pltpu.roll(z, 128 - 32 * (q % 4), 1)
        z = jnp.where(lane < 28, z, 0.0)
        z = z + pltpu.roll(z, 32, 1)
        z = z + pltpu.roll(z, 64, 1)
        coef.append(jnp.concatenate([z, z], axis=0))
    row16 = lax.broadcasted_iota(jnp.int32, (16, 1), 0)
    v = (first_row + row16).astype(F32) * (2.0 / 256.0) + (1.0 / 256.0 - 1.0)
    parts = (coef[0] + v * (coef[2] + v * coef[5]), coef[1] + v * coef[4], coef[3])
    his, los = [], []
    for p in parts:
        wide_p = jnp.concatenate(
            [jnp.where(row16 == 4 * n + lax.shift_right_logical(lane, 5), p, 0.0) for n in range(4)],
            axis=1,
        )
        h = wide_p.astype(BF16)
        his.append(h)
        los.append((wide_p - h.astype(F32)).astype(BF16))
    res = jnp.dot(jnp.concatenate(his + los, axis=0), e_ref[...], preferred_element_type=F32)
    t0, t1, t2 = (res[16 * i : 16 * i + 16] + res[48 + 16 * i : 64 + 16 * i] for i in range(3))
    u = upow[0:1, :]
    out[...] = sci[...] - (t0 + u * (t1 + u * t2))


VM = pl.BlockSpec(memory_space=pltpu.VMEM)
SM = pl.BlockSpec(memory_space=pltpu.SMEM)
LIMIT = 60 * 1024 * 1024


def fit(scal, own, above, below, sci):
    band = jnp.asarray(band_matrix())
    va, vb = (jnp.asarray(m) for m in vertical_matrices())
    upow = jnp.asarray(column_powers())
    return pl.pallas_call(
        fit_kernel,
        out_shape=(
            jax.ShapeDtypeStruct((ROWS * 32, COLS), BF16),
            jax.ShapeDtypeStruct((128, TC), F32),
        ),
        in_specs=[SM] + [VM] * 8,
        out_specs=(VM, VM),
        scratch_shapes=[
            pltpu.VMEM((own.shape[0] + 1, SLOTS, TC), F32),
            pltpu.VMEM((440, COLS), F32),
            pltpu.VMEM((5, 64, TC), F32),
        ],
        compiler_params=pltpu.CompilerParams(vmem_limit_bytes=LIMIT),
        name="fit",
    )(scal, own, above, below, sci, band, va, vb, upow)


def apply(scal, moms, e, sci):
    upow = jnp.asarray(column_powers())
    return pl.pallas_call(
        apply_kernel,
        out_shape=jax.ShapeDtypeStruct((ROWS, COLS), F32),
        in_specs=[SM] + [VM] * 4,
        out_specs=VM,
        scratch_shapes=[pltpu.VMEM((200, 2 * TC), F32), pltpu.VMEM((TC, 2 * TC), F32)],
        compiler_params=pltpu.CompilerParams(vmem_limit_bytes=LIMIT),
        name="apply",
    )(scal, moms, e, sci, upow)


def body(tile_store, tile_source, tile_slot, shift_cols, spatial_order, science):
    strips = lax.axis_size("strip")
    strip = lax.axis_index("strip")
    me = lax.axis_index("ccd") * strips + strip
    pick = jnp.sum(jnp.where(tile_source == me, tile_slot, 0), axis=1)
    outgoing = jnp.take(tile_store, pick, axis=0)
    arrived = lax.all_to_all(outgoing, ("ccd", "strip"), split_axis=0, concat_axis=0, tiled=True)
    owner = lax.dynamic_index_in_dim(tile_source, me, 0, keepdims=False)
    own = jnp.take(arrived, owner, axis=0)
    above = lax.ppermute(own, "strip", [(i, i + 1) for i in range(strips - 1)])
    below = lax.ppermute(own, "strip", [(i + 1, i) for i in range(strips - 1)])
    scal = jnp.stack([shift_cols[0], strip * ROWS, spatial_order[0]]).astype(jnp.int32)
    e, mom = fit(scal, own, above, below, science)
    moms = lax.all_to_all(
        jnp.broadcast_to(mom[None], (strips, *mom.shape)), "strip", 0, 0, tiled=True
    )
    return apply(scal, moms, e, science)


def solution(mesh):
    placed = (
        P(("ccd", "strip"), None, None),
        P(),
        P(),
        P("ccd"),
        P("ccd"),
        P(("ccd", "strip"), None),
    )
    return jax.shard_map(
        body, mesh=mesh, in_specs=placed, out_specs=P(("ccd", "strip"), None), check_vma=False
    )
```

```python
import jax
import jax.numpy as jnp
import numpy as np
from jax import lax
from jax.experimental import pallas as pl
from jax.experimental.pallas import tpu as pltpu
from jax.sharding import PartitionSpec as P

H = 11
CM = 128
ROWS = 16
COLS = 2048
TC = 128
SLOTS = 40
TARGET = 28
ONES = 15

sigmas = (0.7, 1.5, 3.0)
tops = (4, 2, 2)
mono = ((0, 0), (1, 0), (0, 1), (2, 0), (1, 1), (0, 2))
ridge = 0.05
F32 = jnp.float32
BF16 = jnp.bfloat16


def tap_table():
    a = np.arange(-H, H + 1).astype(np.float64)
    rows = []
    for s, top in zip(sigmas, tops):
        e = np.exp(-a * a / (2.0 * s * s))
        for n in range(top + 1):
            rows.append(e * (a / s) ** n / e.sum())
    return np.stack(rows).astype(np.float32)


def to_bf16(x):
    return x.astype(jnp.bfloat16.dtype)


def band_matrix():
    taps = tap_table()
    hi = to_bf16(taps).astype(np.float32)
    lo = to_bf16(taps - hi).astype(np.float32)
    full = []
    for part in (hi, lo):
        m = np.zeros((160, 11, TC), np.float32)
        for f in range(11):
            for x in range(TC):
                m[x : x + 23, f, x] = part[f]
        full.append(m.reshape(160, 11 * TC))
    h, l = full
    tail = np.zeros((TC, 11 * TC), np.float32)
    tail[0:32], tail[32:64], tail[64:96] = h[128:], h[128:], l[128:]
    return to_bf16(np.concatenate([h[:128], h[:128], l[:128], tail]))


def slot_of(row):
    return 16 + row if row < H else (row - H if row < H + ROWS else row)


def vertical_matrices():
    taps = to_bf16(tap_table()).astype(np.float32)
    first = np.zeros((ROWS, 16, 208), np.float32)
    second = np.zeros((ROWS, 16, 240), np.float32)
    slot = 0
    for i in range(5):
        for j in range(5 - i):
            for r in range(ROWS):
                for a in range(23):
                    first[r, slot, i * SLOTS + slot_of(r + a)] = taps[j, a]
            slot += 1
    first[:, ONES, 38] = 1.0
    slot = 0
    for g in range(2):
        for i in range(3):
            for j in range(3 - i):
                for r in range(ROWS):
                    for a in range(23):
                        second[r, slot, (3 * g + i) * SLOTS + slot_of(r + a)] = taps[5 + 3 * g + j, a]
                slot += 1
    return to_bf16(first.reshape(256, 208)), to_bf16(second.reshape(256, 240))


def column_powers():
    u = 2.0 * (np.arange(COLS).astype(np.float32) + np.float32(0.5)) / np.float32(COLS) - np.float32(1.0)
    u = u.astype(np.float32)
    return np.stack([u, u * u] + [np.zeros_like(u)] * 6)


def fit_kernel(scal, own, above, below, sci, band, va, vb, upow, e_out, mom_out, rolled, hs, acc):
    shift = scal[0]
    first_row = scal[1]
    start = CM + shift - H
    tile = lax.shift_right_logical(start, 7)
    rem = lax.bitwise_and(start, 127)
    count = own.shape[0]
    row16 = lax.broadcasted_iota(jnp.int32, (1, 16, TC), 1)
    row8 = lax.broadcasted_iota(jnp.int32, (1, 8, TC), 1)
    a = pltpu.roll(above[...], H, 1)
    b = pltpu.roll(below[...], H, 1)
    mid = jnp.where(row16 < H, a, b)
    end = jnp.where(row8 < 6, b[:, :8], jnp.where(row8 == 6, 1.0, 0.0))
    x = jnp.concatenate([own[...], mid, end], axis=1)
    rolled[0:count] = pltpu.roll(x, lax.bitwise_and(128 - rem, 127), 2)
    rolled[count : count + 1] = jnp.zeros((1, SLOTS, TC), F32)
    lane3 = lax.broadcasted_iota(jnp.int32, (1, SLOTS, TC), 2)
    w = jnp.where(
        lane3 < 128 - rem, rolled[pl.ds(tile, 17)], rolled[pl.ds(tile + 1, 17)]
    ).reshape(17 * SLOTS, TC)
    main = w[: 16 * SLOTS]
    nxt = w[SLOTS:]
    hi = main.astype(BF16)
    lo = (main - hi.astype(F32)).astype(BF16)
    nhi = nxt.astype(BF16).astype(F32)
    nlo = nxt - nhi
    lane = lax.broadcasted_iota(jnp.int32, (1, TC), 1)
    tail = jnp.where(
        lane < 32,
        nhi,
        jnp.where(lane < 64, pltpu.roll(nlo, 32, 1), jnp.where(lane < 96, pltpu.roll(nhi, 64, 1), 0.0)),
    ).astype(BF16)
    lhs = jnp.concatenate([hi, lo, hi, tail], axis=1)
    for c in range(6):
        n = 256 if c < 5 else 128
        res = jnp.dot(lhs, band[:, 256 * c : 256 * c + n], preferred_element_type=F32)
        for f in range(2 * c, 2 * c + n // TC):
            o = (f - 2 * c) * TC
            for j in range(16):
                hs[f * SLOTS : (f + 1) * SLOTS, j * TC : (j + 1) * TC] = res[
                    j * SLOTS : (j + 1) * SLOTS, o : o + TC
                ]
    for c in range(8):
        cols = slice(256 * c, 256 * c + 256)
        oa = jnp.dot(va[...], hs[0:208, cols].astype(BF16), preferred_element_type=F32)
        ob = jnp.dot(vb[...], hs[200:440, cols].astype(BF16), preferred_element_type=F32)
        e = jnp.concatenate([oa.reshape(ROWS, 16, 256), ob.reshape(ROWS, 16, 256)], axis=1)
        e_out[:, cols] = e.reshape(ROWS * 32, 256).astype(BF16)
    acc[...] = jnp.zeros_like(acc)
    u1 = upow[0:1, :]
    u2 = upow[1:2, :]
    brow = lax.broadcasted_iota(jnp.int32, (32, 1), 0)

    def row_step(r, carry):
        e = e_out[pl.ds(pl.multiple_of(r * 32, 32), 32), :].astype(F32)
        e = jnp.where(brow == TARGET, sci[pl.ds(r, 1), :], e)
        e16 = e.astype(BF16)
        e = e16.astype(F32)
        f1 = (e * u1).astype(BF16)
        f2 = (e * u2).astype(BF16)
        g = lax.dot_general(
            jnp.concatenate([e16, f2], axis=0),
            jnp.concatenate([e16, f1, f2], axis=0),
            (((1,), (1,)), ((), ())),
            preferred_element_type=F32,
        )
        v = (first_row + r).astype(F32) * (2.0 / 256.0) + (1.0 / 256.0 - 1.0)
        scale = 1.0
        for m in range(5):
            n = 64 if m < 2 else 32
            acc[m, 0:n, 0:96] += g[0:n] * scale
            scale = scale * v
        return carry

    lax.fori_loop(0, ROWS, row_step, 0)
    units = (
        jnp.where(lane < 96, acc[0, 0:32], pltpu.roll(acc[0, 32:64], 64, 1)),
        jnp.where(lane < 96, acc[1, 0:32], pltpu.roll(acc[1, 32:64], 64, 1)),
        jnp.where(lane < 96, acc[2, 0:32], pltpu.roll(acc[0, 32:64], 32, 1)),
        jnp.where(lane < 64, acc[3, 0:32], pltpu.roll(acc[4, 0:32], 64, 1)),
    )
    for i, unit in enumerate(units):
        mom_out[32 * i : 32 * i + 32] = unit


def unit_of(k, m):
    if m < 2 and k < 4:
        return m, k
    if m == 2:
        return 2, k
    return {(4, 0): (2, 3), (0, 3): (3, 0), (1, 3): (3, 1), (0, 4): (3, 2)}[(k, m)]


def apply_kernel(scal, moms, e_ref, sci, upow, out, mat, fx):
    order = scal[2]
    first_row = scal[1]
    units = [moms[32 * i : 32 * i + 32] for i in range(4)]
    lane = lax.broadcasted_iota(jnp.int32, (1, TC), 1)
    row = lax.broadcasted_iota(jnp.int32, (32, 1), 0)
    degree = lambda q: 0 if q == 0 else (1 if q < 3 else 2)

    def col_active(t):
        q = lax.shift_right_logical(lane, 5) + 4 * t
        deg = jnp.where(q >= 1, 1, 0) + jnp.where(q >= 3, 1, 0)
        return (deg <= order) | (lax.bitwise_and(lane, 31) == ONES)

    for q in range(6):
        row_on = (degree(q) <= order) | (row == ONES)
        for t in range(2):
            block = jnp.zeros((32, TC), F32)
            for s in range(4 if t == 0 else 2):
                p = 4 * t + s
                i, k = unit_of(mono[q][0] + mono[p][0], mono[q][1] + mono[p][1])
                piece = units[i]
                if s != k:
                    piece = pltpu.roll(piece, (32 * (s - k)) % 128, 1)
                block = jnp.where(lax.shift_right_logical(lane, 5) == s, piece, block)
            both = row_on & col_active(t)
            block = jnp.where(both, block, 0.0)
            if t == q // 4:
                diag = lane == row + 32 * (q % 4)
                block = jnp.where(diag, jnp.where(both, block, 1.0) * (1.0 + ridge), block)
            mat[32 * q : 32 * q + 32, TC * t : TC * t + TC] = block
            if q == 0:
                mat[192:200, TC * t : TC * t + TC] = jnp.where(col_active(t), block[24:32], 0.0)
    wide = lax.broadcasted_iota(jnp.int32, (1, 2 * TC), 1)
    for q in range(6):
        t = q // 4
        top = 32 * q
        base = 32 * (q % 4)

        def sweep(b, carry, t=t, top=top, base=base):
            panel = mat[top : top + 32, :]
            prow = mat[pl.ds(top + b, 1), :]
            at = lane == base + b
            col = jnp.sum(
                jnp.where(at, panel[:, TC * t : TC * t + TC], 0.0), axis=1, keepdims=True
            )
            d = jnp.sum(jnp.where(at, prow[:, TC * t : TC * t + TC], 0.0), axis=1, keepdims=True)
            inv = 1.0 / d
            here = row == b
            g = jnp.where(here, -1.0, col) * inv
            atw = wide == TC * t + base + b
            mat[top : top + 32, :] = jnp.where(atw | here, 0.0, panel) - g * jnp.where(atw, 1.0, prow)
            return carry

        lax.fori_loop(0, 28, sweep, 0)
        panel = mat[top : top + 32, :]
        local = wide - (TC * t + base)
        inside = (local >= 0) & (local < 28)
        f = jnp.where(row < 28, jnp.where(inside, -panel, panel), 0.0)
        fx[...] = jnp.zeros_like(fx)
        fx[base : base + 32, :] = f
        rest = mat[top + 32 : 200, :]
        mat[top + 32 : 200, :] = jnp.where(inside, 0.0, rest) - jnp.dot(
            rest[:, TC * t : TC * t + TC],
            fx[...],
            preferred_element_type=F32,
            precision=lax.Precision.HIGHEST,
        )
    coef = []
    for q in range(6):
        z = mat[192:200, TC * (q // 4) : TC * (q // 4) + TC]
        z = jnp.broadcast_to(z[TARGET - 24 : TARGET - 23], (8, TC))
        if q % 4:
            z = pltpu.roll(z, 128 - 32 * (q % 4), 1)
        z = jnp.where(lane < 28, z, 0.0)
        z = z + pltpu.roll(z, 32, 1)
        z = z + pltpu.roll(z, 64, 1)
        coef.append(jnp.concatenate([z, z], axis=0))
    row16 = lax.broadcasted_iota(jnp.int32, (16, 1), 0)
    v = (first_row + row16).astype(F32) * (2.0 / 256.0) + (1.0 / 256.0 - 1.0)
    parts = (coef[0] + v * (coef[2] + v * coef[5]), coef[1] + v * coef[4], coef[3])
    his, los = [], []
    for p in parts:
        wide_p = jnp.concatenate(
            [jnp.where(row16 == 4 * n + lax.shift_right_logical(lane, 5), p, 0.0) for n in range(4)],
            axis=1,
        )
        h = wide_p.astype(BF16)
        his.append(h)
        los.append((wide_p - h.astype(F32)).astype(BF16))
    res = jnp.dot(jnp.concatenate(his + los, axis=0), e_ref[...], preferred_element_type=F32)
    t0, t1, t2 = (res[16 * i : 16 * i + 16] + res[48 + 16 * i : 64 + 16 * i] for i in range(3))
    u = upow[0:1, :]
    out[...] = sci[...] - (t0 + u * (t1 + u * t2))


MESH = pl.DeviceIdType.MESH


def tiles_kernel(ccds, strips, pick, owner, store, own, above, below, sent, got, edge, send, recv, esend, erecv):
    ccd = lax.axis_index("ccd")
    strip = lax.axis_index("strip")
    count = ccds * strips
    me = ccd * strips + strip
    barrier = pltpu.get_barrier_semaphore()

    def peer(k):
        return lax.rem(ccd + k // strips, ccds), lax.rem(strip + lax.rem(k, strips), strips)

    def greet(k, carry):
        pl.semaphore_signal(barrier, inc=1, device_id=peer(k), device_id_type=MESH)
        return carry

    lax.fori_loop(1, count, greet, 0)

    def choose(d, carry):
        sent[d] = store[pick[d]]
        return carry

    lax.fori_loop(0, count, choose, 0)
    got[me] = sent[me]
    pl.semaphore_wait(barrier, count - 1)

    def push(k, carry):
        to = peer(k)
        pltpu.make_async_remote_copy(
            src_ref=sent.at[to[0] * strips + to[1]],
            dst_ref=got.at[me],
            send_sem=send,
            recv_sem=recv,
            device_id=to,
            device_id_type=MESH,
        ).start()
        return carry

    lax.fori_loop(1, count, push, 0)
    rest = got.at[pl.ds(0, count - 1)]
    pltpu.make_async_copy(rest, rest, recv).wait()
    for t in range(own.shape[0]):
        own[t] = got[owner[t]]

    def edge_copy(way):
        return pltpu.make_async_remote_copy(
            src_ref=own,
            dst_ref=edge.at[way],
            send_sem=esend.at[way],
            recv_sem=erecv.at[way],
            device_id=(ccd, lax.rem(strip + (1 if way == 0 else strips - 1), strips)),
            device_id_type=MESH,
        )

    for way in range(2):
        edge_copy(way).start()
    for way in range(2):
        edge_copy(way).wait()
    above[...] = jnp.where(strip > 0, edge[0], 0.0)
    below[...] = jnp.where(strip < strips - 1, edge[1], 0.0)
    pltpu.make_async_copy(rest, rest, send).wait()


def exchange(pick, owner, store, ccds, strips):
    tiles = jax.ShapeDtypeStruct((owner.shape[0], *store.shape[1:]), F32)
    count = ccds * strips
    return pl.pallas_call(
        lambda *refs: tiles_kernel(ccds, strips, *refs),
        out_shape=(tiles, tiles, tiles),
        in_specs=[SM, SM, VM],
        out_specs=(VM, VM, VM),
        scratch_shapes=[
            pltpu.VMEM((count, *store.shape[1:]), F32),
            pltpu.VMEM((count, *store.shape[1:]), F32),
            pltpu.VMEM((2, *tiles.shape), F32),
            pltpu.SemaphoreType.DMA,
            pltpu.SemaphoreType.DMA,
            pltpu.SemaphoreType.DMA((2,)),
            pltpu.SemaphoreType.DMA((2,)),
        ],
        compiler_params=pltpu.CompilerParams(
            collective_id=0, has_side_effects=True, vmem_limit_bytes=LIMIT
        ),
        name="tiles",
    )(pick, owner, store)


def total_kernel(strips, mom, out, got, part, all_parts, s1, r1, s2, r2):
    ccd = lax.axis_index("ccd")
    strip = lax.axis_index("strip")
    barrier = pltpu.get_barrier_semaphore()
    peers = [(ccd, lax.rem(strip + k, strips)) for k in range(1, strips)]
    for to in peers:
        pl.semaphore_signal(barrier, inc=1, device_id=to, device_id_type=MESH)
    pl.semaphore_wait(barrier, strips - 1)
    for to in peers:
        pltpu.make_async_remote_copy(
            src_ref=mom.at[to[1]],
            dst_ref=got.at[strip],
            send_sem=s1,
            recv_sem=r1,
            device_id=to,
            device_id_type=MESH,
        ).start()
    got[strip] = mom[strip]
    rest = got.at[pl.ds(0, strips - 1)]
    pltpu.make_async_copy(rest, rest, r1).wait()
    total = got[0]
    for i in range(1, strips):
        total = total + got[i]
    part[...] = total
    for to in peers:
        pltpu.make_async_remote_copy(
            src_ref=part,
            dst_ref=all_parts.at[strip],
            send_sem=s2,
            recv_sem=r2,
            device_id=to,
            device_id_type=MESH,
        ).start()
    all_parts[strip] = total
    pltpu.make_async_copy(rest, rest, s1).wait()
    pltpu.make_async_copy(rest, rest, s2).wait()
    pltpu.make_async_copy(rest, rest, r2).wait()
    out[...] = all_parts[...]


def sum_over_strips(mom, strips):
    rows = mom.shape[0] // strips
    blocks = mom.reshape(strips, rows, TC)
    buffer = pltpu.VMEM(blocks.shape, F32)
    total = pl.pallas_call(
        lambda *refs: total_kernel(strips, *refs),
        out_shape=jax.ShapeDtypeStruct(blocks.shape, F32),
        in_specs=[VM],
        out_specs=VM,
        scratch_shapes=[buffer, pltpu.VMEM((rows, TC), F32), buffer] + [pltpu.SemaphoreType.DMA] * 4,
        compiler_params=pltpu.CompilerParams(collective_id=1, has_side_effects=True),
        name="total",
    )(blocks)
    return total.reshape(mom.shape)


VM = pl.BlockSpec(memory_space=pltpu.VMEM)
SM = pl.BlockSpec(memory_space=pltpu.SMEM)
LIMIT = 60 * 1024 * 1024


def fit(scal, own, above, below, sci):
    band = jnp.asarray(band_matrix())
    va, vb = (jnp.asarray(m) for m in vertical_matrices())
    upow = jnp.asarray(column_powers())
    return pl.pallas_call(
        fit_kernel,
        out_shape=(
            jax.ShapeDtypeStruct((ROWS * 32, COLS), BF16),
            jax.ShapeDtypeStruct((128, TC), F32),
        ),
        in_specs=[SM] + [VM] * 8,
        out_specs=(VM, VM),
        scratch_shapes=[
            pltpu.VMEM((own.shape[0] + 1, SLOTS, TC), F32),
            pltpu.VMEM((440, COLS), F32),
            pltpu.VMEM((5, 64, TC), F32),
        ],
        compiler_params=pltpu.CompilerParams(vmem_limit_bytes=LIMIT),
        name="fit",
    )(scal, own, above, below, sci, band, va, vb, upow)


def apply(scal, moms, e, sci):
    upow = jnp.asarray(column_powers())
    return pl.pallas_call(
        apply_kernel,
        out_shape=jax.ShapeDtypeStruct((ROWS, COLS), F32),
        in_specs=[SM] + [VM] * 4,
        out_specs=VM,
        scratch_shapes=[pltpu.VMEM((200, 2 * TC), F32), pltpu.VMEM((TC, 2 * TC), F32)],
        compiler_params=pltpu.CompilerParams(vmem_limit_bytes=LIMIT),
        name="apply",
    )(scal, moms, e, sci, upow)


def body(tile_store, tile_source, tile_slot, shift_cols, spatial_order, science):
    strips = lax.axis_size("strip")
    strip = lax.axis_index("strip")
    me = lax.axis_index("ccd") * strips + strip
    pick = jnp.sum(jnp.where(tile_source == me, tile_slot, 0), axis=1)
    owner = lax.dynamic_index_in_dim(tile_source, me, 0, keepdims=False)
    own, above, below = exchange(pick, owner, tile_store, lax.axis_size("ccd"), strips)
    scal = jnp.stack([shift_cols[0], strip * ROWS, spatial_order[0]]).astype(jnp.int32)
    e, mom = fit(scal, own, above, below, science)
    total = sum_over_strips(mom, strips)
    return apply(scal, total, e, science)


def solution(mesh):
    placed = (
        P(("ccd", "strip"), None, None),
        P(),
        P(),
        P("ccd"),
        P("ccd"),
        P(("ccd", "strip"), None),
    )
    return jax.shard_map(
        body, mesh=mesh, in_specs=placed, out_specs=P(("ccd", "strip"), None), check_vma=False
    )
```

```python
import jax
import jax.numpy as jnp
import numpy as np
from jax import lax
from jax.experimental import pallas as pl
from jax.experimental.pallas import tpu as pltpu
from jax.sharding import PartitionSpec as P

H = 11
CM = 128
ROWS = 16
COLS = 2048
TC = 128
SLOTS = 40
TARGET = 28
ONES = 15

sigmas = (0.7, 1.5, 3.0)
tops = (4, 2, 2)
mono = ((0, 0), (1, 0), (0, 1), (2, 0), (1, 1), (0, 2))
ridge = 0.05
F32 = jnp.float32
BF16 = jnp.bfloat16


def tap_table():
    a = np.arange(-H, H + 1).astype(np.float64)
    rows = []
    for s, top in zip(sigmas, tops):
        e = np.exp(-a * a / (2.0 * s * s))
        for n in range(top + 1):
            rows.append(e * (a / s) ** n / e.sum())
    return np.stack(rows).astype(np.float32)


def to_bf16(x):
    return x.astype(jnp.bfloat16.dtype)


def band_matrix():
    taps = tap_table()
    hi = to_bf16(taps).astype(np.float32)
    lo = to_bf16(taps - hi).astype(np.float32)
    full = []
    for part in (hi, lo):
        m = np.zeros((160, 11, TC), np.float32)
        for f in range(11):
            for x in range(TC):
                m[x : x + 23, f, x] = part[f]
        full.append(m.reshape(160, 11 * TC))
    h, l = full
    tail = np.zeros((TC, 11 * TC), np.float32)
    tail[0:32], tail[32:64], tail[64:96] = h[128:], h[128:], l[128:]
    return to_bf16(np.concatenate([h[:128], h[:128], l[:128], tail]))


def slot_of(row):
    return 16 + row if row < H else (row - H if row < H + ROWS else row)


def vertical_matrices():
    taps = to_bf16(tap_table()).astype(np.float32)
    first = np.zeros((ROWS, 16, 208), np.float32)
    second = np.zeros((ROWS, 16, 240), np.float32)
    slot = 0
    for i in range(5):
        for j in range(5 - i):
            for r in range(ROWS):
                for a in range(23):
                    first[r, slot, i * SLOTS + slot_of(r + a)] = taps[j, a]
            slot += 1
    first[:, ONES, 38] = 1.0
    slot = 0
    for g in range(2):
        for i in range(3):
            for j in range(3 - i):
                for r in range(ROWS):
                    for a in range(23):
                        second[r, slot, (3 * g + i) * SLOTS + slot_of(r + a)] = taps[5 + 3 * g + j, a]
                slot += 1
    return to_bf16(first.reshape(256, 208)), to_bf16(second.reshape(256, 240))


def column_powers():
    u = 2.0 * (np.arange(COLS).astype(np.float32) + np.float32(0.5)) / np.float32(COLS) - np.float32(1.0)
    u = u.astype(np.float32)
    return np.stack([u, u * u] + [np.zeros_like(u)] * 6)


def fit_kernel(scal, own, above, below, sci, band, va, vb, upow, e_out, mom_out, rolled, hs, acc):
    shift = scal[0]
    first_row = scal[1]
    start = CM + shift - H
    tile = lax.shift_right_logical(start, 7)
    rem = lax.bitwise_and(start, 127)
    count = own.shape[0]
    row16 = lax.broadcasted_iota(jnp.int32, (1, 16, TC), 1)
    row8 = lax.broadcasted_iota(jnp.int32, (1, 8, TC), 1)
    a = pltpu.roll(above[...], H, 1)
    b = pltpu.roll(below[...], H, 1)
    mid = jnp.where(row16 < H, a, b)
    end = jnp.where(row8 < 6, b[:, :8], jnp.where(row8 == 6, 1.0, 0.0))
    x = jnp.concatenate([own[...], mid, end], axis=1)
    rolled[0:count] = pltpu.roll(x, lax.bitwise_and(128 - rem, 127), 2)
    rolled[count : count + 1] = jnp.zeros((1, SLOTS, TC), F32)
    lane3 = lax.broadcasted_iota(jnp.int32, (1, SLOTS, TC), 2)
    w = jnp.where(
        lane3 < 128 - rem, rolled[pl.ds(tile, 17)], rolled[pl.ds(tile + 1, 17)]
    ).reshape(17 * SLOTS, TC)
    main = w[: 16 * SLOTS]
    nxt = w[SLOTS:]
    hi = main.astype(BF16)
    lo = (main - hi.astype(F32)).astype(BF16)
    nhi = nxt.astype(BF16).astype(F32)
    nlo = nxt - nhi
    lane = lax.broadcasted_iota(jnp.int32, (1, TC), 1)
    tail = jnp.where(
        lane < 32,
        nhi,
        jnp.where(lane < 64, pltpu.roll(nlo, 32, 1), jnp.where(lane < 96, pltpu.roll(nhi, 64, 1), 0.0)),
    ).astype(BF16)
    lhs = jnp.concatenate([hi, lo, hi, tail], axis=1)
    for c in range(6):
        n = 256 if c < 5 else 128
        res = jnp.dot(lhs, band[:, 256 * c : 256 * c + n], preferred_element_type=F32)
        for f in range(2 * c, 2 * c + n // TC):
            o = (f - 2 * c) * TC
            for j in range(16):
                hs[f * SLOTS : (f + 1) * SLOTS, j * TC : (j + 1) * TC] = res[
                    j * SLOTS : (j + 1) * SLOTS, o : o + TC
                ]
    for c in range(8):
        cols = slice(256 * c, 256 * c + 256)
        oa = jnp.dot(va[...], hs[0:208, cols].astype(BF16), preferred_element_type=F32)
        ob = jnp.dot(vb[...], hs[200:440, cols].astype(BF16), preferred_element_type=F32)
        e = jnp.concatenate([oa.reshape(ROWS, 16, 256), ob.reshape(ROWS, 16, 256)], axis=1)
        e_out[:, cols] = e.reshape(ROWS * 32, 256).astype(BF16)
    acc[...] = jnp.zeros_like(acc)
    u1 = upow[0:1, :]
    u2 = upow[1:2, :]
    brow = lax.broadcasted_iota(jnp.int32, (32, 1), 0)

    def row_step(r, carry):
        e = e_out[pl.ds(pl.multiple_of(r * 32, 32), 32), :].astype(F32)
        e = jnp.where(brow == TARGET, sci[pl.ds(r, 1), :], e)
        e16 = e.astype(BF16)
        e = e16.astype(F32)
        f1 = (e * u1).astype(BF16)
        f2 = (e * u2).astype(BF16)
        g = lax.dot_general(
            jnp.concatenate([e16, f2], axis=0),
            jnp.concatenate([e16, f1, f2], axis=0),
            (((1,), (1,)), ((), ())),
            preferred_element_type=F32,
        )
        v = (first_row + r).astype(F32) * (2.0 / 256.0) + (1.0 / 256.0 - 1.0)
        scale = 1.0
        for m in range(5):
            n = 64 if m < 2 else 32
            acc[m, 0:n, 0:96] += g[0:n] * scale
            scale = scale * v
        return carry

    lax.fori_loop(0, ROWS, row_step, 0)
    units = (
        jnp.where(lane < 96, acc[0, 0:32], pltpu.roll(acc[0, 32:64], 64, 1)),
        jnp.where(lane < 96, acc[1, 0:32], pltpu.roll(acc[1, 32:64], 64, 1)),
        jnp.where(lane < 96, acc[2, 0:32], pltpu.roll(acc[0, 32:64], 32, 1)),
        jnp.where(lane < 64, acc[3, 0:32], pltpu.roll(acc[4, 0:32], 64, 1)),
    )
    for i, unit in enumerate(units):
        mom_out[32 * i : 32 * i + 32] = unit


def unit_of(k, m):
    if m < 2 and k < 4:
        return m, k
    if m == 2:
        return 2, k
    return {(4, 0): (2, 3), (0, 3): (3, 0), (1, 3): (3, 1), (0, 4): (3, 2)}[(k, m)]


def inverse2(m):
    (a, b), (c, d) = m
    r = 1.0 / (a * d - b * c)
    return (d * r, -b * r), (-c * r, a * r)


def times2(x, y):
    return tuple(tuple(x[i][0] * y[0][j] + x[i][1] * y[1][j] for j in range(2)) for i in range(2))


def plus2(x, y, sign):
    return tuple(tuple(x[i][j] + sign * y[i][j] for j in range(2)) for i in range(2))


def inverse4(p):
    part = lambda i, j: tuple(tuple(p[2 * i + a][2 * j + b] for b in range(2)) for a in range(2))
    head = inverse2(part(0, 0))
    x = times2(head, part(0, 1))
    y = times2(part(1, 0), head)
    tail = inverse2(plus2(part(1, 1), times2(part(1, 0), x), -1.0))
    xt = times2(x, tail)
    low = times2(tail, y)
    top = plus2(head, times2(xt, y), 1.0)
    return [
        [top[i][j] if i < 2 and j < 2 else tail[i - 2][j - 2] if i > 1 and j > 1
         else -xt[i][j - 2] if i < 2 else -low[i - 2][j] for j in range(4)]
        for i in range(4)
    ]


def sweep_panel(mat, fx, q, lane):
    t = q // 4
    top = 32 * q
    base = 32 * (q % 4)
    sub = lax.broadcasted_iota(jnp.int32, (8, TC), 0)
    tiles = [[mat[top + 8 * i : top + 8 * i + 8, TC * h : TC * h + TC] for h in range(2)] for i in range(4)]
    for k in range(0, 28, 4):
        i0, s0, l0 = k // 8, k % 8, base + k
        cols = [
            [jnp.broadcast_to(tiles[i][t][:, l0 + j : l0 + j + 1], (8, TC)) for j in range(4)]
            for i in range(4)
        ]
        p = [[jnp.broadcast_to(cols[i0][j][s0 + i : s0 + i + 1], (8, TC)) for j in range(4)] for i in range(4)]
        w = inverse4(p)
        in_lane = (lane >= l0) & (lane < l0 + 4)
        in_row = (sub >= s0) & (sub < s0 + 4)
        rows = []
        for h in range(2):
            r = [jnp.broadcast_to(tiles[i0][h][s0 + j : s0 + j + 1], (8, TC)) for j in range(4)]
            if h == t:
                r = [jnp.where(in_lane, jnp.where(lane == l0 + j, 1.0, 0.0), r[j]) for j in range(4)]
            rows.append([
                (w[m][0] * r[0] + w[m][1] * r[1]) + (w[m][2] * r[2] + w[m][3] * r[3]) for m in range(4)
            ])
        for i in range(4):
            c = cols[i]
            if i == i0:
                c = [jnp.where(in_row, jnp.where(sub == s0 + j, -1.0, 0.0), c[j]) for j in range(4)]
            for h in range(2):
                old = tiles[i][h]
                if h == t:
                    old = jnp.where(in_lane, 0.0, old)
                if i == i0:
                    old = jnp.where(in_row, 0.0, old)
                u = rows[h]
                tiles[i][h] = old - ((c[0] * u[0] + c[1] * u[1]) + (c[2] * u[2] + c[3] * u[3]))
    fx[...] = jnp.zeros_like(fx)
    inside = (lane >= base) & (lane < base + 28)
    for i in range(4):
        for h in range(2):
            f = tiles[i][h]
            if h == t:
                f = jnp.where(inside, -f, f)
            if i == 3:
                f = jnp.where(sub < 4, f, 0.0)
            fx[base + 8 * i : base + 8 * i + 8, TC * h : TC * h + TC] = f
    rest = mat[top + 32 : 200, TC * t : TC * t + TC]
    change = jnp.dot(rest, fx[...], preferred_element_type=F32, precision=lax.Precision.HIGHEST)
    for h in range(2):
        old = mat[top + 32 : 200, TC * h : TC * h + TC]
        if h == t:
            old = jnp.where(inside, 0.0, old)
        mat[top + 32 : 200, TC * h : TC * h + TC] = old - change[:, TC * h : TC * h + TC]


def apply_kernel(scal, moms, e_ref, sci, upow, out, mat, fx):
    order = scal[2]
    first_row = scal[1]
    units = [moms[32 * i : 32 * i + 32] for i in range(4)]
    lane = lax.broadcasted_iota(jnp.int32, (1, TC), 1)
    row = lax.broadcasted_iota(jnp.int32, (32, 1), 0)
    degree = lambda q: 0 if q == 0 else (1 if q < 3 else 2)

    def col_active(t):
        q = lax.shift_right_logical(lane, 5) + 4 * t
        deg = jnp.where(q >= 1, 1, 0) + jnp.where(q >= 3, 1, 0)
        return (deg <= order) | (lax.bitwise_and(lane, 31) == ONES)

    for q in range(6):
        row_on = (degree(q) <= order) | (row == ONES)
        for t in range(2):
            block = jnp.zeros((32, TC), F32)
            for s in range(4 if t == 0 else 2):
                p = 4 * t + s
                i, k = unit_of(mono[q][0] + mono[p][0], mono[q][1] + mono[p][1])
                piece = units[i]
                if s != k:
                    piece = pltpu.roll(piece, (32 * (s - k)) % 128, 1)
                block = jnp.where(lax.shift_right_logical(lane, 5) == s, piece, block)
            both = row_on & col_active(t)
            block = jnp.where(both, block, 0.0)
            if t == q // 4:
                diag = lane == row + 32 * (q % 4)
                block = jnp.where(diag, jnp.where(both, block, 1.0) * (1.0 + ridge), block)
            mat[32 * q : 32 * q + 32, TC * t : TC * t + TC] = block
            if q == 0:
                mat[192:200, TC * t : TC * t + TC] = jnp.where(col_active(t), block[24:32], 0.0)
    for q in range(6):
        sweep_panel(mat, fx, q, lane)
    coef = []
    for q in range(6):
        z = mat[192:200, TC * (q // 4) : TC * (q // 4) + TC]
        z = jnp.broadcast_to(z[TARGET - 24 : TARGET - 23], (8, TC))
        if q % 4:
            z = pltpu.roll(z, 128 - 32 * (q % 4), 1)
        z = jnp.where(lane < 28, z, 0.0)
        z = z + pltpu.roll(z, 32, 1)
        z = z + pltpu.roll(z, 64, 1)
        coef.append(jnp.concatenate([z, z], axis=0))
    row16 = lax.broadcasted_iota(jnp.int32, (16, 1), 0)
    v = (first_row + row16).astype(F32) * (2.0 / 256.0) + (1.0 / 256.0 - 1.0)
    parts = (coef[0] + v * (coef[2] + v * coef[5]), coef[1] + v * coef[4], coef[3])
    his, los = [], []
    for p in parts:
        wide_p = jnp.concatenate(
            [jnp.where(row16 == 4 * n + lax.shift_right_logical(lane, 5), p, 0.0) for n in range(4)],
            axis=1,
        )
        h = wide_p.astype(BF16)
        his.append(h)
        los.append((wide_p - h.astype(F32)).astype(BF16))
    res = jnp.dot(jnp.concatenate(his + los, axis=0), e_ref[...], preferred_element_type=F32)
    t0, t1, t2 = (res[16 * i : 16 * i + 16] + res[48 + 16 * i : 64 + 16 * i] for i in range(3))
    u = upow[0:1, :]
    out[...] = sci[...] - (t0 + u * (t1 + u * t2))


MESH = pl.DeviceIdType.MESH


def tiles_kernel(ccds, strips, pick, owner, store, own, above, below, sent, got, edge, send, recv, esend, erecv):
    ccd = lax.axis_index("ccd")
    strip = lax.axis_index("strip")
    count = ccds * strips
    me = ccd * strips + strip
    barrier = pltpu.get_barrier_semaphore()

    def peer(k):
        return lax.rem(ccd + k // strips, ccds), lax.rem(strip + lax.rem(k, strips), strips)

    def greet(k, carry):
        pl.semaphore_signal(barrier, inc=1, device_id=peer(k), device_id_type=MESH)
        return carry

    lax.fori_loop(1, count, greet, 0)

    def choose(d, carry):
        sent[d] = store[pick[d]]
        return carry

    lax.fori_loop(0, count, choose, 0)
    got[me] = sent[me]
    pl.semaphore_wait(barrier, count - 1)

    def push(k, carry):
        to = peer(k)
        pltpu.make_async_remote_copy(
            src_ref=sent.at[to[0] * strips + to[1]],
            dst_ref=got.at[me],
            send_sem=send,
            recv_sem=recv,
            device_id=to,
            device_id_type=MESH,
        ).start()
        return carry

    lax.fori_loop(1, count, push, 0)
    rest = got.at[pl.ds(0, count - 1)]
    pltpu.make_async_copy(rest, rest, recv).wait()
    for t in range(own.shape[0]):
        own[t] = got[owner[t]]

    def edge_copy(way):
        return pltpu.make_async_remote_copy(
            src_ref=own,
            dst_ref=edge.at[way],
            send_sem=esend.at[way],
            recv_sem=erecv.at[way],
            device_id=(ccd, lax.rem(strip + (1 if way == 0 else strips - 1), strips)),
            device_id_type=MESH,
        )

    for way in range(2):
        edge_copy(way).start()
    for way in range(2):
        edge_copy(way).wait()
    above[...] = jnp.where(strip > 0, edge[0], 0.0)
    below[...] = jnp.where(strip < strips - 1, edge[1], 0.0)
    pltpu.make_async_copy(rest, rest, send).wait()


def exchange(pick, owner, store, ccds, strips):
    tiles = jax.ShapeDtypeStruct((owner.shape[0], *store.shape[1:]), F32)
    count = ccds * strips
    return pl.pallas_call(
        lambda *refs: tiles_kernel(ccds, strips, *refs),
        out_shape=(tiles, tiles, tiles),
        in_specs=[SM, SM, VM],
        out_specs=(VM, VM, VM),
        scratch_shapes=[
            pltpu.VMEM((count, *store.shape[1:]), F32),
            pltpu.VMEM((count, *store.shape[1:]), F32),
            pltpu.VMEM((2, *tiles.shape), F32),
            pltpu.SemaphoreType.DMA,
            pltpu.SemaphoreType.DMA,
            pltpu.SemaphoreType.DMA((2,)),
            pltpu.SemaphoreType.DMA((2,)),
        ],
        compiler_params=pltpu.CompilerParams(
            collective_id=0, has_side_effects=True, vmem_limit_bytes=LIMIT
        ),
        name="tiles",
    )(pick, owner, store)


def total_kernel(strips, mom, out, got, part, all_parts, s1, r1, s2, r2):
    ccd = lax.axis_index("ccd")
    strip = lax.axis_index("strip")
    barrier = pltpu.get_barrier_semaphore()
    peers = [(ccd, lax.rem(strip + k, strips)) for k in range(1, strips)]
    for to in peers:
        pl.semaphore_signal(barrier, inc=1, device_id=to, device_id_type=MESH)
    pl.semaphore_wait(barrier, strips - 1)
    for to in peers:
        pltpu.make_async_remote_copy(
            src_ref=mom.at[to[1]],
            dst_ref=got.at[strip],
            send_sem=s1,
            recv_sem=r1,
            device_id=to,
            device_id_type=MESH,
        ).start()
    got[strip] = mom[strip]
    rest = got.at[pl.ds(0, strips - 1)]
    pltpu.make_async_copy(rest, rest, r1).wait()
    total = got[0]
    for i in range(1, strips):
        total = total + got[i]
    part[...] = total
    for to in peers:
        pltpu.make_async_remote_copy(
            src_ref=part,
            dst_ref=all_parts.at[strip],
            send_sem=s2,
            recv_sem=r2,
            device_id=to,
            device_id_type=MESH,
        ).start()
    all_parts[strip] = total
    pltpu.make_async_copy(rest, rest, s1).wait()
    pltpu.make_async_copy(rest, rest, s2).wait()
    pltpu.make_async_copy(rest, rest, r2).wait()
    out[...] = all_parts[...]


def sum_over_strips(mom, strips):
    rows = mom.shape[0] // strips
    blocks = mom.reshape(strips, rows, TC)
    buffer = pltpu.VMEM(blocks.shape, F32)
    total = pl.pallas_call(
        lambda *refs: total_kernel(strips, *refs),
        out_shape=jax.ShapeDtypeStruct(blocks.shape, F32),
        in_specs=[VM],
        out_specs=VM,
        scratch_shapes=[buffer, pltpu.VMEM((rows, TC), F32), buffer] + [pltpu.SemaphoreType.DMA] * 4,
        compiler_params=pltpu.CompilerParams(collective_id=1, has_side_effects=True),
        name="total",
    )(blocks)
    return total.reshape(mom.shape)


VM = pl.BlockSpec(memory_space=pltpu.VMEM)
SM = pl.BlockSpec(memory_space=pltpu.SMEM)
LIMIT = 60 * 1024 * 1024


def fit(scal, own, above, below, sci):
    band = jnp.asarray(band_matrix())
    va, vb = (jnp.asarray(m) for m in vertical_matrices())
    upow = jnp.asarray(column_powers())
    return pl.pallas_call(
        fit_kernel,
        out_shape=(
            jax.ShapeDtypeStruct((ROWS * 32, COLS), BF16),
            jax.ShapeDtypeStruct((128, TC), F32),
        ),
        in_specs=[SM] + [VM] * 8,
        out_specs=(VM, VM),
        scratch_shapes=[
            pltpu.VMEM((own.shape[0] + 1, SLOTS, TC), F32),
            pltpu.VMEM((440, COLS), F32),
            pltpu.VMEM((5, 64, TC), F32),
        ],
        compiler_params=pltpu.CompilerParams(vmem_limit_bytes=LIMIT),
        name="fit",
    )(scal, own, above, below, sci, band, va, vb, upow)


def apply(scal, moms, e, sci):
    upow = jnp.asarray(column_powers())
    return pl.pallas_call(
        apply_kernel,
        out_shape=jax.ShapeDtypeStruct((ROWS, COLS), F32),
        in_specs=[SM] + [VM] * 4,
        out_specs=VM,
        scratch_shapes=[pltpu.VMEM((200, 2 * TC), F32), pltpu.VMEM((TC, 2 * TC), F32)],
        compiler_params=pltpu.CompilerParams(vmem_limit_bytes=LIMIT),
        name="apply",
    )(scal, moms, e, sci, upow)


def body(tile_store, tile_source, tile_slot, shift_cols, spatial_order, science):
    strips = lax.axis_size("strip")
    strip = lax.axis_index("strip")
    me = lax.axis_index("ccd") * strips + strip
    pick = jnp.sum(jnp.where(tile_source == me, tile_slot, 0), axis=1)
    owner = lax.dynamic_index_in_dim(tile_source, me, 0, keepdims=False)
    own, above, below = exchange(pick, owner, tile_store, lax.axis_size("ccd"), strips)
    scal = jnp.stack([shift_cols[0], strip * ROWS, spatial_order[0]]).astype(jnp.int32)
    e, mom = fit(scal, own, above, below, science)
    total = sum_over_strips(mom, strips)
    return apply(scal, total, e, science)


def solution(mesh):
    placed = (
        P(("ccd", "strip"), None, None),
        P(),
        P(),
        P("ccd"),
        P("ccd"),
        P(("ccd", "strip"), None),
    )
    return jax.shard_map(
        body, mesh=mesh, in_specs=placed, out_specs=P(("ccd", "strip"), None), check_vma=False
    )
```

```python
import jax
import jax.numpy as jnp
import numpy as np
from jax import lax
from jax.experimental import pallas as pl
from jax.experimental.pallas import tpu as pltpu
from jax.sharding import PartitionSpec as P

H = 11
CM = 128
ROWS = 16
COLS = 2048
TC = 128
SLOTS = 40
TARGET = 28
ONES = 15

sigmas = (0.7, 1.5, 3.0)
tops = (4, 2, 2)
mono = ((0, 0), (1, 0), (0, 1), (2, 0), (1, 1), (0, 2))
ridge = 0.05
F32 = jnp.float32
BF16 = jnp.bfloat16


def tap_table():
    a = np.arange(-H, H + 1).astype(np.float64)
    rows = []
    for s, top in zip(sigmas, tops):
        e = np.exp(-a * a / (2.0 * s * s))
        for n in range(top + 1):
            rows.append(e * (a / s) ** n / e.sum())
    return np.stack(rows).astype(np.float32)


def to_bf16(x):
    return x.astype(jnp.bfloat16.dtype)


def band_matrix():
    taps = tap_table()
    hi = to_bf16(taps).astype(np.float32)
    lo = to_bf16(taps - hi).astype(np.float32)
    full = []
    for part in (hi, lo):
        m = np.zeros((160, 11, TC), np.float32)
        for f in range(11):
            for x in range(TC):
                m[x : x + 23, f, x] = part[f]
        full.append(m.reshape(160, 11 * TC))
    h, l = full
    tail = np.zeros((TC, 11 * TC), np.float32)
    tail[0:32], tail[32:64], tail[64:96] = h[128:], h[128:], l[128:]
    return to_bf16(np.concatenate([h[:128], h[:128], l[:128], tail]))


def slot_of(row):
    return 16 + row if row < H else (row - H if row < H + ROWS else row)


def vertical_matrices():
    taps = to_bf16(tap_table()).astype(np.float32)
    first = np.zeros((ROWS, 16, 208), np.float32)
    second = np.zeros((ROWS, 16, 240), np.float32)
    slot = 0
    for i in range(5):
        for j in range(5 - i):
            for r in range(ROWS):
                for a in range(23):
                    first[r, slot, i * SLOTS + slot_of(r + a)] = taps[j, a]
            slot += 1
    first[:, ONES, 38] = 1.0
    slot = 0
    for g in range(2):
        for i in range(3):
            for j in range(3 - i):
                for r in range(ROWS):
                    for a in range(23):
                        second[r, slot, (3 * g + i) * SLOTS + slot_of(r + a)] = taps[5 + 3 * g + j, a]
                slot += 1
    return to_bf16(first.reshape(256, 208)), to_bf16(second.reshape(256, 240))


def column_powers():
    u = 2.0 * (np.arange(COLS).astype(np.float32) + np.float32(0.5)) / np.float32(COLS) - np.float32(1.0)
    u = u.astype(np.float32)
    return np.stack([u, u * u] + [np.zeros_like(u)] * 6)


def fit_stage(shift, first_row, own, above, below, sci, band, va, vb, upow, e_out, mom_out, rolled, hs, acc):
    start = CM + shift - H
    tile = lax.shift_right_logical(start, 7)
    rem = lax.bitwise_and(start, 127)
    count = own.shape[0]
    row16 = lax.broadcasted_iota(jnp.int32, (1, 16, TC), 1)
    row8 = lax.broadcasted_iota(jnp.int32, (1, 8, TC), 1)
    a = pltpu.roll(above, H, 1)
    b = pltpu.roll(below, H, 1)
    mid = jnp.where(row16 < H, a, b)
    end = jnp.where(row8 < 6, b[:, :8], jnp.where(row8 == 6, 1.0, 0.0))
    x = jnp.concatenate([own[...], mid, end], axis=1)
    rolled[0:count] = pltpu.roll(x, lax.bitwise_and(128 - rem, 127), 2)
    rolled[count : count + 1] = jnp.zeros((1, SLOTS, TC), F32)
    lane3 = lax.broadcasted_iota(jnp.int32, (1, SLOTS, TC), 2)
    w = jnp.where(
        lane3 < 128 - rem, rolled[pl.ds(tile, 17)], rolled[pl.ds(tile + 1, 17)]
    ).reshape(17 * SLOTS, TC)
    main = w[: 16 * SLOTS]
    nxt = w[SLOTS:]
    hi = main.astype(BF16)
    lo = (main - hi.astype(F32)).astype(BF16)
    nhi = nxt.astype(BF16).astype(F32)
    nlo = nxt - nhi
    lane = lax.broadcasted_iota(jnp.int32, (1, TC), 1)
    tail = jnp.where(
        lane < 32,
        nhi,
        jnp.where(lane < 64, pltpu.roll(nlo, 32, 1), jnp.where(lane < 96, pltpu.roll(nhi, 64, 1), 0.0)),
    ).astype(BF16)
    lhs = jnp.concatenate([hi, lo, hi, tail], axis=1)
    for c in range(6):
        n = 256 if c < 5 else 128
        res = jnp.dot(lhs, band[:, 256 * c : 256 * c + n], preferred_element_type=F32)
        for f in range(2 * c, 2 * c + n // TC):
            o = (f - 2 * c) * TC
            for j in range(16):
                hs[f * SLOTS : (f + 1) * SLOTS, j * TC : (j + 1) * TC] = res[
                    j * SLOTS : (j + 1) * SLOTS, o : o + TC
                ]
    for c in range(8):
        cols = slice(256 * c, 256 * c + 256)
        oa = jnp.dot(va[...], hs[0:208, cols].astype(BF16), preferred_element_type=F32)
        ob = jnp.dot(vb[...], hs[200:440, cols].astype(BF16), preferred_element_type=F32)
        e = jnp.concatenate([oa.reshape(ROWS, 16, 256), ob.reshape(ROWS, 16, 256)], axis=1)
        e_out[:, cols] = e.reshape(ROWS * 32, 256).astype(BF16)
    acc[...] = jnp.zeros_like(acc)
    u1 = upow[0:1, :]
    u2 = upow[1:2, :]
    brow = lax.broadcasted_iota(jnp.int32, (32, 1), 0)

    def row_step(r, carry):
        e = e_out[pl.ds(pl.multiple_of(r * 32, 32), 32), :].astype(F32)
        e = jnp.where(brow == TARGET, sci[pl.ds(r, 1), :], e)
        e16 = e.astype(BF16)
        e = e16.astype(F32)
        f1 = (e * u1).astype(BF16)
        f2 = (e * u2).astype(BF16)
        g = lax.dot_general(
            jnp.concatenate([e16, f2], axis=0),
            jnp.concatenate([e16, f1, f2], axis=0),
            (((1,), (1,)), ((), ())),
            preferred_element_type=F32,
        )
        v = (first_row + r).astype(F32) * (2.0 / 256.0) + (1.0 / 256.0 - 1.0)
        scale = 1.0
        for m in range(5):
            n = 64 if m < 2 else 32
            acc[m, 0:n, 0:96] += g[0:n] * scale
            scale = scale * v
        return carry

    lax.fori_loop(0, ROWS, row_step, 0)
    units = (
        jnp.where(lane < 96, acc[0, 0:32], pltpu.roll(acc[0, 32:64], 64, 1)),
        jnp.where(lane < 96, acc[1, 0:32], pltpu.roll(acc[1, 32:64], 64, 1)),
        jnp.where(lane < 96, acc[2, 0:32], pltpu.roll(acc[0, 32:64], 32, 1)),
        jnp.where(lane < 64, acc[3, 0:32], pltpu.roll(acc[4, 0:32], 64, 1)),
    )
    for i, unit in enumerate(units):
        for j in range(4):
            mom_out[4 * i + j] = unit[8 * j : 8 * j + 8]


def unit_of(k, m):
    if m < 2 and k < 4:
        return m, k
    if m == 2:
        return 2, k
    return {(4, 0): (2, 3), (0, 3): (3, 0), (1, 3): (3, 1), (0, 4): (3, 2)}[(k, m)]


def inverse2(m):
    (a, b), (c, d) = m
    r = 1.0 / (a * d - b * c)
    return (d * r, -b * r), (-c * r, a * r)


def times2(x, y):
    return tuple(tuple(x[i][0] * y[0][j] + x[i][1] * y[1][j] for j in range(2)) for i in range(2))


def plus2(x, y, sign):
    return tuple(tuple(x[i][j] + sign * y[i][j] for j in range(2)) for i in range(2))


def inverse4(p):
    part = lambda i, j: tuple(tuple(p[2 * i + a][2 * j + b] for b in range(2)) for a in range(2))
    head = inverse2(part(0, 0))
    x = times2(head, part(0, 1))
    y = times2(part(1, 0), head)
    tail = inverse2(plus2(part(1, 1), times2(part(1, 0), x), -1.0))
    xt = times2(x, tail)
    low = times2(tail, y)
    top = plus2(head, times2(xt, y), 1.0)
    return [
        [top[i][j] if i < 2 and j < 2 else tail[i - 2][j - 2] if i > 1 and j > 1
         else -xt[i][j - 2] if i < 2 else -low[i - 2][j] for j in range(4)]
        for i in range(4)
    ]


def sweep_panel(mat, fx, q, lane):
    t = q // 4
    top = 32 * q
    base = 32 * (q % 4)
    sub = lax.broadcasted_iota(jnp.int32, (8, TC), 0)
    tiles = [[mat[top + 8 * i : top + 8 * i + 8, TC * h : TC * h + TC] for h in range(2)] for i in range(4)]
    for k in range(0, 28, 4):
        i0, s0, l0 = k // 8, k % 8, base + k
        cols = [
            [jnp.broadcast_to(tiles[i][t][:, l0 + j : l0 + j + 1], (8, TC)) for j in range(4)]
            for i in range(4)
        ]
        p = [[jnp.broadcast_to(cols[i0][j][s0 + i : s0 + i + 1], (8, TC)) for j in range(4)] for i in range(4)]
        w = inverse4(p)
        in_lane = (lane >= l0) & (lane < l0 + 4)
        in_row = (sub >= s0) & (sub < s0 + 4)
        rows = []
        for h in range(2):
            r = [jnp.broadcast_to(tiles[i0][h][s0 + j : s0 + j + 1], (8, TC)) for j in range(4)]
            if h == t:
                r = [jnp.where(in_lane, jnp.where(lane == l0 + j, 1.0, 0.0), r[j]) for j in range(4)]
            rows.append([
                (w[m][0] * r[0] + w[m][1] * r[1]) + (w[m][2] * r[2] + w[m][3] * r[3]) for m in range(4)
            ])
        for i in range(4):
            c = cols[i]
            if i == i0:
                c = [jnp.where(in_row, jnp.where(sub == s0 + j, -1.0, 0.0), c[j]) for j in range(4)]
            for h in range(2):
                old = tiles[i][h]
                if h == t:
                    old = jnp.where(in_lane, 0.0, old)
                if i == i0:
                    old = jnp.where(in_row, 0.0, old)
                u = rows[h]
                tiles[i][h] = old - ((c[0] * u[0] + c[1] * u[1]) + (c[2] * u[2] + c[3] * u[3]))
    fx[...] = jnp.zeros_like(fx)
    inside = (lane >= base) & (lane < base + 28)
    for i in range(4):
        for h in range(2):
            f = tiles[i][h]
            if h == t:
                f = jnp.where(inside, -f, f)
            if i == 3:
                f = jnp.where(sub < 4, f, 0.0)
            fx[base + 8 * i : base + 8 * i + 8, TC * h : TC * h + TC] = f
    rest = mat[top + 32 : 200, TC * t : TC * t + TC]
    change = jnp.dot(rest, fx[...], preferred_element_type=F32, precision=lax.Precision.HIGHEST)
    for h in range(2):
        old = mat[top + 32 : 200, TC * h : TC * h + TC]
        if h == t:
            old = jnp.where(inside, 0.0, old)
        mat[top + 32 : 200, TC * h : TC * h + TC] = old - change[:, TC * h : TC * h + TC]


def apply_stage(order, first_row, moms, e_ref, sci, upow, out, mat, fx):
    units = [jnp.concatenate([moms[4 * i + j] for j in range(4)], axis=0) for i in range(4)]
    lane = lax.broadcasted_iota(jnp.int32, (1, TC), 1)
    row = lax.broadcasted_iota(jnp.int32, (32, 1), 0)
    degree = lambda q: 0 if q == 0 else (1 if q < 3 else 2)

    def col_active(t):
        q = lax.shift_right_logical(lane, 5) + 4 * t
        deg = jnp.where(q >= 1, 1, 0) + jnp.where(q >= 3, 1, 0)
        return (deg <= order) | (lax.bitwise_and(lane, 31) == ONES)

    for q in range(6):
        row_on = (degree(q) <= order) | (row == ONES)
        for t in range(2):
            block = jnp.zeros((32, TC), F32)
            for s in range(4 if t == 0 else 2):
                p = 4 * t + s
                i, k = unit_of(mono[q][0] + mono[p][0], mono[q][1] + mono[p][1])
                piece = units[i]
                if s != k:
                    piece = pltpu.roll(piece, (32 * (s - k)) % 128, 1)
                block = jnp.where(lax.shift_right_logical(lane, 5) == s, piece, block)
            both = row_on & col_active(t)
            block = jnp.where(both, block, 0.0)
            if t == q // 4:
                diag = lane == row + 32 * (q % 4)
                block = jnp.where(diag, jnp.where(both, block, 1.0) * (1.0 + ridge), block)
            mat[32 * q : 32 * q + 32, TC * t : TC * t + TC] = block
            if q == 0:
                mat[192:200, TC * t : TC * t + TC] = jnp.where(col_active(t), block[24:32], 0.0)
    for q in range(6):
        sweep_panel(mat, fx, q, lane)
    coef = []
    for q in range(6):
        z = mat[192:200, TC * (q // 4) : TC * (q // 4) + TC]
        z = jnp.broadcast_to(z[TARGET - 24 : TARGET - 23], (8, TC))
        if q % 4:
            z = pltpu.roll(z, 128 - 32 * (q % 4), 1)
        z = jnp.where(lane < 28, z, 0.0)
        z = z + pltpu.roll(z, 32, 1)
        z = z + pltpu.roll(z, 64, 1)
        coef.append(jnp.concatenate([z, z], axis=0))
    row16 = lax.broadcasted_iota(jnp.int32, (16, 1), 0)
    v = (first_row + row16).astype(F32) * (2.0 / 256.0) + (1.0 / 256.0 - 1.0)
    parts = (coef[0] + v * (coef[2] + v * coef[5]), coef[1] + v * coef[4], coef[3])
    his, los = [], []
    for p in parts:
        wide_p = jnp.concatenate(
            [jnp.where(row16 == 4 * n + lax.shift_right_logical(lane, 5), p, 0.0) for n in range(4)],
            axis=1,
        )
        h = wide_p.astype(BF16)
        his.append(h)
        los.append((wide_p - h.astype(F32)).astype(BF16))
    res = jnp.dot(jnp.concatenate(his + los, axis=0), e_ref[...], preferred_element_type=F32)
    t0, t1, t2 = (res[16 * i : 16 * i + 16] + res[48 + 16 * i : 64 + 16 * i] for i in range(3))
    u = upow[0:1, :]
    out[...] = sci[...] - (t0 + u * (t1 + u * t2))


MESH = pl.DeviceIdType.MESH


def whole_kernel(
    ccds, strips, pick, owner, shift, order, store, sci_h, band_h, va_h, vb_h, upow_h, out,
    sent, got, own, edge, sci, band, va, vb, upow, e, rolled, hs, acc, mom, parts, part, totals, mat, fx,
    local, send, recv, esend, erecv, s1, r1, s2, r2,
):
    ccd = lax.axis_index("ccd")
    strip = lax.axis_index("strip")
    count = ccds * strips
    me = ccd * strips + strip
    barrier = pltpu.get_barrier_semaphore()
    loads = [
        pltpu.make_async_copy(h, v, local.at[i])
        for i, (h, v) in enumerate(
            ((band_h, band), (va_h, va), (vb_h, vb), (upow_h, upow), (sci_h, sci))
        )
    ]

    def peer(k):
        return lax.rem(ccd + k // strips, ccds), lax.rem(strip + lax.rem(k, strips), strips)

    def greet(k, carry):
        pl.semaphore_signal(barrier, inc=1, device_id=peer(k), device_id_type=MESH)
        return carry

    lax.fori_loop(1, count, greet, 0)
    for load in loads:
        load.start()

    def choose(d, carry):
        sent[d] = store[pick[d]]
        return carry

    lax.fori_loop(0, count, choose, 0, unroll=8)
    got[me] = sent[me]
    pl.semaphore_wait(barrier, count - 1)

    def push(k, carry):
        to = peer(k)
        pltpu.make_async_remote_copy(
            src_ref=sent.at[to[0] * strips + to[1]],
            dst_ref=got.at[me],
            send_sem=send,
            recv_sem=recv,
            device_id=to,
            device_id_type=MESH,
        ).start()
        return carry

    lax.fori_loop(1, count, push, 0)
    rest = got.at[pl.ds(0, count - 1)]
    pltpu.make_async_copy(rest, rest, recv).wait()
    for t in range(own.shape[0]):
        own[t] = got[owner[t]]
    edges = [
        pltpu.make_async_remote_copy(
            src_ref=own,
            dst_ref=edge.at[way],
            send_sem=esend.at[way],
            recv_sem=erecv.at[way],
            device_id=(ccd, lax.rem(strip + (1 if way == 0 else strips - 1), strips)),
            device_id_type=MESH,
        )
        for way in range(2)
    ]
    for copy in edges:
        copy.start()
    for load in loads:
        load.wait()
    for copy in edges:
        copy.wait()
    above = jnp.where(strip > 0, edge[0], 0.0)
    below = jnp.where(strip < strips - 1, edge[1], 0.0)
    first_row = strip * ROWS
    fit_stage(shift[0], first_row, own, above, below, sci, band, va, vb, upow, e, mom, rolled, hs, acc)
    peers = [(ccd, lax.rem(strip + k, strips)) for k in range(1, strips)]
    for to in peers:
        pltpu.make_async_remote_copy(
            src_ref=mom.at[to[1]],
            dst_ref=parts.at[strip],
            send_sem=s1,
            recv_sem=r1,
            device_id=to,
            device_id_type=MESH,
        ).start()
    parts[strip] = mom[strip]
    few = parts.at[pl.ds(0, strips - 1)]
    pltpu.make_async_copy(few, few, r1).wait()
    total = parts[0]
    for i in range(1, strips):
        total = total + parts[i]
    part[...] = total
    for to in peers:
        pltpu.make_async_remote_copy(
            src_ref=part,
            dst_ref=totals.at[strip],
            send_sem=s2,
            recv_sem=r2,
            device_id=to,
            device_id_type=MESH,
        ).start()
    totals[strip] = total
    pltpu.make_async_copy(few, few, r2).wait()
    apply_stage(order[0], first_row, totals, e, sci, upow, out, mat, fx)
    pltpu.make_async_copy(rest, rest, send).wait()
    pltpu.make_async_copy(few, few, s1).wait()
    pltpu.make_async_copy(few, few, s2).wait()


VM = pl.BlockSpec(memory_space=pltpu.VMEM)
SM = pl.BlockSpec(memory_space=pltpu.SMEM)
ANY = pl.BlockSpec(memory_space=pl.ANY)
LIMIT = 60 * 1024 * 1024


def whole(pick, owner, shift, order, store, sci, ccds, strips):
    count = ccds * strips
    tiles = (owner.shape[0], *store.shape[1:])
    tables = [band_matrix(), *vertical_matrices(), column_powers()]
    blocks = pltpu.VMEM((strips, 128 // strips, TC), F32)
    dma = pltpu.SemaphoreType.DMA
    return pl.pallas_call(
        lambda *refs: whole_kernel(ccds, strips, *refs),
        out_shape=jax.ShapeDtypeStruct((ROWS, COLS), F32),
        in_specs=[SM] * 4 + [VM] + [ANY] * 5,
        out_specs=VM,
        scratch_shapes=[
            pltpu.VMEM((count, *store.shape[1:]), F32),
            pltpu.VMEM((count, *store.shape[1:]), F32),
            pltpu.VMEM(tiles, F32),
            pltpu.VMEM((2, *tiles), F32),
            pltpu.VMEM((ROWS, COLS), F32),
            *[pltpu.VMEM(x.shape, x.dtype) for x in tables],
            pltpu.VMEM((ROWS * 32, COLS), BF16),
            pltpu.VMEM((tiles[0] + 1, SLOTS, TC), F32),
            pltpu.VMEM((440, COLS), F32),
            pltpu.VMEM((5, 64, TC), F32),
            blocks,
            blocks,
            pltpu.VMEM((128 // strips, TC), F32),
            blocks,
            pltpu.VMEM((200, 2 * TC), F32),
            pltpu.VMEM((TC, 2 * TC), F32),
            dma((5,)),
            dma,
            dma,
            dma((2,)),
            dma((2,)),
            dma,
            dma,
            dma,
            dma,
        ],
        compiler_params=pltpu.CompilerParams(
            collective_id=0, has_side_effects=True, vmem_limit_bytes=LIMIT
        ),
        name="whole",
    )(pick, owner, shift, order, store, sci, *[jnp.asarray(x) for x in tables])


def body(tile_store, tile_source, tile_slot, shift_cols, spatial_order, science):
    strips = lax.axis_size("strip")
    me = lax.axis_index("ccd") * strips + lax.axis_index("strip")
    pick = jnp.sum(jnp.where(tile_source == me, tile_slot, 0), axis=1)
    owner = lax.dynamic_index_in_dim(tile_source, me, 0, keepdims=False)
    return whole(
        pick, owner, shift_cols, spatial_order, tile_store, science, lax.axis_size("ccd"), strips
    )


def solution(mesh):
    placed = (
        P(("ccd", "strip"), None, None),
        P(),
        P(),
        P("ccd"),
        P("ccd"),
        P(("ccd", "strip"), None),
    )
    return jax.shard_map(
        body, mesh=mesh, in_specs=placed, out_specs=P(("ccd", "strip"), None), check_vma=False
    )
```

```python
import jax
import jax.numpy as jnp
import numpy as np
from jax import lax
from jax.experimental import pallas as pl
from jax.experimental.pallas import tpu as pltpu
from jax.sharding import PartitionSpec as P

H = 11
CM = 128
ROWS = 16
COLS = 2048
TC = 128
SLOTS = 40
TARGET = 28
ONES = 15

sigmas = (0.7, 1.5, 3.0)
tops = (4, 2, 2)
mono = ((0, 0), (1, 0), (0, 1), (2, 0), (1, 1), (0, 2))
ridge = 0.05
F32 = jnp.float32
BF16 = jnp.bfloat16


def tap_table():
    a = np.arange(-H, H + 1).astype(np.float64)
    rows = []
    for s, top in zip(sigmas, tops):
        e = np.exp(-a * a / (2.0 * s * s))
        for n in range(top + 1):
            rows.append(e * (a / s) ** n / e.sum())
    return np.stack(rows).astype(np.float32)


def to_bf16(x):
    return x.astype(jnp.bfloat16.dtype)


def band_matrix():
    taps = tap_table()
    hi = to_bf16(taps).astype(np.float32)
    lo = to_bf16(taps - hi).astype(np.float32)
    full = []
    for part in (hi, lo):
        m = np.zeros((160, 11, TC), np.float32)
        for f in range(11):
            for x in range(TC):
                m[x : x + 23, f, x] = part[f]
        full.append(m.reshape(160, 11 * TC))
    h, l = full
    tail = np.zeros((TC, 11 * TC), np.float32)
    tail[0:32], tail[32:64], tail[64:96] = h[128:], h[128:], l[128:]
    return to_bf16(np.concatenate([h[:128], h[:128], l[:128], tail]))


def slot_of(row):
    return 16 + row if row < H else (row - H if row < H + ROWS else row)


def vertical_matrices():
    taps = to_bf16(tap_table()).astype(np.float32)
    first = np.zeros((ROWS, 16, 208), np.float32)
    second = np.zeros((ROWS, 16, 240), np.float32)
    slot = 0
    for i in range(5):
        for j in range(5 - i):
            for r in range(ROWS):
                for a in range(23):
                    first[r, slot, i * SLOTS + slot_of(r + a)] = taps[j, a]
            slot += 1
    first[:, ONES, 38] = 1.0
    slot = 0
    for g in range(2):
        for i in range(3):
            for j in range(3 - i):
                for r in range(ROWS):
                    for a in range(23):
                        second[r, slot, (3 * g + i) * SLOTS + slot_of(r + a)] = taps[5 + 3 * g + j, a]
                slot += 1
    return to_bf16(first.reshape(256, 208)), to_bf16(second.reshape(256, 240))


def column_powers():
    u = 2.0 * (np.arange(COLS).astype(np.float32) + np.float32(0.5)) / np.float32(COLS) - np.float32(1.0)
    u = u.astype(np.float32)
    return u


def column_rows():
    return np.stack([column_powers()] * 8)


def column_factors():
    u = column_powers()
    return to_bf16(np.concatenate([np.stack([u ** (k + 1)] * 16) for k in range(4)]))


def fit_stage(shift, first_row, own, above, below, sci, band, va, vb, powers, e_out, mom_out, rolled, hs, acc, last):
    start = CM + shift - H
    tile = lax.shift_right_logical(start, 7)
    rem = lax.bitwise_and(start, 127)
    count = own.shape[0]
    row16 = lax.broadcasted_iota(jnp.int32, (1, 16, TC), 1)
    row8 = lax.broadcasted_iota(jnp.int32, (1, 8, TC), 1)
    a = pltpu.roll(above, H, 1)
    b = pltpu.roll(below, H, 1)
    mid = jnp.where(row16 < H, a, b)
    end = jnp.where(row8 < 6, b[:, :8], jnp.where(row8 == 6, 1.0, 0.0))
    x = jnp.concatenate([own[...], mid, end], axis=1)
    rolled[0:count] = pltpu.roll(x, lax.bitwise_and(128 - rem, 127), 2)
    rolled[count : count + 1] = jnp.zeros((1, SLOTS, TC), F32)
    lane3 = lax.broadcasted_iota(jnp.int32, (1, SLOTS, TC), 2)
    w = jnp.where(
        lane3 < 128 - rem, rolled[pl.ds(tile, 17)], rolled[pl.ds(tile + 1, 17)]
    ).reshape(17 * SLOTS, TC)
    main = w[: 16 * SLOTS]
    nxt = w[SLOTS:]
    hi = main.astype(BF16)
    lo = (main - hi.astype(F32)).astype(BF16)
    nhi = nxt.astype(BF16).astype(F32)
    nlo = nxt - nhi
    lane = lax.broadcasted_iota(jnp.int32, (1, TC), 1)
    tail = jnp.where(
        lane < 32,
        nhi,
        jnp.where(lane < 64, pltpu.roll(nlo, 32, 1), jnp.where(lane < 96, pltpu.roll(nhi, 64, 1), 0.0)),
    ).astype(BF16)
    lhs = jnp.concatenate([hi, lo, hi, tail], axis=1)
    for c in range(6):
        n = 256 if c < 5 else 128
        res = jnp.dot(lhs, band[:, 256 * c : 256 * c + n], preferred_element_type=F32)
        for f in range(2 * c, 2 * c + n // TC):
            o = (f - 2 * c) * TC
            for j in range(16):
                hs[f * SLOTS : (f + 1) * SLOTS, j * TC : (j + 1) * TC] = res[
                    j * SLOTS : (j + 1) * SLOTS, o : o + TC
                ]
    sub8 = lax.broadcasted_iota(jnp.int32, (8, 1), 0)
    for c in range(8):
        cols = slice(256 * c, 256 * c + 256)
        oa = jnp.dot(va[...], hs[0:208, cols].astype(BF16), preferred_element_type=F32)
        ob = jnp.dot(vb[...], hs[200:440, cols].astype(BF16), preferred_element_type=F32)
        pieces = []
        for r in range(ROWS):
            pieces += [
                oa[16 * r : 16 * r + 16],
                ob[16 * r : 16 * r + 8],
                jnp.where(sub8 == TARGET - 24, sci[r : r + 1, cols], ob[16 * r + 8 : 16 * r + 16]),
            ]
        e_out[:, cols] = jnp.concatenate(pieces, axis=0).astype(BF16)
    acc[...] = jnp.zeros_like(acc)

    def row_step(r, carry):
        e = e_out[pl.ds(pl.multiple_of(r * 32, 32), 32), :]
        rows = [e]
        for k in range(4):
            p = powers[16 * k : 16 * k + 16, :]
            rows += [e[0:16] * p, e[16:32] * p]
        g = lax.dot_general(
            e,
            jnp.concatenate(rows, axis=0),
            (((1,), (1,)), ((), ())),
            preferred_element_type=F32,
        )
        v = (first_row + r).astype(F32) * (2.0 / 256.0) + (1.0 / 256.0 - 1.0)
        last[:, 0:32] += g[:, TC : TC + 32]
        g = g[:, 0:TC]
        scale = v
        acc[0] += g
        for m in range(1, 5):
            acc[m] += g * scale
            scale = scale * v
        return carry

    last[...] = jnp.zeros_like(last)
    lax.fori_loop(0, ROWS, row_step, 0, unroll=4)
    units = (
        acc[0],
        acc[1],
        jnp.where(lane < 96, acc[2], pltpu.roll(last[...], 96, 1)),
        jnp.where(lane < 64, acc[3], pltpu.roll(acc[4], 64, 1)),
    )
    for i, unit in enumerate(units):
        for j in range(4):
            mom_out[4 * i + j] = unit[8 * j : 8 * j + 8]


def unit_of(k, m):
    if m < 2 and k < 4:
        return m, k
    if m == 2:
        return 2, k
    return {(4, 0): (2, 3), (0, 3): (3, 0), (1, 3): (3, 1), (0, 4): (3, 2)}[(k, m)]


def inverse2(m):
    (a, b), (c, d) = m
    r = 1.0 / (a * d - b * c)
    return (d * r, -b * r), (-c * r, a * r)


def times2(x, y):
    return tuple(tuple(x[i][0] * y[0][j] + x[i][1] * y[1][j] for j in range(2)) for i in range(2))


def plus2(x, y, sign):
    return tuple(tuple(x[i][j] + sign * y[i][j] for j in range(2)) for i in range(2))


def inverse4(p):
    part = lambda i, j: tuple(tuple(p[2 * i + a][2 * j + b] for b in range(2)) for a in range(2))
    head = inverse2(part(0, 0))
    x = times2(head, part(0, 1))
    y = times2(part(1, 0), head)
    tail = inverse2(plus2(part(1, 1), times2(part(1, 0), x), -1.0))
    xt = times2(x, tail)
    low = times2(tail, y)
    top = plus2(head, times2(xt, y), 1.0)
    return [
        [top[i][j] if i < 2 and j < 2 else tail[i - 2][j - 2] if i > 1 and j > 1
         else -xt[i][j - 2] if i < 2 else -low[i - 2][j] for j in range(4)]
        for i in range(4)
    ]


def sweep_panel(mat, zero, q, lane):
    t = q // 4
    top = 32 * q
    base = 32 * (q % 4)
    sub = lax.broadcasted_iota(jnp.int32, (8, TC), 0)
    tiles = [[mat[top + 8 * i : top + 8 * i + 8, TC * h : TC * h + TC] for h in range(2)] for i in range(4)]
    for k in range(0, 28, 4):
        i0, s0, l0 = k // 8, k % 8, base + k
        cols = [
            [jnp.broadcast_to(tiles[i][t][:, l0 + j : l0 + j + 1], (8, TC)) for j in range(4)]
            for i in range(4)
        ]
        whole_cols = [cols[i0][j] + zero for j in range(4)]
        p = [
            [jnp.broadcast_to(whole_cols[j][s0 + i : s0 + i + 1], (8, TC)) for j in range(4)]
            for i in range(4)
        ]
        w = inverse4(p)
        in_lane = (lane >= l0) & (lane < l0 + 4)
        in_row = (sub >= s0) & (sub < s0 + 4)
        rows = []
        for h in range(2):
            r = [jnp.broadcast_to(tiles[i0][h][s0 + j : s0 + j + 1], (8, TC)) for j in range(4)]
            if h == t:
                r = [jnp.where(in_lane, jnp.where(lane == l0 + j, 1.0, 0.0), r[j]) for j in range(4)]
            rows.append([
                (w[m][0] * r[0] + w[m][1] * r[1]) + (w[m][2] * r[2] + w[m][3] * r[3]) for m in range(4)
            ])
        for i in range(4):
            c = cols[i]
            if i == i0:
                c = [jnp.where(in_row, jnp.where(sub == s0 + j, -1.0, 0.0), c[j]) for j in range(4)]
            for h in range(2):
                old = tiles[i][h]
                if h == t:
                    old = jnp.where(in_lane, 0.0, old)
                if i == i0:
                    old = jnp.where(in_row, 0.0, old)
                u = rows[h]
                tiles[i][h] = old - ((c[0] * u[0] + c[1] * u[1]) + (c[2] * u[2] + c[3] * u[3]))
    inside = (lane >= base) & (lane < base + 28)
    swept = [[], []]
    for i in range(4):
        for h in range(2):
            f = tiles[i][h]
            if h == t:
                f = jnp.where(inside, -f, f)
            if i == 3:
                f = jnp.where(sub < 4, f, 0.0)
            swept[h].append(f)
    f = jnp.concatenate([jnp.concatenate(swept[h], axis=0) for h in range(2)], axis=1)
    f_hi = f.astype(BF16)
    f = f - f_hi.astype(F32)
    f_mid = f.astype(BF16)
    f_lo = (f - f_mid.astype(F32)).astype(BF16)
    right = jnp.concatenate(
        [f_hi, f_mid, f_hi, f_lo, f_hi, f_mid, jnp.zeros((64, 2 * TC), BF16)], axis=0
    )
    z = jnp.where(inside, mat[top + 32 : 200, TC * t : TC * t + TC], 0.0)
    if base:
        z = pltpu.roll(z, 128 - base, 1)
    z = z + pltpu.roll(z, 32, 1)
    z = z + pltpu.roll(z, 64, 1)
    z_hi = z.astype(BF16).astype(F32)
    z = z - z_hi
    z_mid = z.astype(BF16).astype(F32)
    z_lo = z - z_mid
    slot = lax.shift_right_logical(lane, 5)
    left = jnp.concatenate(
        [
            jnp.where(slot == 2, z_mid, z_hi),
            jnp.where(slot == 0, z_lo, jnp.where(slot == 1, z_mid, 0.0)),
        ],
        axis=1,
    ).astype(BF16)
    change = jnp.dot(left, right, preferred_element_type=F32)
    for h in range(2):
        old = mat[top + 32 : 200, TC * h : TC * h + TC]
        if h == t:
            old = jnp.where(inside, 0.0, old)
        mat[top + 32 : 200, TC * h : TC * h + TC] = old - change[:, TC * h : TC * h + TC]


def apply_stage(order, first_row, moms, e_ref, sci, upow, out, mat, fx):
    units = [jnp.concatenate([moms[4 * i + j] for j in range(4)], axis=0) for i in range(4)]
    lane = lax.broadcasted_iota(jnp.int32, (1, TC), 1)
    row = lax.broadcasted_iota(jnp.int32, (32, 1), 0)
    degree = lambda q: 0 if q == 0 else (1 if q < 3 else 2)

    def col_active(t):
        q = lax.shift_right_logical(lane, 5) + 4 * t
        deg = jnp.where(q >= 1, 1, 0) + jnp.where(q >= 3, 1, 0)
        return (deg <= order) | (lax.bitwise_and(lane, 31) == ONES)

    for q in range(6):
        row_on = (degree(q) <= order) | (row == ONES)
        for t in range(2):
            block = jnp.zeros((32, TC), F32)
            for s in range(4 if t == 0 else 2):
                p = 4 * t + s
                i, k = unit_of(mono[q][0] + mono[p][0], mono[q][1] + mono[p][1])
                piece = units[i]
                if s != k:
                    piece = pltpu.roll(piece, (32 * (s - k)) % 128, 1)
                block = jnp.where(lax.shift_right_logical(lane, 5) == s, piece, block)
            both = row_on & col_active(t)
            block = jnp.where(both, block, 0.0)
            if t == q // 4:
                diag = lane == row + 32 * (q % 4)
                block = jnp.where(diag, jnp.where(both, block, 1.0) * (1.0 + ridge), block)
            mat[32 * q : 32 * q + 32, TC * t : TC * t + TC] = block
            if q == 0:
                mat[192:200, TC * t : TC * t + TC] = jnp.where(col_active(t), block[24:32], 0.0)
    fx[...] = jnp.zeros_like(fx)
    zero = fx[...]
    for q in range(6):
        sweep_panel(mat, zero, q, lane)
    coef = []
    for q in range(6):
        z = mat[192:200, TC * (q // 4) : TC * (q // 4) + TC]
        z = jnp.broadcast_to(z[TARGET - 24 : TARGET - 23], (8, TC))
        if q % 4:
            z = pltpu.roll(z, 128 - 32 * (q % 4), 1)
        z = jnp.where(lane < 28, z, 0.0)
        z = z + pltpu.roll(z, 32, 1)
        z = z + pltpu.roll(z, 64, 1)
        coef.append(jnp.concatenate([z, z], axis=0))
    row16 = lax.broadcasted_iota(jnp.int32, (16, 1), 0)
    v = (first_row + row16).astype(F32) * (2.0 / 256.0) + (1.0 / 256.0 - 1.0)
    parts = (coef[0] + v * (coef[2] + v * coef[5]), coef[1] + v * coef[4], coef[3])
    his, los = [], []
    for p in parts:
        wide_p = jnp.concatenate(
            [jnp.where(row16 == 4 * n + lax.shift_right_logical(lane, 5), p, 0.0) for n in range(4)],
            axis=1,
        )
        h = wide_p.astype(BF16)
        his.append(h)
        los.append((wide_p - h.astype(F32)).astype(BF16))
    res = jnp.dot(jnp.concatenate(his + los, axis=0), e_ref[...], preferred_element_type=F32)
    t0, t1, t2 = (res[16 * i : 16 * i + 16] + res[48 + 16 * i : 64 + 16 * i] for i in range(3))
    u = jnp.concatenate([upow[...]] * 2, axis=0)
    out[...] = sci[...] - (t0 + u * (t1 + u * t2))


MESH = pl.DeviceIdType.MESH


def whole_kernel(
    ccds, strips, pick, owner, shift, order, store, sci_h, band_h, va_h, vb_h, upow_h, powers_h, out,
    sent, got, own, edge, sci, band, va, vb, upow, powers, e, rolled, hs, acc, last, mom, parts, part, totals, mat, fx,
    local, send, recv, esend, erecv, s1, r1, s2, r2,
):
    ccd = lax.axis_index("ccd")
    strip = lax.axis_index("strip")
    count = ccds * strips
    me = ccd * strips + strip
    barrier = pltpu.get_barrier_semaphore()
    loads = [
        pltpu.make_async_copy(h, v, local.at[i])
        for i, (h, v) in enumerate(
            ((band_h, band), (va_h, va), (vb_h, vb), (upow_h, upow), (powers_h, powers), (sci_h, sci))
        )
    ]

    beside = [lax.rem(strip + k, strips) for k in range(strips)]

    def each_peer(act):
        def plane(i, carry):
            to = lax.rem(ccd + ccds - 1 - i, ccds)
            for k in range(strips - 1, -1, -1):
                act(to, beside[k])
            return carry

        lax.fori_loop(0, ccds - 1, plane, 0)
        for k in range(strips - 1, 0, -1):
            act(ccd, beside[k])

    each_peer(
        lambda c, k: pl.semaphore_signal(barrier, inc=1, device_id=(c, k), device_id_type=MESH)
    )
    for load in loads:
        load.start()

    def choose(d, carry):
        sent[d] = store[pick[d]]
        return carry

    lax.fori_loop(0, count, choose, 0, unroll=8)
    got[me] = sent[me]
    pl.semaphore_wait(barrier, count - 1)

    each_peer(
        lambda c, k: pltpu.make_async_remote_copy(
            src_ref=sent.at[c * strips + k],
            dst_ref=got.at[me],
            send_sem=send,
            recv_sem=recv,
            device_id=(c, k),
            device_id_type=MESH,
        ).start()
    )
    rest = got.at[pl.ds(0, count - 1)]
    pltpu.make_async_copy(rest, rest, recv).wait()
    for t in range(own.shape[0]):
        own[t] = got[owner[t]]
    edges = [
        pltpu.make_async_remote_copy(
            src_ref=own,
            dst_ref=edge.at[way],
            send_sem=esend.at[way],
            recv_sem=erecv.at[way],
            device_id=(ccd, lax.rem(strip + (1 if way == 0 else strips - 1), strips)),
            device_id_type=MESH,
        )
        for way in range(2)
    ]
    for copy in edges:
        copy.start()
    for load in loads:
        load.wait()
    for copy in edges:
        copy.wait()
    above = jnp.where(strip > 0, edge[0], 0.0)
    below = jnp.where(strip < strips - 1, edge[1], 0.0)
    first_row = strip * ROWS
    fit_stage(shift[0], first_row, own, above, below, sci, band, va, vb, powers, e, mom, rolled, hs, acc, last)
    peers = [(ccd, k) for k in beside[1:]]
    for to in peers:
        pltpu.make_async_remote_copy(
            src_ref=mom.at[to[1]],
            dst_ref=parts.at[strip],
            send_sem=s1,
            recv_sem=r1,
            device_id=to,
            device_id_type=MESH,
        ).start()
    parts[strip] = mom[strip]
    few = parts.at[pl.ds(0, strips - 1)]
    pltpu.make_async_copy(few, few, r1).wait()
    total = parts[0]
    for i in range(1, strips):
        total = total + parts[i]
    part[...] = total
    for to in peers:
        pltpu.make_async_remote_copy(
            src_ref=part,
            dst_ref=totals.at[strip],
            send_sem=s2,
            recv_sem=r2,
            device_id=to,
            device_id_type=MESH,
        ).start()
    totals[strip] = total
    pltpu.make_async_copy(few, few, r2).wait()
    apply_stage(order[0], first_row, totals, e, sci, upow, out, mat, fx)
    pltpu.make_async_copy(rest, rest, send).wait()
    pltpu.make_async_copy(few, few, s1).wait()
    pltpu.make_async_copy(few, few, s2).wait()


VM = pl.BlockSpec(memory_space=pltpu.VMEM)
SM = pl.BlockSpec(memory_space=pltpu.SMEM)
ANY = pl.BlockSpec(memory_space=pl.ANY)
LIMIT = 60 * 1024 * 1024


def whole(pick, owner, shift, order, store, sci, ccds, strips):
    count = ccds * strips
    tiles = (owner.shape[0], *store.shape[1:])
    tables = [band_matrix(), *vertical_matrices(), column_rows(), column_factors()]
    blocks = pltpu.VMEM((strips, 128 // strips, TC), F32)
    dma = pltpu.SemaphoreType.DMA
    return pl.pallas_call(
        lambda *refs: whole_kernel(ccds, strips, *refs),
        out_shape=jax.ShapeDtypeStruct((ROWS, COLS), F32),
        in_specs=[SM] * 4 + [VM] + [ANY] * 6,
        out_specs=VM,
        scratch_shapes=[
            pltpu.VMEM((count, *store.shape[1:]), F32),
            pltpu.VMEM((count, *store.shape[1:]), F32),
            pltpu.VMEM(tiles, F32),
            pltpu.VMEM((2, *tiles), F32),
            pltpu.VMEM((ROWS, COLS), F32),
            *[pltpu.VMEM(x.shape, x.dtype) for x in tables],
            pltpu.VMEM((ROWS * 32, COLS), BF16),
            pltpu.VMEM((tiles[0] + 1, SLOTS, TC), F32),
            pltpu.VMEM((440, COLS), F32),
            pltpu.VMEM((5, 32, TC), F32),
            pltpu.VMEM((32, TC), F32),
            blocks,
            blocks,
            pltpu.VMEM((128 // strips, TC), F32),
            blocks,
            pltpu.VMEM((200, 2 * TC), F32),
            pltpu.VMEM((8, TC), F32),
            dma((6,)),
            dma,
            dma,
            dma((2,)),
            dma((2,)),
            dma,
            dma,
            dma,
            dma,
        ],
        compiler_params=pltpu.CompilerParams(
            collective_id=0, has_side_effects=True, vmem_limit_bytes=LIMIT
        ),
        name="whole",
    )(pick, owner, shift, order, store, sci, *[jnp.asarray(x) for x in tables])


def body(tile_store, tile_source, tile_slot, shift_cols, spatial_order, science):
    strips = lax.axis_size("strip")
    me = lax.axis_index("ccd") * strips + lax.axis_index("strip")
    pick = jnp.sum(jnp.where(tile_source == me, tile_slot, 0), axis=1)
    owner = lax.dynamic_index_in_dim(tile_source, me, 0, keepdims=False)
    return whole(
        pick, owner, shift_cols, spatial_order, tile_store, science, lax.axis_size("ccd"), strips
    )


def solution(mesh):
    placed = (
        P(("ccd", "strip"), None, None),
        P(),
        P(),
        P("ccd"),
        P("ccd"),
        P(("ccd", "strip"), None),
    )
    return jax.shard_map(
        body, mesh=mesh, in_specs=placed, out_specs=P(("ccd", "strip"), None), check_vma=False
    )
```

```python
import jax
import jax.numpy as jnp
import numpy as np
from jax import lax
from jax.experimental import pallas as pl
from jax.experimental.pallas import tpu as pltpu
from jax.sharding import PartitionSpec as P

H = 11
CM = 128
ROWS = 16
COLS = 2048
TC = 128
SLOTS = 40
TARGET = 28
ONES = 15

sigmas = (0.7, 1.5, 3.0)
tops = (4, 2, 2)
mono = ((0, 0), (1, 0), (0, 1), (2, 0), (1, 1), (0, 2))
ridge = 0.05
F32 = jnp.float32
BF16 = jnp.bfloat16


def tap_table():
    a = np.arange(-H, H + 1).astype(np.float64)
    rows = []
    for s, top in zip(sigmas, tops):
        e = np.exp(-a * a / (2.0 * s * s))
        for n in range(top + 1):
            rows.append(e * (a / s) ** n / e.sum())
    return np.stack(rows).astype(np.float32)


def to_bf16(x):
    return x.astype(jnp.bfloat16.dtype)


def band_matrix():
    taps = tap_table()
    hi = to_bf16(taps).astype(np.float32)
    lo = to_bf16(taps - hi).astype(np.float32)
    full = []
    for part in (hi, lo):
        m = np.zeros((160, 11, TC), np.float32)
        for f in range(11):
            for x in range(TC):
                m[x : x + 23, f, x] = part[f]
        full.append(m.reshape(160, 11 * TC))
    h, l = full
    tail = np.zeros((TC, 11 * TC), np.float32)
    tail[0:32], tail[32:64], tail[64:96] = h[128:], h[128:], l[128:]
    return to_bf16(np.concatenate([h[:128], h[:128], l[:128], tail]))


def slot_of(row):
    return 16 + row if row < H else (row - H if row < H + ROWS else row)


def vertical_matrices():
    taps = to_bf16(tap_table()).astype(np.float32)
    first = np.zeros((ROWS, 16, 208), np.float32)
    second = np.zeros((ROWS, 16, 240), np.float32)
    slot = 0
    for i in range(5):
        for j in range(5 - i):
            for r in range(ROWS):
                for a in range(23):
                    first[r, slot, i * SLOTS + slot_of(r + a)] = taps[j, a]
            slot += 1
    first[:, ONES, 38] = 1.0
    slot = 0
    for g in range(2):
        for i in range(3):
            for j in range(3 - i):
                for r in range(ROWS):
                    for a in range(23):
                        second[r, slot, (3 * g + i) * SLOTS + slot_of(r + a)] = taps[5 + 3 * g + j, a]
                slot += 1
    return to_bf16(first.reshape(256, 208)), to_bf16(second.reshape(256, 240))


def column_powers():
    u = 2.0 * (np.arange(COLS).astype(np.float32) + np.float32(0.5)) / np.float32(COLS) - np.float32(1.0)
    u = u.astype(np.float32)
    return u


def column_rows():
    return np.stack([column_powers()] * 8)


def column_factors():
    u = column_powers()
    return to_bf16(np.concatenate([np.stack([u ** (k + 1)] * 16) for k in range(4)]))


def fit_stage(shift, first_row, own, above, below, sci, band, va, vb, powers, e_out, mom_out, rolled, hs, acc, last):
    start = CM + shift - H
    tile = lax.shift_right_logical(start, 7)
    rem = lax.bitwise_and(start, 127)
    count = own.shape[0]
    row16 = lax.broadcasted_iota(jnp.int32, (1, 16, TC), 1)
    row8 = lax.broadcasted_iota(jnp.int32, (1, 8, TC), 1)
    a = pltpu.roll(above, H, 1)
    b = pltpu.roll(below, H, 1)
    mid = jnp.where(row16 < H, a, b)
    end = jnp.where(row8 < 6, b[:, :8], jnp.where(row8 == 6, 1.0, 0.0))
    x = jnp.concatenate([own[...], mid, end], axis=1)
    rolled[0:count] = pltpu.roll(x, lax.bitwise_and(128 - rem, 127), 2)
    rolled[count : count + 1] = jnp.zeros((1, SLOTS, TC), F32)
    lane3 = lax.broadcasted_iota(jnp.int32, (1, SLOTS, TC), 2)
    w = jnp.where(
        lane3 < 128 - rem, rolled[pl.ds(tile, 17)], rolled[pl.ds(tile + 1, 17)]
    ).reshape(17 * SLOTS, TC)
    main = w[: 16 * SLOTS]
    nxt = w[SLOTS:]
    hi = main.astype(BF16)
    lo = (main - hi.astype(F32)).astype(BF16)
    nhi = nxt.astype(BF16).astype(F32)
    nlo = nxt - nhi
    lane = lax.broadcasted_iota(jnp.int32, (1, TC), 1)
    tail = jnp.where(
        lane < 32,
        nhi,
        jnp.where(lane < 64, pltpu.roll(nlo, 32, 1), jnp.where(lane < 96, pltpu.roll(nhi, 64, 1), 0.0)),
    ).astype(BF16)
    lhs = jnp.concatenate([hi, lo, hi, tail], axis=1)
    for c in range(6):
        n = 256 if c < 5 else 128
        res = jnp.dot(lhs, band[:, 256 * c : 256 * c + n], preferred_element_type=F32)
        for f in range(2 * c, 2 * c + n // TC):
            o = (f - 2 * c) * TC
            for j in range(16):
                hs[f * SLOTS : (f + 1) * SLOTS, j * TC : (j + 1) * TC] = res[
                    j * SLOTS : (j + 1) * SLOTS, o : o + TC
                ]
    sub8 = lax.broadcasted_iota(jnp.int32, (8, 1), 0)
    for c in range(8):
        cols = slice(256 * c, 256 * c + 256)
        oa = jnp.dot(va[...], hs[0:208, cols].astype(BF16), preferred_element_type=F32)
        ob = jnp.dot(vb[...], hs[200:440, cols].astype(BF16), preferred_element_type=F32)
        pieces = []
        for r in range(ROWS):
            pieces += [
                oa[16 * r : 16 * r + 16],
                ob[16 * r : 16 * r + 8],
                jnp.where(sub8 == TARGET - 24, sci[r : r + 1, cols], ob[16 * r + 8 : 16 * r + 16]),
            ]
        e_out[:, cols] = jnp.concatenate(pieces, axis=0).astype(BF16)
    acc[...] = jnp.zeros_like(acc)

    def row_step(r, carry):
        e = e_out[pl.ds(pl.multiple_of(r * 32, 32), 32), :]
        rows = [e]
        for k in range(4):
            p = powers[16 * k : 16 * k + 16, :]
            rows += [e[0:16] * p, e[16:32] * p]
        g = lax.dot_general(
            e,
            jnp.concatenate(rows, axis=0),
            (((1,), (1,)), ((), ())),
            preferred_element_type=F32,
        )
        v = (first_row + r).astype(F32) * (2.0 / 256.0) + (1.0 / 256.0 - 1.0)
        last[:, 0:32] += g[:, TC : TC + 32]
        g = g[:, 0:TC]
        scale = v
        acc[0] += g
        for m in range(1, 5):
            acc[m] += g * scale
            scale = scale * v
        return carry

    last[...] = jnp.zeros_like(last)
    lax.fori_loop(0, ROWS, row_step, 0, unroll=4)
    units = (
        acc[0],
        acc[1],
        jnp.where(lane < 96, acc[2], pltpu.roll(last[...], 96, 1)),
        jnp.where(lane < 64, acc[3], pltpu.roll(acc[4], 64, 1)),
    )
    for i, unit in enumerate(units):
        for j in range(4):
            mom_out[4 * i + j] = unit[8 * j : 8 * j + 8]


def unit_of(k, m):
    if m < 2 and k < 4:
        return m, k
    if m == 2:
        return 2, k
    return {(4, 0): (2, 3), (0, 3): (3, 0), (1, 3): (3, 1), (0, 4): (3, 2)}[(k, m)]


def inverse2(m):
    (a, b), (c, d) = m
    r = 1.0 / (a * d - b * c)
    return (d * r, -b * r), (-c * r, a * r)


def times2(x, y):
    return tuple(tuple(x[i][0] * y[0][j] + x[i][1] * y[1][j] for j in range(2)) for i in range(2))


def plus2(x, y, sign):
    return tuple(tuple(x[i][j] + sign * y[i][j] for j in range(2)) for i in range(2))


def inverse4(p):
    part = lambda i, j: tuple(tuple(p[2 * i + a][2 * j + b] for b in range(2)) for a in range(2))
    head = inverse2(part(0, 0))
    x = times2(head, part(0, 1))
    y = times2(part(1, 0), head)
    tail = inverse2(plus2(part(1, 1), times2(part(1, 0), x), -1.0))
    xt = times2(x, tail)
    low = times2(tail, y)
    top = plus2(head, times2(xt, y), 1.0)
    return [
        [top[i][j] if i < 2 and j < 2 else tail[i - 2][j - 2] if i > 1 and j > 1
         else -xt[i][j - 2] if i < 2 else -low[i - 2][j] for j in range(4)]
        for i in range(4)
    ]


def sweep_panel(mat, zero, q, lane):
    t = q // 4
    top = 32 * q
    base = 32 * (q % 4)
    sub = lax.broadcasted_iota(jnp.int32, (8, TC), 0)
    tiles = [[mat[top + 8 * i : top + 8 * i + 8, TC * h : TC * h + TC] for h in range(2)] for i in range(4)]
    for k in range(0, 28, 4):
        i0, s0, l0 = k // 8, k % 8, base + k
        cols = [
            [jnp.broadcast_to(tiles[i][t][:, l0 + j : l0 + j + 1], (8, TC)) for j in range(4)]
            for i in range(4)
        ]
        whole_cols = [cols[i0][j] + zero for j in range(4)]
        p = [
            [jnp.broadcast_to(whole_cols[j][s0 + i : s0 + i + 1], (8, TC)) for j in range(4)]
            for i in range(4)
        ]
        w = inverse4(p)
        in_lane = (lane >= l0) & (lane < l0 + 4)
        in_row = (sub >= s0) & (sub < s0 + 4)
        rows = []
        for h in range(2):
            r = [jnp.broadcast_to(tiles[i0][h][s0 + j : s0 + j + 1], (8, TC)) for j in range(4)]
            if h == t:
                r = [jnp.where(in_lane, jnp.where(lane == l0 + j, 1.0, 0.0), r[j]) for j in range(4)]
            rows.append([
                (w[m][0] * r[0] + w[m][1] * r[1]) + (w[m][2] * r[2] + w[m][3] * r[3]) for m in range(4)
            ])
        for i in range(4):
            c = cols[i]
            if i == i0:
                c = [jnp.where(in_row, jnp.where(sub == s0 + j, -1.0, 0.0), c[j]) for j in range(4)]
            for h in range(2):
                old = tiles[i][h]
                if h == t:
                    old = jnp.where(in_lane, 0.0, old)
                if i == i0:
                    old = jnp.where(in_row, 0.0, old)
                u = rows[h]
                tiles[i][h] = old - ((c[0] * u[0] + c[1] * u[1]) + (c[2] * u[2] + c[3] * u[3]))
    inside = (lane >= base) & (lane < base + 28)
    swept = [[], []]
    for i in range(4):
        for h in range(2):
            f = tiles[i][h]
            if h == t:
                f = jnp.where(inside, -f, f)
            if i == 3:
                f = jnp.where(sub < 4, f, 0.0)
            swept[h].append(f)
    f = jnp.concatenate([jnp.concatenate(swept[h], axis=0) for h in range(2)], axis=1)
    f_hi = f.astype(BF16)
    f = f - f_hi.astype(F32)
    f_mid = f.astype(BF16)
    f_lo = (f - f_mid.astype(F32)).astype(BF16)
    right = jnp.concatenate(
        [f_hi, f_mid, f_hi, f_lo, f_hi, f_mid, jnp.zeros((64, 2 * TC), BF16)], axis=0
    )
    z = jnp.where(inside, mat[top + 32 : 200, TC * t : TC * t + TC], 0.0)
    if base:
        z = pltpu.roll(z, 128 - base, 1)
    z = z + pltpu.roll(z, 32, 1)
    z = z + pltpu.roll(z, 64, 1)
    z_hi = z.astype(BF16).astype(F32)
    z = z - z_hi
    z_mid = z.astype(BF16).astype(F32)
    z_lo = z - z_mid
    slot = lax.shift_right_logical(lane, 5)
    left = jnp.concatenate(
        [
            jnp.where(slot == 2, z_mid, z_hi),
            jnp.where(slot == 0, z_lo, jnp.where(slot == 1, z_mid, 0.0)),
        ],
        axis=1,
    ).astype(BF16)
    change = jnp.dot(left, right, preferred_element_type=F32)
    for h in range(2):
        old = mat[top + 32 : 200, TC * h : TC * h + TC]
        if h == t:
            old = jnp.where(inside, 0.0, old)
        mat[top + 32 : 200, TC * h : TC * h + TC] = old - change[:, TC * h : TC * h + TC]


def apply_stage(order, first_row, moms, e_ref, sci, upow, out, mat, fx):
    units = [jnp.concatenate([moms[4 * i + j] for j in range(4)], axis=0) for i in range(4)]
    lane = lax.broadcasted_iota(jnp.int32, (1, TC), 1)
    row = lax.broadcasted_iota(jnp.int32, (32, 1), 0)
    degree = lambda q: 0 if q == 0 else (1 if q < 3 else 2)

    def col_active(t):
        q = lax.shift_right_logical(lane, 5) + 4 * t
        deg = jnp.where(q >= 1, 1, 0) + jnp.where(q >= 3, 1, 0)
        return (deg <= order) | (lax.bitwise_and(lane, 31) == ONES)

    for q in range(6):
        row_on = (degree(q) <= order) | (row == ONES)
        for t in range(2):
            block = jnp.zeros((32, TC), F32)
            for s in range(4 if t == 0 else 2):
                p = 4 * t + s
                i, k = unit_of(mono[q][0] + mono[p][0], mono[q][1] + mono[p][1])
                piece = units[i]
                if s != k:
                    piece = pltpu.roll(piece, (32 * (s - k)) % 128, 1)
                block = jnp.where(lax.shift_right_logical(lane, 5) == s, piece, block)
            both = row_on & col_active(t)
            block = jnp.where(both, block, 0.0)
            if t == q // 4:
                diag = lane == row + 32 * (q % 4)
                block = jnp.where(diag, jnp.where(both, block, 1.0) * (1.0 + ridge), block)
            mat[32 * q : 32 * q + 32, TC * t : TC * t + TC] = block
            if q == 0:
                mat[192:200, TC * t : TC * t + TC] = jnp.where(col_active(t), block[24:32], 0.0)
    fx[...] = jnp.zeros_like(fx)
    zero = fx[...]
    for q in range(6):
        sweep_panel(mat, zero, q, lane)
    coef = []
    for q in range(6):
        z = mat[192:200, TC * (q // 4) : TC * (q // 4) + TC]
        z = jnp.broadcast_to(z[TARGET - 24 : TARGET - 23], (8, TC))
        if q % 4:
            z = pltpu.roll(z, 128 - 32 * (q % 4), 1)
        z = jnp.where(lane < 28, z, 0.0)
        z = z + pltpu.roll(z, 32, 1)
        z = z + pltpu.roll(z, 64, 1)
        coef.append(jnp.concatenate([z, z], axis=0))
    row16 = lax.broadcasted_iota(jnp.int32, (16, 1), 0)
    v = (first_row + row16).astype(F32) * (2.0 / 256.0) + (1.0 / 256.0 - 1.0)
    parts = (coef[0] + v * (coef[2] + v * coef[5]), coef[1] + v * coef[4], coef[3])
    his, los = [], []
    for p in parts:
        wide_p = jnp.concatenate(
            [jnp.where(row16 == 4 * n + lax.shift_right_logical(lane, 5), p, 0.0) for n in range(4)],
            axis=1,
        )
        h = wide_p.astype(BF16)
        his.append(h)
        los.append((wide_p - h.astype(F32)).astype(BF16))
    res = jnp.dot(jnp.concatenate(his + los, axis=0), e_ref[...], preferred_element_type=F32)
    t0, t1, t2 = (res[16 * i : 16 * i + 16] + res[48 + 16 * i : 64 + 16 * i] for i in range(3))
    u = jnp.concatenate([upow[...]] * 2, axis=0)
    out[...] = sci[...] - (t0 + u * (t1 + u * t2))


MESH = pl.DeviceIdType.MESH


def whole_kernel(
    ccds, strips, shift, order, source, slot, store, sci_h, band_h, va_h, vb_h, upow_h, powers_h, out,
    sent, got, own, edge, sci, band, va, vb, upow, powers, e, rolled, hs, acc, last, mom, parts, part, totals, mat, fx,
    table, index, local, index_sem, send, recv, esend, erecv, s1, r1, s2, r2,
):
    ccd = lax.axis_index("ccd")
    strip = lax.axis_index("strip")
    count = ccds * strips
    me = ccd * strips + strip
    barrier = pltpu.get_barrier_semaphore()
    loads = [
        pltpu.make_async_copy(h, v, local.at[i])
        for i, (h, v) in enumerate(
            ((band_h, band), (va_h, va), (vb_h, vb), (upow_h, upow), (powers_h, powers), (sci_h, sci))
        )
    ]

    beside = [lax.rem(strip + k, strips) for k in range(strips)]
    hops = (0, 1, 2, 1)
    turn = lambda i, k: lax.rem(i + k, 4)
    shifts = [(y, c, z, x) for y in range(4) for c in range(2) for z in range(4) for x in range(4)]
    shifts.sort(key=lambda o: -(hops[o[0]] + hops[o[2]] + hops[o[3]] + 0.5 * o[1]))
    rows = [[turn(ccd // 2, y) * 2 + lax.rem(ccd + c, 2) for c in range(2)] for y in range(4)]
    cells = [[turn(strip // 4, z) * 4 + turn(lax.rem(strip, 4), x) for x in range(4)] for z in range(4)]

    def each_peer(act):
        for y, c, z, x in shifts[:-1]:
            act(rows[y][c], cells[z][x])

    each_peer(
        lambda c, k: pl.semaphore_signal(barrier, inc=1, device_id=(c, k), device_id_type=MESH)
    )
    for load in loads:
        load.start()

    tiles = source.shape[0]
    pick = jnp.sum(jnp.where(source[...] == me, slot[...], 0), axis=0, keepdims=True)
    table[0:8] = jnp.broadcast_to(pick, (8, count))
    table[24:32] = jnp.zeros((8, count), jnp.int32)
    table[8 : 8 + tiles] = source[...]
    to_index = pltpu.make_async_copy(table, index, index_sem)
    to_index.start()
    to_index.wait()

    def choose(d, carry):
        sent[d] = store[index[0, d]]
        return carry

    lax.fori_loop(0, count, choose, 0, unroll=8)
    got[me] = sent[me]
    pl.semaphore_wait(barrier, count - 1)

    each_peer(
        lambda c, k: pltpu.make_async_remote_copy(
            src_ref=sent.at[c * strips + k],
            dst_ref=got.at[me],
            send_sem=send,
            recv_sem=recv,
            device_id=(c, k),
            device_id_type=MESH,
        ).start()
    )
    rest = got.at[pl.ds(0, count - 1)]
    pltpu.make_async_copy(rest, rest, recv).wait()
    for t in range(own.shape[0]):
        own[t] = got[index[8 + t, me]]
    edges = [
        pltpu.make_async_remote_copy(
            src_ref=own,
            dst_ref=edge.at[way],
            send_sem=esend.at[way],
            recv_sem=erecv.at[way],
            device_id=(ccd, lax.rem(strip + (1 if way == 0 else strips - 1), strips)),
            device_id_type=MESH,
        )
        for way in range(2)
    ]
    for copy in edges:
        copy.start()
    for load in loads:
        load.wait()
    for copy in edges:
        copy.wait()
    above = jnp.where(strip > 0, edge[0], 0.0)
    below = jnp.where(strip < strips - 1, edge[1], 0.0)
    first_row = strip * ROWS
    fit_stage(shift[0], first_row, own, above, below, sci, band, va, vb, powers, e, mom, rolled, hs, acc, last)
    peers = [(ccd, k) for k in beside[1:]]
    for to in peers:
        pltpu.make_async_remote_copy(
            src_ref=mom.at[to[1]],
            dst_ref=parts.at[strip],
            send_sem=s1,
            recv_sem=r1,
            device_id=to,
            device_id_type=MESH,
        ).start()
    parts[strip] = mom[strip]
    few = parts.at[pl.ds(0, strips - 1)]
    pltpu.make_async_copy(few, few, r1).wait()
    total = parts[0]
    for i in range(1, strips):
        total = total + parts[i]
    part[...] = total
    for to in peers:
        pltpu.make_async_remote_copy(
            src_ref=part,
            dst_ref=totals.at[strip],
            send_sem=s2,
            recv_sem=r2,
            device_id=to,
            device_id_type=MESH,
        ).start()
    totals[strip] = total
    pltpu.make_async_copy(few, few, r2).wait()
    apply_stage(order[0], first_row, totals, e, sci, upow, out, mat, fx)
    pltpu.make_async_copy(rest, rest, send).wait()
    pltpu.make_async_copy(few, few, s1).wait()
    pltpu.make_async_copy(few, few, s2).wait()


VM = pl.BlockSpec(memory_space=pltpu.VMEM)
SM = pl.BlockSpec(memory_space=pltpu.SMEM)
ANY = pl.BlockSpec(memory_space=pl.ANY)
LIMIT = 60 * 1024 * 1024


def whole(shift, order, source, slot, store, sci, ccds, strips):
    count = ccds * strips
    tiles = (source.shape[0], *store.shape[1:])
    tables = [band_matrix(), *vertical_matrices(), column_rows(), column_factors()]
    blocks = pltpu.VMEM((strips, 128 // strips, TC), F32)
    dma = pltpu.SemaphoreType.DMA
    return pl.pallas_call(
        lambda *refs: whole_kernel(ccds, strips, *refs),
        out_shape=pltpu.VMEM((ROWS, COLS), F32),
        in_specs=[SM] * 2 + [VM] * 3 + [ANY] * 6,
        out_specs=VM,
        scratch_shapes=[
            pltpu.VMEM((count, *store.shape[1:]), F32),
            pltpu.VMEM((count, *store.shape[1:]), F32),
            pltpu.VMEM(tiles, F32),
            pltpu.VMEM((2, *tiles), F32),
            pltpu.VMEM((ROWS, COLS), F32),
            *[pltpu.VMEM(x.shape, x.dtype) for x in tables],
            pltpu.VMEM((ROWS * 32, COLS), BF16),
            pltpu.VMEM((tiles[0] + 1, SLOTS, TC), F32),
            pltpu.VMEM((440, COLS), F32),
            pltpu.VMEM((5, 32, TC), F32),
            pltpu.VMEM((32, TC), F32),
            blocks,
            blocks,
            pltpu.VMEM((128 // strips, TC), F32),
            blocks,
            pltpu.VMEM((200, 2 * TC), F32),
            pltpu.VMEM((8, TC), F32),
            pltpu.VMEM((32, count), jnp.int32),
            pltpu.SMEM((32, count), jnp.int32),
            dma((6,)),
            dma,
            dma,
            dma,
            dma((2,)),
            dma((2,)),
            dma,
            dma,
            dma,
            dma,
        ],
        compiler_params=pltpu.CompilerParams(
            collective_id=0, has_side_effects=True, vmem_limit_bytes=LIMIT
        ),
        name="whole",
    )(shift, order, source, slot, store, sci, *[jnp.asarray(x) for x in tables])


def body(tile_store, tile_source, tile_slot, shift_cols, spatial_order, science):
    strips = lax.axis_size("strip")
    return whole(
        shift_cols, spatial_order, tile_source.T, tile_slot.T, tile_store, science,
        lax.axis_size("ccd"), strips,
    )


def solution(mesh):
    placed = (
        P(("ccd", "strip"), None, None),
        P(),
        P(),
        P("ccd"),
        P("ccd"),
        P(("ccd", "strip"), None),
    )
    return jax.shard_map(
        body, mesh=mesh, in_specs=placed, out_specs=P(("ccd", "strip"), None), check_vma=False
    )
```

```python
import jax
import jax.numpy as jnp
import numpy as np
from jax import lax
from jax.experimental import pallas as pl
from jax.experimental.pallas import tpu as pltpu
from jax.sharding import PartitionSpec as P

H = 11
CM = 128
ROWS = 16
COLS = 2048
TC = 128
SLOTS = 40
TARGET = 28
ONES = 15

sigmas = (0.7, 1.5, 3.0)
tops = (4, 2, 2)
mono = ((0, 0), (1, 0), (0, 1), (2, 0), (1, 1), (0, 2))
ridge = 0.05
F32 = jnp.float32
BF16 = jnp.bfloat16


def tap_table():
    a = np.arange(-H, H + 1).astype(np.float64)
    rows = []
    for s, top in zip(sigmas, tops):
        e = np.exp(-a * a / (2.0 * s * s))
        for n in range(top + 1):
            rows.append(e * (a / s) ** n / e.sum())
    return np.stack(rows).astype(np.float32)


def to_bf16(x):
    return x.astype(jnp.bfloat16.dtype)


def band_matrix():
    taps = tap_table()
    hi = to_bf16(taps).astype(np.float32)
    lo = to_bf16(taps - hi).astype(np.float32)
    full = []
    for part in (hi, lo):
        m = np.zeros((160, 11, TC), np.float32)
        for f in range(11):
            for x in range(TC):
                m[x : x + 23, f, x] = part[f]
        full.append(m.reshape(160, 11 * TC))
    h, l = full
    tail = np.zeros((TC, 11 * TC), np.float32)
    tail[0:32], tail[32:64], tail[64:96] = h[128:], h[128:], l[128:]
    return to_bf16(np.concatenate([h[:128], h[:128], l[:128], tail]))


def slot_of(row):
    return 16 + row if row < H else (row - H if row < H + ROWS else row)


def vertical_matrices():
    taps = to_bf16(tap_table()).astype(np.float32)
    first = np.zeros((ROWS, 16, 208), np.float32)
    second = np.zeros((ROWS, 16, 240), np.float32)
    slot = 0
    for i in range(5):
        for j in range(5 - i):
            for r in range(ROWS):
                for a in range(23):
                    first[r, slot, i * SLOTS + slot_of(r + a)] = taps[j, a]
            slot += 1
    first[:, ONES, 38] = 1.0
    slot = 0
    for g in range(2):
        for i in range(3):
            for j in range(3 - i):
                for r in range(ROWS):
                    for a in range(23):
                        second[r, slot, (3 * g + i) * SLOTS + slot_of(r + a)] = taps[5 + 3 * g + j, a]
                slot += 1
    return to_bf16(first.reshape(256, 208)), to_bf16(second.reshape(256, 240))


def column_powers():
    u = 2.0 * (np.arange(COLS).astype(np.float32) + np.float32(0.5)) / np.float32(COLS) - np.float32(1.0)
    u = u.astype(np.float32)
    return u


def column_rows():
    return np.stack([column_powers()] * 8)


def column_factors():
    u = column_powers()
    return to_bf16(np.concatenate([np.stack([u ** (k + 1)] * 16) for k in range(4)]))


def pack_rows(x):
    pairs = x.reshape(x.shape[0] // 2, 2, 16, TC)
    a, b = pairs[:, 0], pairs[:, 1]
    row = lax.broadcasted_iota(jnp.int32, (1, 8, TC), 1)
    mid = jnp.where(row < 3, a[:, 8:], pltpu.roll(b[:, :8], 3, 1))
    return jnp.concatenate([a[:, :8], mid, pltpu.roll(b, H, 1)[:, :8]], axis=1)


def unpack_rows(x):
    row = lax.broadcasted_iota(jnp.int32, (1, 8, TC), 1)
    end = pltpu.roll(x[:, 16:], 5, 1)
    b = jnp.concatenate([jnp.where(row < 5, pltpu.roll(x[:, 8:16], 5, 1), end), end], axis=1)
    pairs = jnp.concatenate([x[:, None, :16], b[:, None]], axis=1)
    return pairs.reshape(2 * x.shape[0], 16, TC)


def window_rows(shift, x, first, rolled, hs, band):
    count, rows, _ = x.shape
    start = CM + shift - H
    tile = lax.shift_right_logical(start, 7)
    rem = lax.bitwise_and(start, 127)
    rolled[0:count, 0:rows] = pltpu.roll(x, lax.bitwise_and(128 - rem, 127), 2)
    rolled[count : count + 1, 0:rows] = jnp.zeros((1, rows, TC), F32)
    lane3 = lax.broadcasted_iota(jnp.int32, (1, rows, TC), 2)
    w = jnp.where(
        lane3 < 128 - rem, rolled[pl.ds(tile, 17), 0:rows], rolled[pl.ds(tile + 1, 17), 0:rows]
    ).reshape(17 * rows, TC)
    main = w[: 16 * rows]
    nxt = w[rows:]
    hi = main.astype(BF16)
    lo = (main - hi.astype(F32)).astype(BF16)
    nhi = nxt.astype(BF16).astype(F32)
    nlo = nxt - nhi
    lane = lax.broadcasted_iota(jnp.int32, (1, TC), 1)
    tail = jnp.where(
        lane < 32,
        nhi,
        jnp.where(lane < 64, pltpu.roll(nlo, 32, 1), jnp.where(lane < 96, pltpu.roll(nhi, 64, 1), 0.0)),
    ).astype(BF16)
    lhs = jnp.concatenate([hi, lo, hi, tail], axis=1)
    for c in range(6):
        n = 256 if c < 5 else 128
        res = jnp.dot(lhs, band[:, 256 * c : 256 * c + n], preferred_element_type=F32)
        for f in range(2 * c, 2 * c + n // TC):
            o = (f - 2 * c) * TC
            for j in range(16):
                hs[f * SLOTS + first : f * SLOTS + first + rows, j * TC : (j + 1) * TC] = res[
                    j * rows : (j + 1) * rows, o : o + TC
                ]


def fit_stage(shift, first_row, above, below, sci, band, va, vb, powers, e_out, mom_out, rolled, hs, acc, last):
    row16 = lax.broadcasted_iota(jnp.int32, (1, 16, TC), 1)
    row8 = lax.broadcasted_iota(jnp.int32, (1, 8, TC), 1)
    lane = lax.broadcasted_iota(jnp.int32, (1, TC), 1)
    b = pltpu.roll(below, H, 1)
    mid = jnp.where(row16 < H, above, b)
    end = jnp.where(row8 < 6, b[:, :8], jnp.where(row8 == 6, 1.0, 0.0))
    window_rows(shift, jnp.concatenate([mid, end], axis=1), ROWS, rolled, hs, band)
    sub8 = lax.broadcasted_iota(jnp.int32, (8, 1), 0)
    for c in range(8):
        cols = slice(256 * c, 256 * c + 256)
        oa = jnp.dot(va[...], hs[0:208, cols].astype(BF16), preferred_element_type=F32)
        ob = jnp.dot(vb[...], hs[200:440, cols].astype(BF16), preferred_element_type=F32)
        pieces = []
        for r in range(ROWS):
            pieces += [
                oa[16 * r : 16 * r + 16],
                ob[16 * r : 16 * r + 8],
                jnp.where(sub8 == TARGET - 24, sci[r : r + 1, cols], ob[16 * r + 8 : 16 * r + 16]),
            ]
        e_out[:, cols] = jnp.concatenate(pieces, axis=0).astype(BF16)
    acc[...] = jnp.zeros_like(acc)

    def row_step(r, carry):
        e = e_out[pl.ds(pl.multiple_of(r * 32, 32), 32), :]
        rows = [e]
        for k in range(4):
            p = powers[16 * k : 16 * k + 16, :]
            rows += [e[0:16] * p, e[16:32] * p]
        g = lax.dot_general(
            e,
            jnp.concatenate(rows, axis=0),
            (((1,), (1,)), ((), ())),
            preferred_element_type=F32,
        )
        v = (first_row + r).astype(F32) * (2.0 / 256.0) + (1.0 / 256.0 - 1.0)
        last[:, 0:32] += g[:, TC : TC + 32]
        g = g[:, 0:TC]
        scale = v
        acc[0] += g
        for m in range(1, 5):
            acc[m] += g * scale
            scale = scale * v
        return carry

    last[...] = jnp.zeros_like(last)
    lax.fori_loop(0, ROWS, row_step, 0, unroll=4)
    units = (
        acc[0],
        acc[1],
        jnp.where(lane < 96, acc[2], pltpu.roll(last[...], 96, 1)),
        jnp.where(lane < 64, acc[3], pltpu.roll(acc[4], 64, 1)),
    )
    for i, unit in enumerate(units):
        for j in range(4):
            mom_out[4 * i + j] = unit[8 * j : 8 * j + 8]


def unit_of(k, m):
    if m < 2 and k < 4:
        return m, k
    if m == 2:
        return 2, k
    return {(4, 0): (2, 3), (0, 3): (3, 0), (1, 3): (3, 1), (0, 4): (3, 2)}[(k, m)]


def inverse2(m):
    (a, b), (c, d) = m
    r = 1.0 / (a * d - b * c)
    return (d * r, -b * r), (-c * r, a * r)


def times2(x, y):
    return tuple(tuple(x[i][0] * y[0][j] + x[i][1] * y[1][j] for j in range(2)) for i in range(2))


def plus2(x, y, sign):
    return tuple(tuple(x[i][j] + sign * y[i][j] for j in range(2)) for i in range(2))


def inverse4(p):
    part = lambda i, j: tuple(tuple(p[2 * i + a][2 * j + b] for b in range(2)) for a in range(2))
    head = inverse2(part(0, 0))
    x = times2(head, part(0, 1))
    y = times2(part(1, 0), head)
    tail = inverse2(plus2(part(1, 1), times2(part(1, 0), x), -1.0))
    xt = times2(x, tail)
    low = times2(tail, y)
    top = plus2(head, times2(xt, y), 1.0)
    return [
        [top[i][j] if i < 2 and j < 2 else tail[i - 2][j - 2] if i > 1 and j > 1
         else -xt[i][j - 2] if i < 2 else -low[i - 2][j] for j in range(4)]
        for i in range(4)
    ]


def sweep_panel(mat, zero, q, lane):
    t = q // 4
    top = 32 * q
    base = 32 * (q % 4)
    sub = lax.broadcasted_iota(jnp.int32, (8, TC), 0)
    tiles = [[mat[top + 8 * i : top + 8 * i + 8, TC * h : TC * h + TC] for h in range(2)] for i in range(4)]
    for k in range(0, 28, 4):
        i0, s0, l0 = k // 8, k % 8, base + k
        cols = [
            [jnp.broadcast_to(tiles[i][t][:, l0 + j : l0 + j + 1], (8, TC)) for j in range(4)]
            for i in range(4)
        ]
        whole_cols = [cols[i0][j] + zero for j in range(4)]
        p = [
            [jnp.broadcast_to(whole_cols[j][s0 + i : s0 + i + 1], (8, TC)) for j in range(4)]
            for i in range(4)
        ]
        w = inverse4(p)
        in_lane = (lane >= l0) & (lane < l0 + 4)
        in_row = (sub >= s0) & (sub < s0 + 4)
        rows = []
        for h in range(2):
            r = [jnp.broadcast_to(tiles[i0][h][s0 + j : s0 + j + 1], (8, TC)) for j in range(4)]
            if h == t:
                r = [jnp.where(in_lane, jnp.where(lane == l0 + j, 1.0, 0.0), r[j]) for j in range(4)]
            rows.append([
                (w[m][0] * r[0] + w[m][1] * r[1]) + (w[m][2] * r[2] + w[m][3] * r[3]) for m in range(4)
            ])
        for i in range(4):
            c = cols[i]
            if i == i0:
                c = [jnp.where(in_row, jnp.where(sub == s0 + j, -1.0, 0.0), c[j]) for j in range(4)]
            for h in range(2):
                old = tiles[i][h]
                if h == t:
                    old = jnp.where(in_lane, 0.0, old)
                if i == i0:
                    old = jnp.where(in_row, 0.0, old)
                u = rows[h]
                tiles[i][h] = old - ((c[0] * u[0] + c[1] * u[1]) + (c[2] * u[2] + c[3] * u[3]))
    inside = (lane >= base) & (lane < base + 28)
    swept = [[], []]
    for i in range(4):
        for h in range(2):
            f = tiles[i][h]
            if h == t:
                f = jnp.where(inside, -f, f)
            if i == 3:
                f = jnp.where(sub < 4, f, 0.0)
            swept[h].append(f)
    f = jnp.concatenate([jnp.concatenate(swept[h], axis=0) for h in range(2)], axis=1)
    f_hi = f.astype(BF16)
    f = f - f_hi.astype(F32)
    f_mid = f.astype(BF16)
    f_lo = (f - f_mid.astype(F32)).astype(BF16)
    right = jnp.concatenate(
        [f_hi, f_mid, f_hi, f_lo, f_hi, f_mid, jnp.zeros((64, 2 * TC), BF16)], axis=0
    )
    z = jnp.where(inside, mat[top + 32 : 200, TC * t : TC * t + TC], 0.0)
    if base:
        z = pltpu.roll(z, 128 - base, 1)
    z = z + pltpu.roll(z, 32, 1)
    z = z + pltpu.roll(z, 64, 1)
    z_hi = z.astype(BF16).astype(F32)
    z = z - z_hi
    z_mid = z.astype(BF16).astype(F32)
    z_lo = z - z_mid
    slot = lax.shift_right_logical(lane, 5)
    left = jnp.concatenate(
        [
            jnp.where(slot == 2, z_mid, z_hi),
            jnp.where(slot == 0, z_lo, jnp.where(slot == 1, z_mid, 0.0)),
        ],
        axis=1,
    ).astype(BF16)
    change = jnp.dot(left, right, preferred_element_type=F32)
    for h in range(2):
        old = mat[top + 32 : 200, TC * h : TC * h + TC]
        if h == t:
            old = jnp.where(inside, 0.0, old)
        mat[top + 32 : 200, TC * h : TC * h + TC] = old - change[:, TC * h : TC * h + TC]


def apply_stage(order, first_row, moms, e_ref, sci, upow, out, mat, fx):
    units = [jnp.concatenate([moms[4 * i + j] for j in range(4)], axis=0) for i in range(4)]
    lane = lax.broadcasted_iota(jnp.int32, (1, TC), 1)
    row = lax.broadcasted_iota(jnp.int32, (32, 1), 0)
    degree = lambda q: 0 if q == 0 else (1 if q < 3 else 2)

    def col_active(t):
        q = lax.shift_right_logical(lane, 5) + 4 * t
        deg = jnp.where(q >= 1, 1, 0) + jnp.where(q >= 3, 1, 0)
        return (deg <= order) | (lax.bitwise_and(lane, 31) == ONES)

    for q in range(6):
        row_on = (degree(q) <= order) | (row == ONES)
        for t in range(2):
            block = jnp.zeros((32, TC), F32)
            for s in range(4 if t == 0 else 2):
                p = 4 * t + s
                i, k = unit_of(mono[q][0] + mono[p][0], mono[q][1] + mono[p][1])
                piece = units[i]
                if s != k:
                    piece = pltpu.roll(piece, (32 * (s - k)) % 128, 1)
                block = jnp.where(lax.shift_right_logical(lane, 5) == s, piece, block)
            both = row_on & col_active(t)
            block = jnp.where(both, block, 0.0)
            if t == q // 4:
                diag = lane == row + 32 * (q % 4)
                block = jnp.where(diag, jnp.where(both, block, 1.0) * (1.0 + ridge), block)
            mat[32 * q : 32 * q + 32, TC * t : TC * t + TC] = block
            if q == 0:
                mat[192:200, TC * t : TC * t + TC] = jnp.where(col_active(t), block[24:32], 0.0)
    fx[...] = jnp.zeros_like(fx)
    zero = fx[...]
    for q in range(6):
        sweep_panel(mat, zero, q, lane)
    coef = []
    for q in range(6):
        z = mat[192:200, TC * (q // 4) : TC * (q // 4) + TC]
        z = jnp.broadcast_to(z[TARGET - 24 : TARGET - 23], (8, TC))
        if q % 4:
            z = pltpu.roll(z, 128 - 32 * (q % 4), 1)
        z = jnp.where(lane < 28, z, 0.0)
        z = z + pltpu.roll(z, 32, 1)
        z = z + pltpu.roll(z, 64, 1)
        coef.append(jnp.concatenate([z, z], axis=0))
    row16 = lax.broadcasted_iota(jnp.int32, (16, 1), 0)
    v = (first_row + row16).astype(F32) * (2.0 / 256.0) + (1.0 / 256.0 - 1.0)
    parts = (coef[0] + v * (coef[2] + v * coef[5]), coef[1] + v * coef[4], coef[3])
    his, los = [], []
    for p in parts:
        wide_p = jnp.concatenate(
            [jnp.where(row16 == 4 * n + lax.shift_right_logical(lane, 5), p, 0.0) for n in range(4)],
            axis=1,
        )
        h = wide_p.astype(BF16)
        his.append(h)
        los.append((wide_p - h.astype(F32)).astype(BF16))
    res = jnp.dot(jnp.concatenate(his + los, axis=0), e_ref[...], preferred_element_type=F32)
    t0, t1, t2 = (res[16 * i : 16 * i + 16] + res[48 + 16 * i : 64 + 16 * i] for i in range(3))
    u = jnp.concatenate([upow[...]] * 2, axis=0)
    out[...] = sci[...] - (t0 + u * (t1 + u * t2))


MESH = pl.DeviceIdType.MESH


def whole_kernel(
    ccds, strips, shift_h, order_h, source_h, slot_h, store_h, sci_h, band_h, va_h, vb_h, upow_h, powers_h, out,
    sent, got, own, edge, sci, band, va, vb, upow, powers, e, rolled, hs, acc, last, mom, parts, part, totals, mat, fx,
    shift, order, source, slot, store, packed, table, index, local, index_sem, send, recv, esend, erecv, s1, r1, s2, r2,
):
    ccd = lax.axis_index("ccd")
    strip = lax.axis_index("strip")
    count = ccds * strips
    me = ccd * strips + strip
    barrier = pltpu.get_barrier_semaphore()
    loads = [
        pltpu.make_async_copy(h, v, local.at[i])
        for i, (h, v) in enumerate(
            ((source_h, source), (slot_h, slot), (store_h, store), (shift_h, shift), (order_h, order),
             (band_h, band), (va_h, va), (vb_h, vb), (upow_h, upow), (powers_h, powers), (sci_h, sci))
        )
    ]

    hops = (0, 1, 2, 1)
    turn = lambda i, k: lax.rem(i + k, 4)
    shifts = [(y, c, z, x) for y in range(4) for c in range(2) for z in range(4) for x in range(4)]
    shifts.sort(key=lambda o: -(hops[o[0]] + hops[o[2]] + hops[o[3]] + 0.5 * o[1]))
    rows = [[turn(ccd // 2, y) * 2 + lax.rem(ccd + c, 2) for c in range(2)] for y in range(4)]
    cells = [[turn(strip // 4, z) * 4 + turn(lax.rem(strip, 4), x) for x in range(4)] for z in range(4)]

    def each_peer(act):
        for y, c, z, x in shifts[:-1]:
            act(rows[y][c], cells[z][x])

    each_peer(
        lambda c, k: pl.semaphore_signal(barrier, inc=1, device_id=(c, k), device_id_type=MESH)
    )
    for load in loads:
        load.start()
    for load in loads[:3]:
        load.wait()

    tiles = source.shape[0]
    pick = jnp.sum(jnp.where(source[...] == me, slot[...], 0), axis=0, keepdims=True)
    table[0:8] = jnp.broadcast_to(pick, (8, count))
    table[24:32] = jnp.zeros((8, count), jnp.int32)
    table[8 : 8 + tiles] = source[...]
    to_index = pltpu.make_async_copy(table, index, index_sem)
    to_index.start()
    to_index.wait()

    def choose(d, carry):
        sent[d] = store[index[0, d]]
        return carry

    lax.fori_loop(0, count, choose, 0, unroll=8)
    got[me] = sent[me]
    pl.semaphore_wait(barrier, count - 1)

    each_peer(
        lambda c, k: pltpu.make_async_remote_copy(
            src_ref=sent.at[c * strips + k],
            dst_ref=got.at[me],
            send_sem=send,
            recv_sem=recv,
            device_id=(c, k),
            device_id_type=MESH,
        ).start()
    )
    rest = got.at[pl.ds(0, count - 1)]
    pltpu.make_async_copy(rest, rest, recv).wait()
    for t in range(own.shape[0]):
        own[t] = got[index[8 + t, me]]
    packed[0] = pack_rows(pltpu.roll(own[...], 16 - 5, 1))
    packed[1] = pack_rows(own[...])
    edges = [
        pltpu.make_async_remote_copy(
            src_ref=packed.at[way],
            dst_ref=edge.at[way],
            send_sem=esend.at[way],
            recv_sem=erecv.at[way],
            device_id=(ccd, lax.rem(strip + (1 if way == 0 else strips - 1), strips)),
            device_id_type=MESH,
        )
        for way in range(2)
    ]
    for copy in edges:
        copy.start()
    for load in loads[3:]:
        load.wait()
    window_rows(shift[0], own[...], 0, rolled, hs, band)
    for copy in edges:
        copy.wait()
    above = jnp.where(strip > 0, unpack_rows(edge[0]), 0.0)
    below = jnp.where(strip < strips - 1, unpack_rows(edge[1]), 0.0)
    first_row = strip * ROWS
    fit_stage(shift[0], first_row, above, below, sci, band, va, vb, powers, e, mom, rolled, hs, acc, last)
    peers = [(ccd, cells[z][x]) for y, c, z, x in shifts[:-1] if y == 0 and c == 0]
    for to in peers:
        pltpu.make_async_remote_copy(
            src_ref=mom.at[to[1]],
            dst_ref=parts.at[strip],
            send_sem=s1,
            recv_sem=r1,
            device_id=to,
            device_id_type=MESH,
        ).start()
    parts[strip] = mom[strip]
    few = parts.at[pl.ds(0, strips - 1)]
    pltpu.make_async_copy(few, few, r1).wait()
    total = parts[0]
    for i in range(1, strips):
        total = total + parts[i]
    part[...] = total
    for to in peers:
        pltpu.make_async_remote_copy(
            src_ref=part,
            dst_ref=totals.at[strip],
            send_sem=s2,
            recv_sem=r2,
            device_id=to,
            device_id_type=MESH,
        ).start()
    totals[strip] = total
    pltpu.make_async_copy(few, few, r2).wait()
    apply_stage(order[0], first_row, totals, e, sci, upow, out, mat, fx)
    pltpu.make_async_copy(rest, rest, send).wait()
    pltpu.make_async_copy(few, few, s1).wait()
    pltpu.make_async_copy(few, few, s2).wait()


VM = pl.BlockSpec(memory_space=pltpu.VMEM)
SM = pl.BlockSpec(memory_space=pltpu.SMEM)
ANY = pl.BlockSpec(memory_space=pl.ANY)
LIMIT = 60 * 1024 * 1024


def whole(shift, order, source, slot, store, sci, ccds, strips):
    count = ccds * strips
    tiles = (source.shape[0], *store.shape[1:])
    tables = [band_matrix(), *vertical_matrices(), column_rows(), column_factors()]
    blocks = pltpu.VMEM((strips, 128 // strips, TC), F32)
    dma = pltpu.SemaphoreType.DMA
    return pl.pallas_call(
        lambda *refs: whole_kernel(ccds, strips, *refs),
        out_shape=pltpu.VMEM((ROWS, COLS), F32),
        in_specs=[ANY] * 11,
        out_specs=VM,
        scratch_shapes=[
            pltpu.VMEM((count, *store.shape[1:]), F32),
            pltpu.VMEM((count, *store.shape[1:]), F32),
            pltpu.VMEM(tiles, F32),
            pltpu.VMEM((2, tiles[0] // 2, 24, TC), F32),
            pltpu.VMEM((ROWS, COLS), F32),
            *[pltpu.VMEM(x.shape, x.dtype) for x in tables],
            pltpu.VMEM((ROWS * 32, COLS), BF16),
            pltpu.VMEM((tiles[0] + 1, SLOTS - ROWS, TC), F32),
            pltpu.VMEM((440, COLS), F32),
            pltpu.VMEM((5, 32, TC), F32),
            pltpu.VMEM((32, TC), F32),
            blocks,
            blocks,
            pltpu.VMEM((128 // strips, TC), F32),
            blocks,
            pltpu.VMEM((200, 2 * TC), F32),
            pltpu.VMEM((8, TC), F32),
            pltpu.SMEM((1,), jnp.int32),
            pltpu.SMEM((1,), jnp.int32),
            pltpu.VMEM(source.shape, jnp.int32),
            pltpu.VMEM(source.shape, jnp.int32),
            pltpu.VMEM(store.shape, F32),
            pltpu.VMEM((2, tiles[0] // 2, 24, TC), F32),
            pltpu.VMEM((32, count), jnp.int32),
            pltpu.SMEM((32, count), jnp.int32),
            dma((11,)),
            dma,
            dma,
            dma,
            dma((2,)),
            dma((2,)),
            dma,
            dma,
            dma,
            dma,
        ],
        compiler_params=pltpu.CompilerParams(
            collective_id=0, has_side_effects=True, vmem_limit_bytes=LIMIT
        ),
        name="whole",
    )(shift, order, source, slot, store, sci, *[jnp.asarray(x) for x in tables])


def body(tile_store, tile_source, tile_slot, shift_cols, spatial_order, science):
    strips = lax.axis_size("strip")
    return whole(
        shift_cols, spatial_order, tile_source.T, tile_slot.T, tile_store, science,
        lax.axis_size("ccd"), strips,
    )


def solution(mesh):
    placed = (
        P(("ccd", "strip"), None, None),
        P(),
        P(),
        P("ccd"),
        P("ccd"),
        P(("ccd", "strip"), None),
    )
    return jax.shard_map(
        body, mesh=mesh, in_specs=placed, out_specs=P(("ccd", "strip"), None), check_vma=False
    )
```

```python
import jax
import jax.numpy as jnp
import numpy as np
from jax import lax
from jax.experimental import pallas as pl
from jax.experimental.pallas import tpu as pltpu
from jax.sharding import PartitionSpec as P

H = 11
CM = 128
ROWS = 16
COLS = 2048
TC = 128
SLOTS = 40
TARGET = 28
ONES = 15

sigmas = (0.7, 1.5, 3.0)
tops = (4, 2, 2)
mono = ((0, 0), (1, 0), (0, 1), (2, 0), (1, 1), (0, 2))
ridge = 0.05
F32 = jnp.float32
BF16 = jnp.bfloat16


def tap_table():
    a = np.arange(-H, H + 1).astype(np.float64)
    rows = []
    for s, top in zip(sigmas, tops):
        e = np.exp(-a * a / (2.0 * s * s))
        for n in range(top + 1):
            rows.append(e * (a / s) ** n / e.sum())
    return np.stack(rows).astype(np.float32)


def to_bf16(x):
    return x.astype(jnp.bfloat16.dtype)


def band_matrix():
    taps = tap_table()
    hi = to_bf16(taps).astype(np.float32)
    lo = to_bf16(taps - hi).astype(np.float32)
    full = []
    for part in (hi, lo):
        m = np.zeros((160, 11, TC), np.float32)
        for f in range(11):
            for x in range(TC):
                m[x : x + 23, f, x] = part[f]
        full.append(m.reshape(160, 11 * TC))
    h, l = full
    tail = np.zeros((TC, 11 * TC), np.float32)
    tail[0:32], tail[32:64], tail[64:96] = h[128:], h[128:], l[128:]
    return to_bf16(np.concatenate([h[:128], h[:128], l[:128], tail]))


def slot_of(row):
    return 16 + row if row < H else (row - H if row < H + ROWS else row)


def vertical_matrices():
    taps = to_bf16(tap_table()).astype(np.float32)
    first = np.zeros((ROWS, 16, 208), np.float32)
    second = np.zeros((ROWS, 16, 240), np.float32)
    slot = 0
    for i in range(5):
        for j in range(5 - i):
            for r in range(ROWS):
                for a in range(23):
                    first[r, slot, i * SLOTS + slot_of(r + a)] = taps[j, a]
            slot += 1
    first[:, ONES, 38] = 1.0
    slot = 0
    for g in range(2):
        for i in range(3):
            for j in range(3 - i):
                for r in range(ROWS):
                    for a in range(23):
                        second[r, slot, (3 * g + i) * SLOTS + slot_of(r + a)] = taps[5 + 3 * g + j, a]
                slot += 1
    return to_bf16(first.reshape(256, 208)), to_bf16(second.reshape(256, 240))


def column_powers():
    u = 2.0 * (np.arange(COLS).astype(np.float32) + np.float32(0.5)) / np.float32(COLS) - np.float32(1.0)
    u = u.astype(np.float32)
    return u


def column_rows():
    return np.stack([column_powers()] * 8)


def column_factors():
    u = column_powers()
    return to_bf16(np.concatenate([np.stack([u ** (k + 1)] * 16) for k in range(4)]))


def pack_rows(x):
    pairs = x.reshape(x.shape[0] // 2, 2, 16, TC)
    a, b = pairs[:, 0], pairs[:, 1]
    row = lax.broadcasted_iota(jnp.int32, (1, 8, TC), 1)
    mid = jnp.where(row < 3, a[:, 8:], pltpu.roll(b[:, :8], 3, 1))
    return jnp.concatenate([a[:, :8], mid, pltpu.roll(b, H, 1)[:, :8]], axis=1)


def unpack_rows(x):
    row = lax.broadcasted_iota(jnp.int32, (1, 8, TC), 1)
    end = pltpu.roll(x[:, 16:], 5, 1)
    b = jnp.concatenate([jnp.where(row < 5, pltpu.roll(x[:, 8:16], 5, 1), end), end], axis=1)
    pairs = jnp.concatenate([x[:, None, :16], b[:, None]], axis=1)
    return pairs.reshape(2 * x.shape[0], 16, TC)


def window_rows(shift, x, rolled, hs, band):
    count, rows, _ = x.shape
    start = CM + shift - H
    tile = lax.shift_right_logical(start, 7)
    rem = lax.bitwise_and(start, 127)
    rolled[0:count, 0:rows] = pltpu.roll(x, lax.bitwise_and(128 - rem, 127), 2)
    rolled[count : count + 1, 0:rows] = jnp.zeros((1, rows, TC), F32)
    lane3 = lax.broadcasted_iota(jnp.int32, (1, rows, TC), 2)
    w = jnp.where(
        lane3 < 128 - rem, rolled[pl.ds(tile, 17), 0:rows], rolled[pl.ds(tile + 1, 17), 0:rows]
    ).reshape(17 * rows, TC)
    main = w[: 16 * rows]
    nxt = w[rows:]
    hi = main.astype(BF16)
    lo = (main - hi.astype(F32)).astype(BF16)
    nhi = nxt.astype(BF16).astype(F32)
    nlo = nxt - nhi
    lane = lax.broadcasted_iota(jnp.int32, (1, TC), 1)
    tail = jnp.where(
        lane < 32,
        nhi,
        jnp.where(lane < 64, pltpu.roll(nlo, 32, 1), jnp.where(lane < 96, pltpu.roll(nhi, 64, 1), 0.0)),
    ).astype(BF16)
    lhs = jnp.concatenate([hi, lo, hi, tail], axis=1)
    for c in range(6):
        n = 256 if c < 5 else 128
        res = jnp.dot(lhs, band[:, 256 * c : 256 * c + n], preferred_element_type=F32)
        for f in range(2 * c, 2 * c + n // TC):
            o = (f - 2 * c) * TC
            for j in range(16):
                hs[f * SLOTS : f * SLOTS + rows, j * TC : (j + 1) * TC] = res[
                    j * rows : (j + 1) * rows, o : o + TC
                ]


def fit_stage(shift, first_row, own, above, below, sci, band, va, vb, powers, e_out, mom_out, rolled, hs, acc, last):
    row16 = lax.broadcasted_iota(jnp.int32, (1, 16, TC), 1)
    row8 = lax.broadcasted_iota(jnp.int32, (1, 8, TC), 1)
    lane = lax.broadcasted_iota(jnp.int32, (1, TC), 1)
    b = pltpu.roll(below, H, 1)
    mid = jnp.where(row16 < H, above, b)
    end = jnp.where(row8 < 6, b[:, :8], jnp.where(row8 == 6, 1.0, 0.0))
    window_rows(shift, jnp.concatenate([own, mid, end], axis=1), rolled, hs, band)
    sub8 = lax.broadcasted_iota(jnp.int32, (8, 1), 0)
    for c in range(8):
        cols = slice(256 * c, 256 * c + 256)
        oa = jnp.dot(va[...], hs[0:208, cols].astype(BF16), preferred_element_type=F32)
        ob = jnp.dot(vb[...], hs[200:440, cols].astype(BF16), preferred_element_type=F32)
        pieces = []
        for r in range(ROWS):
            pieces += [
                oa[16 * r : 16 * r + 16],
                ob[16 * r : 16 * r + 8],
                jnp.where(sub8 == TARGET - 24, sci[r : r + 1, cols], ob[16 * r + 8 : 16 * r + 16]),
            ]
        e_out[:, cols] = jnp.concatenate(pieces, axis=0).astype(BF16)
    acc[...] = jnp.zeros_like(acc)

    def row_step(r, carry):
        e = e_out[pl.ds(pl.multiple_of(r * 32, 32), 32), :]
        rows = [e]
        for k in range(4):
            p = powers[16 * k : 16 * k + 16, :]
            rows += [e[0:16] * p, e[16:32] * p]
        g = lax.dot_general(
            e,
            jnp.concatenate(rows, axis=0),
            (((1,), (1,)), ((), ())),
            preferred_element_type=F32,
        )
        v = (first_row + r).astype(F32) * (2.0 / 256.0) + (1.0 / 256.0 - 1.0)
        last[:, 0:32] += g[:, TC : TC + 32]
        g = g[:, 0:TC]
        scale = v
        acc[0] += g
        for m in range(1, 5):
            acc[m] += g * scale
            scale = scale * v
        return carry

    last[...] = jnp.zeros_like(last)
    lax.fori_loop(0, ROWS, row_step, 0, unroll=4)
    units = (
        acc[0],
        acc[1],
        jnp.where(lane < 96, acc[2], pltpu.roll(last[...], 96, 1)),
        jnp.where(lane < 64, acc[3], pltpu.roll(acc[4], 64, 1)),
    )
    for i, unit in enumerate(units):
        for j in range(4):
            mom_out[4 * i + j] = unit[8 * j : 8 * j + 8]


def unit_of(k, m):
    if m < 2 and k < 4:
        return m, k
    if m == 2:
        return 2, k
    return {(4, 0): (2, 3), (0, 3): (3, 0), (1, 3): (3, 1), (0, 4): (3, 2)}[(k, m)]


def inverse2(m):
    (a, b), (c, d) = m
    r = 1.0 / (a * d - b * c)
    return (d * r, -b * r), (-c * r, a * r)


def times2(x, y):
    return tuple(tuple(x[i][0] * y[0][j] + x[i][1] * y[1][j] for j in range(2)) for i in range(2))


def plus2(x, y, sign):
    return tuple(tuple(x[i][j] + sign * y[i][j] for j in range(2)) for i in range(2))


def inverse4(p):
    part = lambda i, j: tuple(tuple(p[2 * i + a][2 * j + b] for b in range(2)) for a in range(2))
    head = inverse2(part(0, 0))
    x = times2(head, part(0, 1))
    y = times2(part(1, 0), head)
    tail = inverse2(plus2(part(1, 1), times2(part(1, 0), x), -1.0))
    xt = times2(x, tail)
    low = times2(tail, y)
    top = plus2(head, times2(xt, y), 1.0)
    return [
        [top[i][j] if i < 2 and j < 2 else tail[i - 2][j - 2] if i > 1 and j > 1
         else -xt[i][j - 2] if i < 2 else -low[i - 2][j] for j in range(4)]
        for i in range(4)
    ]


def sweep_panel(mat, zero, q, lane):
    t = q // 4
    top = 32 * q
    base = 32 * (q % 4)
    sub = lax.broadcasted_iota(jnp.int32, (8, TC), 0)
    tiles = [[mat[top + 8 * i : top + 8 * i + 8, TC * h : TC * h + TC] for h in range(2)] for i in range(4)]
    for k in range(0, 28, 4):
        i0, s0, l0 = k // 8, k % 8, base + k
        cols = [
            [jnp.broadcast_to(tiles[i][t][:, l0 + j : l0 + j + 1], (8, TC)) for j in range(4)]
            for i in range(4)
        ]
        whole_cols = [cols[i0][j] + zero for j in range(4)]
        p = [
            [jnp.broadcast_to(whole_cols[j][s0 + i : s0 + i + 1], (8, TC)) for j in range(4)]
            for i in range(4)
        ]
        w = inverse4(p)
        in_lane = (lane >= l0) & (lane < l0 + 4)
        in_row = (sub >= s0) & (sub < s0 + 4)
        rows = []
        for h in range(2):
            r = [jnp.broadcast_to(tiles[i0][h][s0 + j : s0 + j + 1], (8, TC)) for j in range(4)]
            if h == t:
                r = [jnp.where(in_lane, jnp.where(lane == l0 + j, 1.0, 0.0), r[j]) for j in range(4)]
            rows.append([
                (w[m][0] * r[0] + w[m][1] * r[1]) + (w[m][2] * r[2] + w[m][3] * r[3]) for m in range(4)
            ])
        for i in range(4):
            c = cols[i]
            if i == i0:
                c = [jnp.where(in_row, jnp.where(sub == s0 + j, -1.0, 0.0), c[j]) for j in range(4)]
            for h in range(2):
                old = tiles[i][h]
                if h == t:
                    old = jnp.where(in_lane, 0.0, old)
                if i == i0:
                    old = jnp.where(in_row, 0.0, old)
                u = rows[h]
                tiles[i][h] = old - ((c[0] * u[0] + c[1] * u[1]) + (c[2] * u[2] + c[3] * u[3]))
    inside = (lane >= base) & (lane < base + 28)
    swept = [[], []]
    for i in range(4):
        for h in range(2):
            f = tiles[i][h]
            if h == t:
                f = jnp.where(inside, -f, f)
            if i == 3:
                f = jnp.where(sub < 4, f, 0.0)
            swept[h].append(f)
    f = jnp.concatenate([jnp.concatenate(swept[h], axis=0) for h in range(2)], axis=1)
    f_hi = f.astype(BF16)
    f = f - f_hi.astype(F32)
    f_mid = f.astype(BF16)
    f_lo = (f - f_mid.astype(F32)).astype(BF16)
    right = jnp.concatenate(
        [f_hi, f_mid, f_hi, f_lo, f_hi, f_mid, jnp.zeros((64, 2 * TC), BF16)], axis=0
    )
    z = jnp.where(inside, mat[top + 32 : 200, TC * t : TC * t + TC], 0.0)
    if base:
        z = pltpu.roll(z, 128 - base, 1)
    z = z + pltpu.roll(z, 32, 1)
    z = z + pltpu.roll(z, 64, 1)
    z_hi = z.astype(BF16).astype(F32)
    z = z - z_hi
    z_mid = z.astype(BF16).astype(F32)
    z_lo = z - z_mid
    slot = lax.shift_right_logical(lane, 5)
    left = jnp.concatenate(
        [
            jnp.where(slot == 2, z_mid, z_hi),
            jnp.where(slot == 0, z_lo, jnp.where(slot == 1, z_mid, 0.0)),
        ],
        axis=1,
    ).astype(BF16)
    change = jnp.dot(left, right, preferred_element_type=F32)
    for h in range(2):
        old = mat[top + 32 : 200, TC * h : TC * h + TC]
        if h == t:
            old = jnp.where(inside, 0.0, old)
        mat[top + 32 : 200, TC * h : TC * h + TC] = old - change[:, TC * h : TC * h + TC]


def apply_stage(order, first_row, moms, e_ref, sci, upow, out, mat, fx):
    units = [jnp.concatenate([moms[4 * i + j] for j in range(4)], axis=0) for i in range(4)]
    lane = lax.broadcasted_iota(jnp.int32, (1, TC), 1)
    row = lax.broadcasted_iota(jnp.int32, (32, 1), 0)
    degree = lambda q: 0 if q == 0 else (1 if q < 3 else 2)

    def col_active(t):
        q = lax.shift_right_logical(lane, 5) + 4 * t
        deg = jnp.where(q >= 1, 1, 0) + jnp.where(q >= 3, 1, 0)
        return (deg <= order) | (lax.bitwise_and(lane, 31) == ONES)

    for q in range(6):
        row_on = (degree(q) <= order) | (row == ONES)
        for t in range(2):
            block = jnp.zeros((32, TC), F32)
            for s in range(4 if t == 0 else 2):
                p = 4 * t + s
                i, k = unit_of(mono[q][0] + mono[p][0], mono[q][1] + mono[p][1])
                piece = units[i]
                if s != k:
                    piece = pltpu.roll(piece, (32 * (s - k)) % 128, 1)
                block = jnp.where(lax.shift_right_logical(lane, 5) == s, piece, block)
            both = row_on & col_active(t)
            block = jnp.where(both, block, 0.0)
            if t == q // 4:
                diag = lane == row + 32 * (q % 4)
                block = jnp.where(diag, jnp.where(both, block, 1.0) * (1.0 + ridge), block)
            mat[32 * q : 32 * q + 32, TC * t : TC * t + TC] = block
            if q == 0:
                mat[192:200, TC * t : TC * t + TC] = jnp.where(col_active(t), block[24:32], 0.0)
    fx[...] = jnp.zeros_like(fx)
    zero = fx[...]
    for q in range(6):
        sweep_panel(mat, zero, q, lane)
    coef = []
    for q in range(6):
        z = mat[192:200, TC * (q // 4) : TC * (q // 4) + TC]
        z = jnp.broadcast_to(z[TARGET - 24 : TARGET - 23], (8, TC))
        if q % 4:
            z = pltpu.roll(z, 128 - 32 * (q % 4), 1)
        z = jnp.where(lane < 28, z, 0.0)
        z = z + pltpu.roll(z, 32, 1)
        z = z + pltpu.roll(z, 64, 1)
        coef.append(jnp.concatenate([z, z], axis=0))
    row16 = lax.broadcasted_iota(jnp.int32, (16, 1), 0)
    v = (first_row + row16).astype(F32) * (2.0 / 256.0) + (1.0 / 256.0 - 1.0)
    parts = (coef[0] + v * (coef[2] + v * coef[5]), coef[1] + v * coef[4], coef[3])
    his, los = [], []
    for p in parts:
        wide_p = jnp.concatenate(
            [jnp.where(row16 == 4 * n + lax.shift_right_logical(lane, 5), p, 0.0) for n in range(4)],
            axis=1,
        )
        h = wide_p.astype(BF16)
        his.append(h)
        los.append((wide_p - h.astype(F32)).astype(BF16))
    res = jnp.dot(jnp.concatenate(his + los, axis=0), e_ref[...], preferred_element_type=F32)
    t0, t1, t2 = (res[16 * i : 16 * i + 16] + res[48 + 16 * i : 64 + 16 * i] for i in range(3))
    u = jnp.concatenate([upow[...]] * 2, axis=0)
    out[...] = sci[...] - (t0 + u * (t1 + u * t2))


MESH = pl.DeviceIdType.MESH


def whole_kernel(
    ccds, strips, shift_h, order_h, source_h, slot_h, store_h, sci_h, band_h, va_h, vb_h, upow_h, powers_h, out,
    sent, got, sent2, got2, sci, band, va, vb, upow, powers, e, rolled, hs, acc, last, mom, parts, part, totals, mat, fx,
    shift, order, source, slot, store, local, send, recv, send2, recv2, s1, r1, s2, r2,
):
    ccd = lax.axis_index("ccd")
    strip = lax.axis_index("strip")
    count = ccds * strips
    me = ccd * strips + strip
    barrier = pltpu.get_barrier_semaphore()
    loads = [
        pltpu.make_async_copy(h, v, local.at[i])
        for i, (h, v) in enumerate(
            ((source_h, source), (slot_h, slot), (store_h, store), (shift_h, shift), (order_h, order),
             (band_h, band), (va_h, va), (vb_h, vb), (upow_h, upow), (powers_h, powers), (sci_h, sci))
        )
    ]

    hops = (0, 1, 2, 1)
    turn = lambda i, k: lax.rem(i + k, 4)
    shifts = [(y, c, z, x) for y in range(4) for c in range(2) for z in range(4) for x in range(4)]
    shifts.sort(key=lambda o: -(hops[o[0]] + hops[o[2]] + hops[o[3]] + 0.5 * o[1]))
    rows = [[turn(ccd // 2, y) * 2 + lax.rem(ccd + c, 2) for c in range(2)] for y in range(4)]
    cells = [[turn(strip // 4, z) * 4 + turn(lax.rem(strip, 4), x) for x in range(4)] for z in range(4)]

    def each_peer(act):
        for y, c, z, x in shifts[:-1]:
            act(rows[y][c], cells[z][x])

    each_peer(
        lambda c, k: pl.semaphore_signal(barrier, inc=1, device_id=(c, k), device_id_type=MESH)
    )
    for load in loads:
        load.start()
    for load in loads[:3]:
        load.wait()

    tiles = source.shape[0]
    flat = tiles * ROWS
    sheet = jnp.concatenate([store[...].reshape(flat, TC), jnp.zeros((-flat % TC, TC), F32)], axis=0)
    near = sheet.shape[0] // TC
    for i in range(near):
        sent[pl.ds(i, count, stride=near), :] = jnp.transpose(sheet[TC * i : TC * i + TC])
    for i in range(near):
        got[pl.ds(near * me + i, 1), :] = sent[pl.ds(near * me + i, 1), :]
    pl.semaphore_wait(barrier, count - 1)

    def send_all(src, dst, size, done, arrived):
        each_peer(
            lambda c, k: pltpu.make_async_remote_copy(
                src_ref=src.at[pl.ds(size * (c * strips + k), size)],
                dst_ref=dst.at[pl.ds(size * me, size)],
                send_sem=done,
                recv_sem=arrived,
                device_id=(c, k),
                device_id_type=MESH,
            ).start()
        )

    send_all(sent, got, near, send, recv)
    rest = got.at[pl.ds(0, near * (count - 1))]
    pltpu.make_async_copy(rest, rest, recv).wait()
    sheet = jnp.concatenate(
        [jnp.transpose(got[pl.ds(i, count, stride=near), :]) for i in range(near)], axis=0
    )
    found = []
    for t in range(tiles):
        owner = jnp.broadcast_to(source[t : t + 1, :], (8, count))
        place = jnp.broadcast_to(slot[t : t + 1, :], (8, count))
        for h in range(0, ROWS, 8):
            tile = jnp.zeros((8, count), F32)
            for p in range(tiles):
                tile = jnp.where(
                    place == p,
                    jnp.take_along_axis(
                        sheet[ROWS * p + h : ROWS * p + h + 8], owner, axis=1, mode="promise_in_bounds"
                    ),
                    tile,
                )
            found.append(tile)
    mine = jnp.concatenate(found, axis=0)
    up = pack_rows(pltpu.roll(pltpu.roll(mine, 1, 1).reshape(tiles, ROWS, count), 16 - 5, 1))
    down = pack_rows(pltpu.roll(mine, count - 1, 1).reshape(tiles, ROWS, count))
    half = tiles // 2 * 24
    sheet = jnp.concatenate(
        [
            mine,
            up.reshape(half, count),
            down.reshape(half, count),
            jnp.zeros((-(flat + 2 * half) % TC, count), F32),
        ],
        axis=0,
    )
    far = sheet.shape[0] // TC
    for i in range(far):
        sent2[pl.ds(i, count, stride=far), :] = jnp.transpose(sheet[TC * i : TC * i + TC])
    send_all(sent2, got2, far, send2, recv2)
    for i in range(far):
        got2[pl.ds(far * me + i, 1), :] = sent2[pl.ds(far * me + i, 1), :]
    for load in loads[3:]:
        load.wait()
    rest2 = got2.at[pl.ds(0, far * (count - 1))]
    pltpu.make_async_copy(rest2, rest2, recv2).wait()
    sheet = jnp.concatenate(
        [jnp.transpose(got2[pl.ds(i, count, stride=far), :]) for i in range(far)], axis=0
    )
    own = sheet[:flat].reshape(tiles, ROWS, TC)
    above = unpack_rows(sheet[flat : flat + half].reshape(tiles // 2, 24, TC))
    below = unpack_rows(sheet[flat + half : flat + 2 * half].reshape(tiles // 2, 24, TC))
    above = jnp.where(strip > 0, above, 0.0)
    below = jnp.where(strip < strips - 1, below, 0.0)
    first_row = strip * ROWS
    fit_stage(shift[0], first_row, own, above, below, sci, band, va, vb, powers, e, mom, rolled, hs, acc, last)
    peers = [(ccd, cells[z][x]) for y, c, z, x in shifts[:-1] if y == 0 and c == 0]
    for to in peers:
        pltpu.make_async_remote_copy(
            src_ref=mom.at[to[1]],
            dst_ref=parts.at[strip],
            send_sem=s1,
            recv_sem=r1,
            device_id=to,
            device_id_type=MESH,
        ).start()
    parts[strip] = mom[strip]
    few = parts.at[pl.ds(0, strips - 1)]
    pltpu.make_async_copy(few, few, r1).wait()
    total = parts[0]
    for i in range(1, strips):
        total = total + parts[i]
    part[...] = total
    for to in peers:
        pltpu.make_async_remote_copy(
            src_ref=part,
            dst_ref=totals.at[strip],
            send_sem=s2,
            recv_sem=r2,
            device_id=to,
            device_id_type=MESH,
        ).start()
    totals[strip] = total
    pltpu.make_async_copy(few, few, r2).wait()
    apply_stage(order[0], first_row, totals, e, sci, upow, out, mat, fx)
    pltpu.make_async_copy(rest, rest, send).wait()
    pltpu.make_async_copy(rest2, rest2, send2).wait()
    pltpu.make_async_copy(few, few, s1).wait()
    pltpu.make_async_copy(few, few, s2).wait()


VM = pl.BlockSpec(memory_space=pltpu.VMEM)
SM = pl.BlockSpec(memory_space=pltpu.SMEM)
ANY = pl.BlockSpec(memory_space=pl.ANY)
LIMIT = 60 * 1024 * 1024


def whole(shift, order, source, slot, store, sci, ccds, strips):
    count = ccds * strips
    tiles = source.shape[0]
    near = -(-tiles * ROWS // TC)
    far = -(-(tiles * ROWS + tiles * 24) // TC)
    tables = [band_matrix(), *vertical_matrices(), column_rows(), column_factors()]
    blocks = pltpu.VMEM((strips, 128 // strips, TC), F32)
    dma = pltpu.SemaphoreType.DMA
    return pl.pallas_call(
        lambda *refs: whole_kernel(ccds, strips, *refs),
        out_shape=pltpu.VMEM((ROWS, COLS), F32),
        in_specs=[ANY] * 11,
        out_specs=VM,
        scratch_shapes=[
            pltpu.VMEM((near * count, TC), F32),
            pltpu.VMEM((near * count, TC), F32),
            pltpu.VMEM((far * count, TC), F32),
            pltpu.VMEM((far * count, TC), F32),
            pltpu.VMEM((ROWS, COLS), F32),
            *[pltpu.VMEM(x.shape, x.dtype) for x in tables],
            pltpu.VMEM((ROWS * 32, COLS), BF16),
            pltpu.VMEM((tiles + 1, SLOTS, TC), F32),
            pltpu.VMEM((440, COLS), F32),
            pltpu.VMEM((5, 32, TC), F32),
            pltpu.VMEM((32, TC), F32),
            blocks,
            blocks,
            pltpu.VMEM((128 // strips, TC), F32),
            blocks,
            pltpu.VMEM((200, 2 * TC), F32),
            pltpu.VMEM((8, TC), F32),
            pltpu.SMEM((1,), jnp.int32),
            pltpu.SMEM((1,), jnp.int32),
            pltpu.VMEM(source.shape, jnp.int32),
            pltpu.VMEM(source.shape, jnp.int32),
            pltpu.VMEM(store.shape, F32),
            dma((11,)),
            dma,
            dma,
            dma,
            dma,
            dma,
            dma,
            dma,
            dma,
        ],
        compiler_params=pltpu.CompilerParams(
            collective_id=0, has_side_effects=True, vmem_limit_bytes=LIMIT
        ),
        name="whole",
    )(shift, order, source, slot, store, sci, *[jnp.asarray(x) for x in tables])


def body(tile_store, tile_source, tile_slot, shift_cols, spatial_order, science):
    strips = lax.axis_size("strip")
    return whole(
        shift_cols, spatial_order, tile_source.T, tile_slot.T, tile_store, science,
        lax.axis_size("ccd"), strips,
    )


def solution(mesh):
    placed = (
        P(("ccd", "strip"), None, None),
        P(),
        P(),
        P("ccd"),
        P("ccd"),
        P(("ccd", "strip"), None),
    )
    return jax.shard_map(
        body, mesh=mesh, in_specs=placed, out_specs=P(("ccd", "strip"), None), check_vma=False
    )
```

```python
import jax
import jax.numpy as jnp
import numpy as np
from jax import lax
from jax.experimental import pallas as pl
from jax.experimental.pallas import tpu as pltpu
from jax.sharding import PartitionSpec as P

H = 11
CM = 128
ROWS = 16
COLS = 2048
TC = 128
SLOTS = 40
TARGET = 28
ONES = 15

sigmas = (0.7, 1.5, 3.0)
tops = (4, 2, 2)
mono = ((0, 0), (1, 0), (0, 1), (2, 0), (1, 1), (0, 2))
ridge = 0.05
F32 = jnp.float32
BF16 = jnp.bfloat16


def tap_table():
    a = np.arange(-H, H + 1).astype(np.float64)
    rows = []
    for s, top in zip(sigmas, tops):
        e = np.exp(-a * a / (2.0 * s * s))
        for n in range(top + 1):
            rows.append(e * (a / s) ** n / e.sum())
    return np.stack(rows).astype(np.float32)


def to_bf16(x):
    return x.astype(jnp.bfloat16.dtype)


def band_matrix():
    taps = tap_table()
    hi = to_bf16(taps).astype(np.float32)
    lo = to_bf16(taps - hi).astype(np.float32)
    full = []
    for part in (hi, lo):
        m = np.zeros((160, 11, TC), np.float32)
        for f in range(11):
            for x in range(TC):
                m[x : x + 23, f, x] = part[f]
        full.append(m.reshape(160, 11 * TC))
    h, l = full
    tail = np.zeros((TC, 11 * TC), np.float32)
    tail[0:32], tail[32:64], tail[64:96] = h[128:], h[128:], l[128:]
    return to_bf16(np.concatenate([h[:128], h[:128], l[:128], tail]))


def slot_of(row):
    return 16 + row if row < H else (row - H if row < H + ROWS else row)


def vertical_matrices():
    taps = to_bf16(tap_table()).astype(np.float32)
    first = np.zeros((ROWS, 16, 208), np.float32)
    second = np.zeros((ROWS, 16, 240), np.float32)
    slot = 0
    for i in range(5):
        for j in range(5 - i):
            for r in range(ROWS):
                for a in range(23):
                    first[r, slot, i * SLOTS + slot_of(r + a)] = taps[j, a]
            slot += 1
    first[:, ONES, 38] = 1.0
    slot = 0
    for g in range(2):
        for i in range(3):
            for j in range(3 - i):
                for r in range(ROWS):
                    for a in range(23):
                        second[r, slot, (3 * g + i) * SLOTS + slot_of(r + a)] = taps[5 + 3 * g + j, a]
                slot += 1
    return to_bf16(first.reshape(256, 208)), to_bf16(second.reshape(256, 240))


def column_powers():
    u = 2.0 * (np.arange(COLS).astype(np.float32) + np.float32(0.5)) / np.float32(COLS) - np.float32(1.0)
    u = u.astype(np.float32)
    return u


def column_rows():
    return np.stack([column_powers()] * 8)


def column_factors():
    u = column_powers()
    return to_bf16(np.concatenate([np.stack([u ** (k + 1)] * 16) for k in range(4)]))


def pack_rows(x):
    pairs = x.reshape(x.shape[0] // 2, 2, 16, TC)
    a, b = pairs[:, 0], pairs[:, 1]
    row = lax.broadcasted_iota(jnp.int32, (1, 8, TC), 1)
    mid = jnp.where(row < 3, a[:, 8:], pltpu.roll(b[:, :8], 3, 1))
    return jnp.concatenate([a[:, :8], mid, pltpu.roll(b, H, 1)[:, :8]], axis=1)


def unpack_rows(x):
    row = lax.broadcasted_iota(jnp.int32, (1, 8, TC), 1)
    end = pltpu.roll(x[:, 16:], 5, 1)
    b = jnp.concatenate([jnp.where(row < 5, pltpu.roll(x[:, 8:16], 5, 1), end), end], axis=1)
    pairs = jnp.concatenate([x[:, None, :16], b[:, None]], axis=1)
    return pairs.reshape(2 * x.shape[0], 16, TC)


def window_rows(shift, x, rolled, hs, band):
    count, rows, _ = x.shape
    start = CM + shift - H
    tile = lax.shift_right_logical(start, 7)
    rem = lax.bitwise_and(start, 127)
    rolled[0:count, 0:rows] = pltpu.roll(x, lax.bitwise_and(128 - rem, 127), 2)
    rolled[count : count + 1, 0:rows] = jnp.zeros((1, rows, TC), F32)
    lane3 = lax.broadcasted_iota(jnp.int32, (1, rows, TC), 2)
    w = jnp.where(
        lane3 < 128 - rem, rolled[pl.ds(tile, 17), 0:rows], rolled[pl.ds(tile + 1, 17), 0:rows]
    ).reshape(17 * rows, TC)
    main = w[: 16 * rows]
    nxt = w[rows:]
    hi = main.astype(BF16)
    lo = (main - hi.astype(F32)).astype(BF16)
    nhi = nxt.astype(BF16).astype(F32)
    nlo = nxt - nhi
    lane = lax.broadcasted_iota(jnp.int32, (1, TC), 1)
    tail = jnp.where(
        lane < 32,
        nhi,
        jnp.where(lane < 64, pltpu.roll(nlo, 32, 1), jnp.where(lane < 96, pltpu.roll(nhi, 64, 1), 0.0)),
    ).astype(BF16)
    lhs = jnp.concatenate([hi, lo, hi, tail], axis=1)
    for c in range(6):
        n = 256 if c < 5 else 128
        res = jnp.dot(lhs, band[:, 256 * c : 256 * c + n], preferred_element_type=F32)
        for f in range(2 * c, 2 * c + n // TC):
            o = (f - 2 * c) * TC
            for j in range(16):
                hs[f * SLOTS : f * SLOTS + rows, j * TC : (j + 1) * TC] = res[
                    j * rows : (j + 1) * rows, o : o + TC
                ]


def fit_stage(shift, first_row, own, above, below, sci, band, va, vb, powers, e_out, mom_out, rolled, hs, acc, last):
    row16 = lax.broadcasted_iota(jnp.int32, (1, 16, TC), 1)
    row8 = lax.broadcasted_iota(jnp.int32, (1, 8, TC), 1)
    lane = lax.broadcasted_iota(jnp.int32, (1, TC), 1)
    b = pltpu.roll(below, H, 1)
    mid = jnp.where(row16 < H, above, b)
    end = jnp.where(row8 < 6, b[:, :8], jnp.where(row8 == 6, 1.0, 0.0))
    window_rows(shift, jnp.concatenate([own, mid, end], axis=1), rolled, hs, band)
    sub8 = lax.broadcasted_iota(jnp.int32, (8, 1), 0)
    for c in range(8):
        cols = slice(256 * c, 256 * c + 256)
        oa = jnp.dot(va[...], hs[0:208, cols].astype(BF16), preferred_element_type=F32)
        ob = jnp.dot(vb[...], hs[200:440, cols].astype(BF16), preferred_element_type=F32)
        pieces = []
        for r in range(ROWS):
            pieces += [
                oa[16 * r : 16 * r + 16],
                ob[16 * r : 16 * r + 8],
                jnp.where(sub8 == TARGET - 24, sci[r : r + 1, cols], ob[16 * r + 8 : 16 * r + 16]),
            ]
        e_out[:, cols] = jnp.concatenate(pieces, axis=0).astype(BF16)
    acc[...] = jnp.zeros_like(acc)

    def row_step(r, carry):
        e = e_out[pl.ds(pl.multiple_of(r * 32, 32), 32), :]
        rows = [e]
        for k in range(4):
            p = powers[16 * k : 16 * k + 16, :]
            rows += [e[0:16] * p, e[16:32] * p]
        g = lax.dot_general(
            e,
            jnp.concatenate(rows, axis=0),
            (((1,), (1,)), ((), ())),
            preferred_element_type=F32,
        )
        v = (first_row + r).astype(F32) * (2.0 / 256.0) + (1.0 / 256.0 - 1.0)
        last[:, 0:32] += g[:, TC : TC + 32]
        g = g[:, 0:TC]
        scale = v
        acc[0] += g
        for m in range(1, 5):
            acc[m] += g * scale
            scale = scale * v
        return carry

    last[...] = jnp.zeros_like(last)
    lax.fori_loop(0, ROWS, row_step, 0, unroll=4)
    units = (
        acc[0],
        acc[1],
        jnp.where(lane < 96, acc[2], pltpu.roll(last[...], 96, 1)),
        jnp.where(lane < 64, acc[3], pltpu.roll(acc[4], 64, 1)),
    )
    for i, unit in enumerate(units):
        for j in range(4):
            mom_out[4 * i + j] = unit[8 * j : 8 * j + 8]


def unit_of(k, m):
    if m < 2 and k < 4:
        return m, k
    if m == 2:
        return 2, k
    return {(4, 0): (2, 3), (0, 3): (3, 0), (1, 3): (3, 1), (0, 4): (3, 2)}[(k, m)]


def inverse2(m):
    (a, b), (c, d) = m
    r = 1.0 / (a * d - b * c)
    return (d * r, -b * r), (-c * r, a * r)


def times2(x, y):
    return tuple(tuple(x[i][0] * y[0][j] + x[i][1] * y[1][j] for j in range(2)) for i in range(2))


def plus2(x, y, sign):
    return tuple(tuple(x[i][j] + sign * y[i][j] for j in range(2)) for i in range(2))


def factor4(p):
    part = lambda i, j: tuple(tuple(p[2 * i + a][2 * j + b] for b in range(2)) for a in range(2))
    head = inverse2(part(0, 0))
    x = times2(head, part(0, 1))
    low = part(1, 0)
    return head, x, low, inverse2(plus2(part(1, 1), times2(low, x), -1.0))


def solve4(parts, r):
    head, x, low, tail = parts
    y = [head[i][0] * r[0] + head[i][1] * r[1] for i in range(2)]
    z = [r[2 + i] - (low[i][0] * y[0] + low[i][1] * y[1]) for i in range(2)]
    u = [tail[i][0] * z[0] + tail[i][1] * z[1] for i in range(2)]
    return [y[i] - (x[i][0] * u[0] + x[i][1] * u[1]) for i in range(2)] + u


def sweep_panel(mat, zero, q, lane):
    t = q // 4
    top = 32 * q
    base = 32 * (q % 4)
    sub = lax.broadcasted_iota(jnp.int32, (8, TC), 0)
    tiles = [[mat[top + 8 * i : top + 8 * i + 8, TC * h : TC * h + TC] for h in range(2)] for i in range(4)]
    for k in range(0, 28, 4):
        i0, s0, l0 = k // 8, k % 8, base + k
        cols = [
            [jnp.broadcast_to(tiles[i][t][:, l0 + j : l0 + j + 1], (8, TC)) for j in range(4)]
            for i in range(4)
        ]
        whole_cols = [cols[i0][j] + zero for j in range(4)]
        p = [
            [jnp.broadcast_to(whole_cols[j][s0 + i : s0 + i + 1], (8, TC)) for j in range(4)]
            for i in range(4)
        ]
        parts = factor4(p)
        in_lane = (lane >= l0) & (lane < l0 + 4)
        in_row = (sub >= s0) & (sub < s0 + 4)
        rows = []
        for h in range(2):
            r = [jnp.broadcast_to(tiles[i0][h][s0 + j : s0 + j + 1], (8, TC)) for j in range(4)]
            if h == t:
                r = [jnp.where(in_lane, jnp.where(lane == l0 + j, 1.0, 0.0), r[j]) for j in range(4)]
            rows.append(solve4(parts, r))
        for i in range(4):
            c = cols[i]
            if i == i0:
                c = [jnp.where(in_row, jnp.where(sub == s0 + j, -1.0, 0.0), c[j]) for j in range(4)]
            for h in range(2):
                old = tiles[i][h]
                if h == t:
                    old = jnp.where(in_lane, 0.0, old)
                if i == i0:
                    old = jnp.where(in_row, 0.0, old)
                u = rows[h]
                tiles[i][h] = old - ((c[0] * u[0] + c[1] * u[1]) + (c[2] * u[2] + c[3] * u[3]))
    inside = (lane >= base) & (lane < base + 28)
    swept = [[], []]
    for i in range(4):
        for h in range(2):
            f = tiles[i][h]
            if h == t:
                f = jnp.where(inside, -f, f)
            if i == 3:
                f = jnp.where(sub < 4, f, 0.0)
            swept[h].append(f)
    f = jnp.concatenate([jnp.concatenate(swept[h], axis=0) for h in range(2)], axis=1)
    f_hi = f.astype(BF16)
    f = f - f_hi.astype(F32)
    f_mid = f.astype(BF16)
    f_lo = (f - f_mid.astype(F32)).astype(BF16)
    right = jnp.concatenate(
        [f_hi, f_mid, f_hi, f_lo, f_hi, f_mid, jnp.zeros((64, 2 * TC), BF16)], axis=0
    )
    z = jnp.where(inside, mat[top + 32 : 200, TC * t : TC * t + TC], 0.0)
    if base:
        z = pltpu.roll(z, 128 - base, 1)
    z = z + pltpu.roll(z, 32, 1)
    z = z + pltpu.roll(z, 64, 1)
    z_hi = z.astype(BF16).astype(F32)
    z = z - z_hi
    z_mid = z.astype(BF16).astype(F32)
    z_lo = z - z_mid
    slot = lax.shift_right_logical(lane, 5)
    left = jnp.concatenate(
        [
            jnp.where(slot == 2, z_mid, z_hi),
            jnp.where(slot == 0, z_lo, jnp.where(slot == 1, z_mid, 0.0)),
        ],
        axis=1,
    ).astype(BF16)
    change = jnp.dot(left, right, preferred_element_type=F32)
    for h in range(2):
        old = mat[top + 32 : 200, TC * h : TC * h + TC]
        if h == t:
            old = jnp.where(inside, 0.0, old)
        mat[top + 32 : 200, TC * h : TC * h + TC] = old - change[:, TC * h : TC * h + TC]


def apply_stage(order, first_row, moms, e_ref, sci, upow, out, mat, fx):
    units = [jnp.concatenate([moms[4 * i + j] for j in range(4)], axis=0) for i in range(4)]
    lane = lax.broadcasted_iota(jnp.int32, (1, TC), 1)
    row = lax.broadcasted_iota(jnp.int32, (32, 1), 0)
    degree = lambda q: 0 if q == 0 else (1 if q < 3 else 2)

    def col_active(t):
        q = lax.shift_right_logical(lane, 5) + 4 * t
        deg = jnp.where(q >= 1, 1, 0) + jnp.where(q >= 3, 1, 0)
        return (deg <= order) | (lax.bitwise_and(lane, 31) == ONES)

    for q in range(6):
        row_on = (degree(q) <= order) | (row == ONES)
        for t in range(2):
            block = jnp.zeros((32, TC), F32)
            for s in range(4 if t == 0 else 2):
                p = 4 * t + s
                i, k = unit_of(mono[q][0] + mono[p][0], mono[q][1] + mono[p][1])
                piece = units[i]
                if s != k:
                    piece = pltpu.roll(piece, (32 * (s - k)) % 128, 1)
                block = jnp.where(lax.shift_right_logical(lane, 5) == s, piece, block)
            both = row_on & col_active(t)
            block = jnp.where(both, block, 0.0)
            if t == q // 4:
                diag = lane == row + 32 * (q % 4)
                block = jnp.where(diag, jnp.where(both, block, 1.0) * (1.0 + ridge), block)
            mat[32 * q : 32 * q + 32, TC * t : TC * t + TC] = block
            if q == 0:
                mat[192:200, TC * t : TC * t + TC] = jnp.where(col_active(t), block[24:32], 0.0)
    fx[...] = jnp.zeros_like(fx)
    zero = fx[...]
    for q in range(6):
        sweep_panel(mat, zero, q, lane)
    coef = []
    for q in range(6):
        z = mat[192:200, TC * (q // 4) : TC * (q // 4) + TC]
        z = jnp.broadcast_to(z[TARGET - 24 : TARGET - 23], (8, TC))
        if q % 4:
            z = pltpu.roll(z, 128 - 32 * (q % 4), 1)
        z = jnp.where(lane < 28, z, 0.0)
        z = z + pltpu.roll(z, 32, 1)
        z = z + pltpu.roll(z, 64, 1)
        coef.append(jnp.concatenate([z, z], axis=0))
    row16 = lax.broadcasted_iota(jnp.int32, (16, 1), 0)
    v = (first_row + row16).astype(F32) * (2.0 / 256.0) + (1.0 / 256.0 - 1.0)
    parts = (coef[0] + v * (coef[2] + v * coef[5]), coef[1] + v * coef[4], coef[3])
    his, los = [], []
    for p in parts:
        wide_p = jnp.concatenate(
            [jnp.where(row16 == 4 * n + lax.shift_right_logical(lane, 5), p, 0.0) for n in range(4)],
            axis=1,
        )
        h = wide_p.astype(BF16)
        his.append(h)
        los.append((wide_p - h.astype(F32)).astype(BF16))
    res = jnp.dot(jnp.concatenate(his + los, axis=0), e_ref[...], preferred_element_type=F32)
    t0, t1, t2 = (res[16 * i : 16 * i + 16] + res[48 + 16 * i : 64 + 16 * i] for i in range(3))
    u = jnp.concatenate([upow[...]] * 2, axis=0)
    out[...] = sci[...] - (t0 + u * (t1 + u * t2))


MESH = pl.DeviceIdType.MESH


def whole_kernel(
    ccds, strips, shift_h, order_h, source_h, slot_h, store_h, sci_h, band_h, va_h, vb_h, upow_h, powers_h, out,
    sent, got, sent2, got2, sci, band, va, vb, upow, powers, e, rolled, hs, acc, last, mom, parts, part, totals, mat, fx,
    shift, order, source, slot, store, local, send, recv, send2, recv2, s1, r1, s2, r2,
):
    ccd = lax.axis_index("ccd")
    strip = lax.axis_index("strip")
    count = ccds * strips
    me = ccd * strips + strip
    barrier = pltpu.get_barrier_semaphore()
    loads = [
        pltpu.make_async_copy(h, v, local.at[i])
        for i, (h, v) in enumerate(
            ((source_h, source), (slot_h, slot), (store_h, store), (shift_h, shift), (order_h, order),
             (band_h, band), (va_h, va), (vb_h, vb), (upow_h, upow), (powers_h, powers), (sci_h, sci))
        )
    ]

    hops = (0, 1, 2, 1)
    turn = lambda i, k: lax.rem(i + k, 4)
    shifts = [(y, c, z, x) for y in range(4) for c in range(2) for z in range(4) for x in range(4)]
    shifts.sort(key=lambda o: -(hops[o[0]] + hops[o[2]] + hops[o[3]] + 0.5 * o[1]))
    rows = [[turn(ccd // 2, y) * 2 + lax.rem(ccd + c, 2) for c in range(2)] for y in range(4)]
    cells = [[turn(strip // 4, z) * 4 + turn(lax.rem(strip, 4), x) for x in range(4)] for z in range(4)]

    def each_peer(act):
        for y, c, z, x in shifts[:-1]:
            act(rows[y][c], cells[z][x])

    each_peer(
        lambda c, k: pl.semaphore_signal(barrier, inc=1, device_id=(c, k), device_id_type=MESH)
    )
    for load in loads:
        load.start()
    for load in loads[:3]:
        load.wait()

    tiles = source.shape[0]
    flat = tiles * ROWS
    sheet = jnp.concatenate([store[...].reshape(flat, TC), jnp.zeros((-flat % TC, TC), F32)], axis=0)
    near = sheet.shape[0] // TC
    for i in range(near):
        sent[pl.ds(i, count, stride=near), :] = jnp.transpose(sheet[TC * i : TC * i + TC])
    for i in range(near):
        got[pl.ds(near * me + i, 1), :] = sent[pl.ds(near * me + i, 1), :]
    pl.semaphore_wait(barrier, count - 1)

    def send_all(src, dst, size, done, arrived):
        each_peer(
            lambda c, k: pltpu.make_async_remote_copy(
                src_ref=src.at[pl.ds(size * (c * strips + k), size)],
                dst_ref=dst.at[pl.ds(size * me, size)],
                send_sem=done,
                recv_sem=arrived,
                device_id=(c, k),
                device_id_type=MESH,
            ).start()
        )

    send_all(sent, got, near, send, recv)
    rest = got.at[pl.ds(0, near * (count - 1))]
    pltpu.make_async_copy(rest, rest, recv).wait()
    sheet = jnp.concatenate(
        [jnp.transpose(got[pl.ds(i, count, stride=near), :]) for i in range(near)], axis=0
    )
    found = []
    for t in range(tiles):
        owner = jnp.broadcast_to(source[t : t + 1, :], (8, count))
        place = jnp.broadcast_to(slot[t : t + 1, :], (8, count))
        for h in range(0, ROWS, 8):
            tile = jnp.zeros((8, count), F32)
            for p in range(tiles):
                tile = jnp.where(
                    place == p,
                    jnp.take_along_axis(
                        sheet[ROWS * p + h : ROWS * p + h + 8], owner, axis=1, mode="promise_in_bounds"
                    ),
                    tile,
                )
            found.append(tile)
    mine = jnp.concatenate(found, axis=0)
    up = pack_rows(pltpu.roll(pltpu.roll(mine, 1, 1).reshape(tiles, ROWS, count), 16 - 5, 1))
    down = pack_rows(pltpu.roll(mine, count - 1, 1).reshape(tiles, ROWS, count))
    half = tiles // 2 * 24
    sheet = jnp.concatenate(
        [
            mine,
            up.reshape(half, count),
            down.reshape(half, count),
            jnp.zeros((-(flat + 2 * half) % TC, count), F32),
        ],
        axis=0,
    )
    far = sheet.shape[0] // TC
    for i in range(far):
        sent2[pl.ds(i, count, stride=far), :] = jnp.transpose(sheet[TC * i : TC * i + TC])
    send_all(sent2, got2, far, send2, recv2)
    for i in range(far):
        got2[pl.ds(far * me + i, 1), :] = sent2[pl.ds(far * me + i, 1), :]
    for load in loads[3:]:
        load.wait()
    rest2 = got2.at[pl.ds(0, far * (count - 1))]
    pltpu.make_async_copy(rest2, rest2, recv2).wait()
    sheet = jnp.concatenate(
        [jnp.transpose(got2[pl.ds(i, count, stride=far), :]) for i in range(far)], axis=0
    )
    own = sheet[:flat].reshape(tiles, ROWS, TC)
    above = unpack_rows(sheet[flat : flat + half].reshape(tiles // 2, 24, TC))
    below = unpack_rows(sheet[flat + half : flat + 2 * half].reshape(tiles // 2, 24, TC))
    above = jnp.where(strip > 0, above, 0.0)
    below = jnp.where(strip < strips - 1, below, 0.0)
    first_row = strip * ROWS
    fit_stage(shift[0], first_row, own, above, below, sci, band, va, vb, powers, e, mom, rolled, hs, acc, last)
    peers = [(ccd, cells[z][x]) for y, c, z, x in shifts[:-1] if y == 0 and c == 0]
    for to in peers:
        pltpu.make_async_remote_copy(
            src_ref=mom.at[to[1]],
            dst_ref=parts.at[strip],
            send_sem=s1,
            recv_sem=r1,
            device_id=to,
            device_id_type=MESH,
        ).start()
    parts[strip] = mom[strip]
    few = parts.at[pl.ds(0, strips - 1)]
    pltpu.make_async_copy(few, few, r1).wait()
    total = parts[0]
    for i in range(1, strips):
        total = total + parts[i]
    part[...] = total
    for to in peers:
        pltpu.make_async_remote_copy(
            src_ref=part,
            dst_ref=totals.at[strip],
            send_sem=s2,
            recv_sem=r2,
            device_id=to,
            device_id_type=MESH,
        ).start()
    totals[strip] = total
    pltpu.make_async_copy(few, few, r2).wait()
    apply_stage(order[0], first_row, totals, e, sci, upow, out, mat, fx)
    pltpu.make_async_copy(rest, rest, send).wait()
    pltpu.make_async_copy(rest2, rest2, send2).wait()
    pltpu.make_async_copy(few, few, s1).wait()
    pltpu.make_async_copy(few, few, s2).wait()


VM = pl.BlockSpec(memory_space=pltpu.VMEM)
SM = pl.BlockSpec(memory_space=pltpu.SMEM)
ANY = pl.BlockSpec(memory_space=pl.ANY)
LIMIT = 60 * 1024 * 1024


def whole(shift, order, source, slot, store, sci, ccds, strips):
    count = ccds * strips
    tiles = source.shape[0]
    near = -(-tiles * ROWS // TC)
    far = -(-(tiles * ROWS + tiles * 24) // TC)
    tables = [band_matrix(), *vertical_matrices(), column_rows(), column_factors()]
    blocks = pltpu.VMEM((strips, 128 // strips, TC), F32)
    dma = pltpu.SemaphoreType.DMA
    return pl.pallas_call(
        lambda *refs: whole_kernel(ccds, strips, *refs),
        out_shape=pltpu.VMEM((ROWS, COLS), F32),
        in_specs=[ANY] * 11,
        out_specs=VM,
        scratch_shapes=[
            pltpu.VMEM((near * count, TC), F32),
            pltpu.VMEM((near * count, TC), F32),
            pltpu.VMEM((far * count, TC), F32),
            pltpu.VMEM((far * count, TC), F32),
            pltpu.VMEM((ROWS, COLS), F32),
            *[pltpu.VMEM(x.shape, x.dtype) for x in tables],
            pltpu.VMEM((ROWS * 32, COLS), BF16),
            pltpu.VMEM((tiles + 1, SLOTS, TC), F32),
            pltpu.VMEM((440, COLS), F32),
            pltpu.VMEM((5, 32, TC), F32),
            pltpu.VMEM((32, TC), F32),
            blocks,
            blocks,
            pltpu.VMEM((128 // strips, TC), F32),
            blocks,
            pltpu.VMEM((200, 2 * TC), F32),
            pltpu.VMEM((8, TC), F32),
            pltpu.SMEM((1,), jnp.int32),
            pltpu.SMEM((1,), jnp.int32),
            pltpu.VMEM(source.shape, jnp.int32),
            pltpu.VMEM(source.shape, jnp.int32),
            pltpu.VMEM(store.shape, F32),
            dma((11,)),
            dma,
            dma,
            dma,
            dma,
            dma,
            dma,
            dma,
            dma,
        ],
        compiler_params=pltpu.CompilerParams(
            collective_id=0, has_side_effects=True, vmem_limit_bytes=LIMIT
        ),
        name="whole",
    )(shift, order, source, slot, store, sci, *[jnp.asarray(x) for x in tables])


def body(tile_store, tile_source, tile_slot, shift_cols, spatial_order, science):
    strips = lax.axis_size("strip")
    return whole(
        shift_cols, spatial_order, tile_source.T, tile_slot.T, tile_store, science,
        lax.axis_size("ccd"), strips,
    )


def solution(mesh):
    placed = (
        P(("ccd", "strip"), None, None),
        P(),
        P(),
        P("ccd"),
        P("ccd"),
        P(("ccd", "strip"), None),
    )
    return jax.shard_map(
        body, mesh=mesh, in_specs=placed, out_specs=P(("ccd", "strip"), None), check_vma=False
    )
```

```python
import jax
import jax.numpy as jnp
import numpy as np
from jax import lax
from jax.experimental import pallas as pl
from jax.experimental.pallas import tpu as pltpu
from jax.sharding import PartitionSpec as P

H = 11
CM = 128
ROWS = 16
COLS = 2048
TC = 128
SLOTS = 40
TARGET = 28
ONES = 15

sigmas = (0.7, 1.5, 3.0)
tops = (4, 2, 2)
mono = ((0, 0), (1, 0), (0, 1), (2, 0), (1, 1), (0, 2))
ridge = 0.05
F32 = jnp.float32
BF16 = jnp.bfloat16


def tap_table():
    a = np.arange(-H, H + 1).astype(np.float64)
    rows = []
    for s, top in zip(sigmas, tops):
        e = np.exp(-a * a / (2.0 * s * s))
        for n in range(top + 1):
            rows.append(e * (a / s) ** n / e.sum())
    return np.stack(rows).astype(np.float32)


def to_bf16(x):
    return x.astype(jnp.bfloat16.dtype)


def band_matrix():
    taps = tap_table()
    hi = to_bf16(taps).astype(np.float32)
    lo = to_bf16(taps - hi).astype(np.float32)
    full = []
    for part in (hi, lo):
        m = np.zeros((160, 11, TC), np.float32)
        for f in range(11):
            for x in range(TC):
                m[x : x + 23, f, x] = part[f]
        full.append(m.reshape(160, 11 * TC))
    h, l = full
    tail = np.zeros((TC, 11 * TC), np.float32)
    tail[0:32], tail[32:64], tail[64:96] = h[128:], h[128:], l[128:]
    return to_bf16(np.concatenate([h[:128], h[:128], l[:128], tail]))


def slot_of(row):
    return 16 + row if row < H else (row - H if row < H + ROWS else row)


def vertical_matrices():
    taps = to_bf16(tap_table()).astype(np.float32)
    first = np.zeros((ROWS, 16, 208), np.float32)
    second = np.zeros((ROWS, 16, 240), np.float32)
    slot = 0
    for i in range(5):
        for j in range(5 - i):
            for r in range(ROWS):
                for a in range(23):
                    first[r, slot, i * SLOTS + slot_of(r + a)] = taps[j, a]
            slot += 1
    first[:, ONES, 38] = 1.0
    slot = 0
    for g in range(2):
        for i in range(3):
            for j in range(3 - i):
                for r in range(ROWS):
                    for a in range(23):
                        second[r, slot, (3 * g + i) * SLOTS + slot_of(r + a)] = taps[5 + 3 * g + j, a]
                slot += 1
    return to_bf16(first.reshape(256, 208)), to_bf16(second.reshape(256, 240))


def column_powers():
    u = 2.0 * (np.arange(COLS).astype(np.float32) + np.float32(0.5)) / np.float32(COLS) - np.float32(1.0)
    u = u.astype(np.float32)
    return u


def column_rows():
    return np.stack([column_powers()] * 8)


def column_factors():
    u = column_powers()
    return to_bf16(np.concatenate([np.stack([u ** (k + 1)] * 16) for k in range(2)]))


def pack_rows(x):
    pairs = x.reshape(x.shape[0] // 2, 2, 16, TC)
    a, b = pairs[:, 0], pairs[:, 1]
    row = lax.broadcasted_iota(jnp.int32, (1, 8, TC), 1)
    mid = jnp.where(row < 3, a[:, 8:], pltpu.roll(b[:, :8], 3, 1))
    return jnp.concatenate([a[:, :8], mid, pltpu.roll(b, H, 1)[:, :8]], axis=1)


def unpack_rows(x):
    row = lax.broadcasted_iota(jnp.int32, (1, 8, TC), 1)
    end = pltpu.roll(x[:, 16:], 5, 1)
    b = jnp.concatenate([jnp.where(row < 5, pltpu.roll(x[:, 8:16], 5, 1), end), end], axis=1)
    pairs = jnp.concatenate([x[:, None, :16], b[:, None]], axis=1)
    return pairs.reshape(2 * x.shape[0], 16, TC)


def window_rows(shift, x, rolled, hs, band):
    count, rows, _ = x.shape
    start = CM + shift - H
    tile = lax.shift_right_logical(start, 7)
    rem = lax.bitwise_and(start, 127)
    rolled[0:count, 0:rows] = pltpu.roll(x, lax.bitwise_and(128 - rem, 127), 2)
    rolled[count : count + 1, 0:rows] = jnp.zeros((1, rows, TC), F32)
    lane3 = lax.broadcasted_iota(jnp.int32, (1, rows, TC), 2)
    w = jnp.where(
        lane3 < 128 - rem, rolled[pl.ds(tile, 17), 0:rows], rolled[pl.ds(tile + 1, 17), 0:rows]
    ).reshape(17 * rows, TC)
    main = w[: 16 * rows]
    nxt = w[rows:]
    hi = main.astype(BF16)
    lo = (main - hi.astype(F32)).astype(BF16)
    nhi = nxt.astype(BF16).astype(F32)
    nlo = nxt - nhi
    lane = lax.broadcasted_iota(jnp.int32, (1, TC), 1)
    tail = jnp.where(
        lane < 32,
        nhi,
        jnp.where(lane < 64, pltpu.roll(nlo, 32, 1), jnp.where(lane < 96, pltpu.roll(nhi, 64, 1), 0.0)),
    ).astype(BF16)
    lhs = jnp.concatenate([hi, lo, hi, tail], axis=1)
    for c in range(6):
        n = 256 if c < 5 else 128
        res = jnp.dot(lhs, band[:, 256 * c : 256 * c + n], preferred_element_type=F32)
        for f in range(2 * c, 2 * c + n // TC):
            o = (f - 2 * c) * TC
            for j in range(16):
                hs[f * SLOTS : f * SLOTS + rows, j * TC : (j + 1) * TC] = res[
                    j * rows : (j + 1) * rows, o : o + TC
                ]


def fit_stage(shift, first_row, own, above, below, sci, band, va, vb, powers, e_out, mom_out, rolled, hs, acc, last):
    row16 = lax.broadcasted_iota(jnp.int32, (1, 16, TC), 1)
    row8 = lax.broadcasted_iota(jnp.int32, (1, 8, TC), 1)
    lane = lax.broadcasted_iota(jnp.int32, (1, TC), 1)
    b = pltpu.roll(below, H, 1)
    mid = jnp.where(row16 < H, above, b)
    end = jnp.where(row8 < 6, b[:, :8], jnp.where(row8 == 6, 1.0, 0.0))
    window_rows(shift, jnp.concatenate([own, mid, end], axis=1), rolled, hs, band)
    sub8 = lax.broadcasted_iota(jnp.int32, (8, 1), 0)
    for c in range(8):
        cols = slice(256 * c, 256 * c + 256)
        oa = jnp.dot(va[...], hs[0:208, cols].astype(BF16), preferred_element_type=F32)
        ob = jnp.dot(vb[...], hs[200:440, cols].astype(BF16), preferred_element_type=F32)
        pieces = []
        for r in range(ROWS):
            pieces += [
                oa[16 * r : 16 * r + 16],
                ob[16 * r : 16 * r + 8],
                jnp.where(sub8 == TARGET - 24, sci[r : r + 1, cols], ob[16 * r + 8 : 16 * r + 16]),
            ]
        e_out[:, cols] = jnp.concatenate(pieces, axis=0).astype(BF16)
    acc[...] = jnp.zeros_like(acc)

    def row_step(r, carry):
        e = e_out[pl.ds(pl.multiple_of(r * 32, 32), 32), :]
        rows = [e]
        for k in range(2):
            p = powers[16 * k : 16 * k + 16, :]
            rows += [e[0:16] * p, e[16:32] * p]
        g = lax.dot_general(
            jnp.concatenate([e] + rows[3:], axis=0),
            jnp.concatenate(rows, axis=0),
            (((1,), (1,)), ((), ())),
            preferred_element_type=F32,
        )
        v = (first_row + r).astype(F32) * (2.0 / 256.0) + (1.0 / 256.0 - 1.0)
        low = g[32:64]
        g = g[0:32]
        last[0, :, 0:96] += low
        last[1, :, 0:96] += low * v
        scale = v
        acc[0, :, 0:96] += g
        for m in range(1, 5):
            acc[m, :, 0:96] += g * scale
            scale = scale * v
        return carry

    last[...] = jnp.zeros_like(last)
    lax.fori_loop(0, ROWS, row_step, 0, unroll=4)
    units = (
        jnp.where(lane < 96, acc[0], pltpu.roll(last[0], 64, 1)),
        jnp.where(lane < 96, acc[1], pltpu.roll(last[1], 64, 1)),
        jnp.where(lane < 96, acc[2], pltpu.roll(last[0], 32, 1)),
        jnp.where(lane < 64, acc[3], pltpu.roll(acc[4], 64, 1)),
    )
    for i, unit in enumerate(units):
        for j in range(4):
            mom_out[4 * i + j] = unit[8 * j : 8 * j + 8]


def unit_of(k, m):
    if m < 2 and k < 4:
        return m, k
    if m == 2:
        return 2, k
    return {(4, 0): (2, 3), (0, 3): (3, 0), (1, 3): (3, 1), (0, 4): (3, 2)}[(k, m)]


def inverse2(m):
    (a, b), (c, d) = m
    r = 1.0 / (a * d - b * c)
    return (d * r, -b * r), (-c * r, a * r)


def times2(x, y):
    return tuple(tuple(x[i][0] * y[0][j] + x[i][1] * y[1][j] for j in range(2)) for i in range(2))


def plus2(x, y, sign):
    return tuple(tuple(x[i][j] + sign * y[i][j] for j in range(2)) for i in range(2))


def factor4(p):
    part = lambda i, j: tuple(tuple(p[2 * i + a][2 * j + b] for b in range(2)) for a in range(2))
    head = inverse2(part(0, 0))
    x = times2(head, part(0, 1))
    low = part(1, 0)
    return head, x, low, inverse2(plus2(part(1, 1), times2(low, x), -1.0))


def solve4(parts, r):
    head, x, low, tail = parts
    y = [head[i][0] * r[0] + head[i][1] * r[1] for i in range(2)]
    z = [r[2 + i] - (low[i][0] * y[0] + low[i][1] * y[1]) for i in range(2)]
    u = [tail[i][0] * z[0] + tail[i][1] * z[1] for i in range(2)]
    return [y[i] - (x[i][0] * u[0] + x[i][1] * u[1]) for i in range(2)] + u


def sweep_panel(mat, zero, q, lane):
    t = q // 4
    top = 32 * q
    base = 32 * (q % 4)
    sub = lax.broadcasted_iota(jnp.int32, (8, TC), 0)
    tiles = [[mat[top + 8 * i : top + 8 * i + 8, TC * h : TC * h + TC] for h in range(2)] for i in range(4)]
    for k in range(0, 28, 4):
        i0, s0, l0 = k // 8, k % 8, base + k
        cols = [
            [jnp.broadcast_to(tiles[i][t][:, l0 + j : l0 + j + 1], (8, TC)) for j in range(4)]
            for i in range(4)
        ]
        whole_cols = [cols[i0][j] + zero for j in range(4)]
        p = [
            [jnp.broadcast_to(whole_cols[j][s0 + i : s0 + i + 1], (8, TC)) for j in range(4)]
            for i in range(4)
        ]
        parts = factor4(p)
        in_lane = (lane >= l0) & (lane < l0 + 4)
        in_row = (sub >= s0) & (sub < s0 + 4)
        rows = []
        for h in range(2):
            r = [jnp.broadcast_to(tiles[i0][h][s0 + j : s0 + j + 1], (8, TC)) for j in range(4)]
            if h == t:
                r = [jnp.where(in_lane, jnp.where(lane == l0 + j, 1.0, 0.0), r[j]) for j in range(4)]
            rows.append(solve4(parts, r))
        for i in range(4):
            c = cols[i]
            if i == i0:
                c = [jnp.where(in_row, jnp.where(sub == s0 + j, -1.0, 0.0), c[j]) for j in range(4)]
            for h in range(2):
                old = tiles[i][h]
                if h == t:
                    old = jnp.where(in_lane, 0.0, old)
                if i == i0:
                    old = jnp.where(in_row, 0.0, old)
                u = rows[h]
                tiles[i][h] = old - ((c[0] * u[0] + c[1] * u[1]) + (c[2] * u[2] + c[3] * u[3]))
    inside = (lane >= base) & (lane < base + 28)
    swept = [[], []]
    for i in range(4):
        for h in range(2):
            f = tiles[i][h]
            if h == t:
                f = jnp.where(inside, -f, f)
            if i == 3:
                f = jnp.where(sub < 4, f, 0.0)
            swept[h].append(f)
    f = jnp.concatenate([jnp.concatenate(swept[h], axis=0) for h in range(2)], axis=1)
    f_hi = f.astype(BF16)
    f = f - f_hi.astype(F32)
    f_mid = f.astype(BF16)
    f_lo = (f - f_mid.astype(F32)).astype(BF16)
    right = jnp.concatenate(
        [f_hi, f_mid, f_hi, f_lo, f_hi, f_mid, jnp.zeros((64, 2 * TC), BF16)], axis=0
    )
    z = jnp.where(inside, mat[top + 32 : 200, TC * t : TC * t + TC], 0.0)
    if base:
        z = pltpu.roll(z, 128 - base, 1)
    z = z + pltpu.roll(z, 32, 1)
    z = z + pltpu.roll(z, 64, 1)
    z_hi = z.astype(BF16).astype(F32)
    z = z - z_hi
    z_mid = z.astype(BF16).astype(F32)
    z_lo = z - z_mid
    slot = lax.shift_right_logical(lane, 5)
    left = jnp.concatenate(
        [
            jnp.where(slot == 2, z_mid, z_hi),
            jnp.where(slot == 0, z_lo, jnp.where(slot == 1, z_mid, 0.0)),
        ],
        axis=1,
    ).astype(BF16)
    change = jnp.dot(left, right, preferred_element_type=F32)
    for h in range(2):
        old = mat[top + 32 : 200, TC * h : TC * h + TC]
        if h == t:
            old = jnp.where(inside, 0.0, old)
        mat[top + 32 : 200, TC * h : TC * h + TC] = old - change[:, TC * h : TC * h + TC]


def apply_stage(order, first_row, moms, e_ref, sci, upow, out, mat, fx):
    units = [jnp.concatenate([moms[4 * i + j] for j in range(4)], axis=0) for i in range(4)]
    lane = lax.broadcasted_iota(jnp.int32, (1, TC), 1)
    row = lax.broadcasted_iota(jnp.int32, (32, 1), 0)
    degree = lambda q: 0 if q == 0 else (1 if q < 3 else 2)

    def col_active(t):
        q = lax.shift_right_logical(lane, 5) + 4 * t
        deg = jnp.where(q >= 1, 1, 0) + jnp.where(q >= 3, 1, 0)
        return (deg <= order) | (lax.bitwise_and(lane, 31) == ONES)

    for q in range(6):
        row_on = (degree(q) <= order) | (row == ONES)
        for t in range(2):
            block = jnp.zeros((32, TC), F32)
            for s in range(4 if t == 0 else 2):
                p = 4 * t + s
                i, k = unit_of(mono[q][0] + mono[p][0], mono[q][1] + mono[p][1])
                piece = units[i]
                if s != k:
                    piece = pltpu.roll(piece, (32 * (s - k)) % 128, 1)
                block = jnp.where(lax.shift_right_logical(lane, 5) == s, piece, block)
            both = row_on & col_active(t)
            block = jnp.where(both, block, 0.0)
            if t == q // 4:
                diag = lane == row + 32 * (q % 4)
                block = jnp.where(diag, jnp.where(both, block, 1.0) * (1.0 + ridge), block)
            mat[32 * q : 32 * q + 32, TC * t : TC * t + TC] = block
            if q == 0:
                mat[192:200, TC * t : TC * t + TC] = jnp.where(col_active(t), block[24:32], 0.0)
    fx[...] = jnp.zeros_like(fx)
    zero = fx[...]
    for q in range(6):
        sweep_panel(mat, zero, q, lane)
    coef = []
    for q in range(6):
        z = mat[192:200, TC * (q // 4) : TC * (q // 4) + TC]
        z = jnp.broadcast_to(z[TARGET - 24 : TARGET - 23], (8, TC))
        if q % 4:
            z = pltpu.roll(z, 128 - 32 * (q % 4), 1)
        z = jnp.where(lane < 28, z, 0.0)
        z = z + pltpu.roll(z, 32, 1)
        z = z + pltpu.roll(z, 64, 1)
        coef.append(jnp.concatenate([z, z], axis=0))
    row16 = lax.broadcasted_iota(jnp.int32, (16, 1), 0)
    v = (first_row + row16).astype(F32) * (2.0 / 256.0) + (1.0 / 256.0 - 1.0)
    parts = (coef[0] + v * (coef[2] + v * coef[5]), coef[1] + v * coef[4], coef[3])
    his, los = [], []
    for p in parts:
        wide_p = jnp.concatenate(
            [jnp.where(row16 == 4 * n + lax.shift_right_logical(lane, 5), p, 0.0) for n in range(4)],
            axis=1,
        )
        h = wide_p.astype(BF16)
        his.append(h)
        los.append((wide_p - h.astype(F32)).astype(BF16))
    res = jnp.dot(jnp.concatenate(his + los, axis=0), e_ref[...], preferred_element_type=F32)
    t0, t1, t2 = (res[16 * i : 16 * i + 16] + res[48 + 16 * i : 64 + 16 * i] for i in range(3))
    u = jnp.concatenate([upow[...]] * 2, axis=0)
    out[...] = sci[...] - (t0 + u * (t1 + u * t2))


MESH = pl.DeviceIdType.MESH


def whole_kernel(
    ccds, strips, shift_h, order_h, source_h, slot_h, store_h, sci_h, band_h, va_h, vb_h, upow_h, powers_h, out,
    sent, got, sent2, got2, sci, band, va, vb, upow, powers, e, rolled, hs, acc, last, mom, parts, part, totals, mat, fx,
    shift, order, source, slot, store, local, send, recv, send2, recv2, s1, r1, s2, r2,
):
    ccd = lax.axis_index("ccd")
    strip = lax.axis_index("strip")
    count = ccds * strips
    me = ccd * strips + strip
    barrier = pltpu.get_barrier_semaphore()
    loads = [
        pltpu.make_async_copy(h, v, local.at[i])
        for i, (h, v) in enumerate(
            ((source_h, source), (slot_h, slot), (store_h, store), (shift_h, shift), (order_h, order),
             (band_h, band), (va_h, va), (vb_h, vb), (upow_h, upow), (powers_h, powers), (sci_h, sci))
        )
    ]

    hops = (0, 1, 2, 1)
    turn = lambda i, k: lax.rem(i + k, 4)
    shifts = [(y, c, z, x) for y in range(4) for c in range(2) for z in range(4) for x in range(4)]
    shifts.sort(key=lambda o: -(hops[o[0]] + hops[o[2]] + hops[o[3]] + 0.5 * o[1]))
    rows = [[turn(ccd // 2, y) * 2 + lax.rem(ccd + c, 2) for c in range(2)] for y in range(4)]
    cells = [[turn(strip // 4, z) * 4 + turn(lax.rem(strip, 4), x) for x in range(4)] for z in range(4)]

    def each_peer(act):
        for y, c, z, x in shifts[:-1]:
            act(rows[y][c], cells[z][x])

    each_peer(
        lambda c, k: pl.semaphore_signal(barrier, inc=1, device_id=(c, k), device_id_type=MESH)
    )
    for load in loads:
        load.start()
    for load in loads[:3]:
        load.wait()

    tiles = source.shape[0]
    flat = tiles * ROWS
    sheet = jnp.concatenate([store[...].reshape(flat, TC), jnp.zeros((-flat % TC, TC), F32)], axis=0)
    near = sheet.shape[0] // TC
    for i in range(near):
        sent[pl.ds(i, count, stride=near), :] = jnp.transpose(sheet[TC * i : TC * i + TC])
    for i in range(near):
        got[pl.ds(near * me + i, 1), :] = sent[pl.ds(near * me + i, 1), :]
    pl.semaphore_wait(barrier, count - 1)

    def send_all(src, dst, size, done, arrived):
        each_peer(
            lambda c, k: pltpu.make_async_remote_copy(
                src_ref=src.at[pl.ds(size * (c * strips + k), size)],
                dst_ref=dst.at[pl.ds(size * me, size)],
                send_sem=done,
                recv_sem=arrived,
                device_id=(c, k),
                device_id_type=MESH,
            ).start()
        )

    send_all(sent, got, near, send, recv)
    rest = got.at[pl.ds(0, near * (count - 1))]
    pltpu.make_async_copy(rest, rest, recv).wait()
    sheet = jnp.concatenate(
        [jnp.transpose(got[pl.ds(i, count, stride=near), :]) for i in range(near)], axis=0
    )
    found = []
    for t in range(tiles):
        owner = jnp.broadcast_to(source[t : t + 1, :], (8, count))
        place = jnp.broadcast_to(slot[t : t + 1, :], (8, count))
        for h in range(0, ROWS, 8):
            tile = jnp.zeros((8, count), F32)
            for p in range(tiles):
                tile = jnp.where(
                    place == p,
                    jnp.take_along_axis(
                        sheet[ROWS * p + h : ROWS * p + h + 8], owner, axis=1, mode="promise_in_bounds"
                    ),
                    tile,
                )
            found.append(tile)
    mine = jnp.concatenate(found, axis=0)
    up = pack_rows(pltpu.roll(pltpu.roll(mine, 1, 1).reshape(tiles, ROWS, count), 16 - 5, 1))
    down = pack_rows(pltpu.roll(mine, count - 1, 1).reshape(tiles, ROWS, count))
    half = tiles // 2 * 24
    sheet = jnp.concatenate(
        [
            mine,
            up.reshape(half, count),
            down.reshape(half, count),
            jnp.zeros((-(flat + 2 * half) % TC, count), F32),
        ],
        axis=0,
    )
    far = sheet.shape[0] // TC
    for i in range(far):
        sent2[pl.ds(i, count, stride=far), :] = jnp.transpose(sheet[TC * i : TC * i + TC])
    send_all(sent2, got2, far, send2, recv2)
    for i in range(far):
        got2[pl.ds(far * me + i, 1), :] = sent2[pl.ds(far * me + i, 1), :]
    for load in loads[3:]:
        load.wait()
    rest2 = got2.at[pl.ds(0, far * (count - 1))]
    pltpu.make_async_copy(rest2, rest2, recv2).wait()
    sheet = jnp.concatenate(
        [jnp.transpose(got2[pl.ds(i, count, stride=far), :]) for i in range(far)], axis=0
    )
    own = sheet[:flat].reshape(tiles, ROWS, TC)
    above = unpack_rows(sheet[flat : flat + half].reshape(tiles // 2, 24, TC))
    below = unpack_rows(sheet[flat + half : flat + 2 * half].reshape(tiles // 2, 24, TC))
    above = jnp.where(strip > 0, above, 0.0)
    below = jnp.where(strip < strips - 1, below, 0.0)
    first_row = strip * ROWS
    fit_stage(shift[0], first_row, own, above, below, sci, band, va, vb, powers, e, mom, rolled, hs, acc, last)
    peers = [(ccd, cells[z][x]) for y, c, z, x in shifts[:-1] if y == 0 and c == 0]
    for to in peers:
        pltpu.make_async_remote_copy(
            src_ref=mom.at[to[1]],
            dst_ref=parts.at[strip],
            send_sem=s1,
            recv_sem=r1,
            device_id=to,
            device_id_type=MESH,
        ).start()
    parts[strip] = mom[strip]
    few = parts.at[pl.ds(0, strips - 1)]
    pltpu.make_async_copy(few, few, r1).wait()
    total = parts[0]
    for i in range(1, strips):
        total = total + parts[i]
    part[...] = total
    for to in peers:
        pltpu.make_async_remote_copy(
            src_ref=part,
            dst_ref=totals.at[strip],
            send_sem=s2,
            recv_sem=r2,
            device_id=to,
            device_id_type=MESH,
        ).start()
    totals[strip] = total
    pltpu.make_async_copy(few, few, r2).wait()
    apply_stage(order[0], first_row, totals, e, sci, upow, out, mat, fx)
    pltpu.make_async_copy(rest, rest, send).wait()
    pltpu.make_async_copy(rest2, rest2, send2).wait()
    pltpu.make_async_copy(few, few, s1).wait()
    pltpu.make_async_copy(few, few, s2).wait()


VM = pl.BlockSpec(memory_space=pltpu.VMEM)
SM = pl.BlockSpec(memory_space=pltpu.SMEM)
ANY = pl.BlockSpec(memory_space=pl.ANY)
LIMIT = 60 * 1024 * 1024


def whole(shift, order, source, slot, store, sci, ccds, strips):
    count = ccds * strips
    tiles = source.shape[0]
    near = -(-tiles * ROWS // TC)
    far = -(-(tiles * ROWS + tiles * 24) // TC)
    tables = [band_matrix(), *vertical_matrices(), column_rows(), column_factors()]
    blocks = pltpu.VMEM((strips, 128 // strips, TC), F32)
    dma = pltpu.SemaphoreType.DMA
    return pl.pallas_call(
        lambda *refs: whole_kernel(ccds, strips, *refs),
        out_shape=pltpu.VMEM((ROWS, COLS), F32),
        in_specs=[ANY] * 11,
        out_specs=VM,
        scratch_shapes=[
            pltpu.VMEM((near * count, TC), F32),
            pltpu.VMEM((near * count, TC), F32),
            pltpu.VMEM((far * count, TC), F32),
            pltpu.VMEM((far * count, TC), F32),
            pltpu.VMEM((ROWS, COLS), F32),
            *[pltpu.VMEM(x.shape, x.dtype) for x in tables],
            pltpu.VMEM((ROWS * 32, COLS), BF16),
            pltpu.VMEM((tiles + 1, SLOTS, TC), F32),
            pltpu.VMEM((440, COLS), F32),
            pltpu.VMEM((5, 32, TC), F32),
            pltpu.VMEM((2, 32, TC), F32),
            blocks,
            blocks,
            pltpu.VMEM((128 // strips, TC), F32),
            blocks,
            pltpu.VMEM((200, 2 * TC), F32),
            pltpu.VMEM((8, TC), F32),
            pltpu.SMEM((1,), jnp.int32),
            pltpu.SMEM((1,), jnp.int32),
            pltpu.VMEM(source.shape, jnp.int32),
            pltpu.VMEM(source.shape, jnp.int32),
            pltpu.VMEM(store.shape, F32),
            dma((11,)),
            dma,
            dma,
            dma,
            dma,
            dma,
            dma,
            dma,
            dma,
        ],
        compiler_params=pltpu.CompilerParams(
            collective_id=0, has_side_effects=True, vmem_limit_bytes=LIMIT
        ),
        name="whole",
    )(shift, order, source, slot, store, sci, *[jnp.asarray(x) for x in tables])


def body(tile_store, tile_source, tile_slot, shift_cols, spatial_order, science):
    strips = lax.axis_size("strip")
    return whole(
        shift_cols, spatial_order, tile_source.T, tile_slot.T, tile_store, science,
        lax.axis_size("ccd"), strips,
    )


def solution(mesh):
    placed = (
        P(("ccd", "strip"), None, None),
        P(),
        P(),
        P("ccd"),
        P("ccd"),
        P(("ccd", "strip"), None),
    )
    return jax.shard_map(
        body, mesh=mesh, in_specs=placed, out_specs=P(("ccd", "strip"), None), check_vma=False
    )
```

```python
import jax
import jax.numpy as jnp
import numpy as np
from jax import lax
from jax.experimental import pallas as pl
from jax.experimental.pallas import tpu as pltpu
from jax.sharding import PartitionSpec as P

H = 11
CM = 128
ROWS = 16
COLS = 2048
TC = 128
SLOTS = 40
TARGET = 28
ONES = 15

sigmas = (0.7, 1.5, 3.0)
tops = (4, 2, 2)
mono = ((0, 0), (1, 0), (0, 1), (2, 0), (1, 1), (0, 2))
ridge = 0.05
F32 = jnp.float32
BF16 = jnp.bfloat16


def tap_table():
    a = np.arange(-H, H + 1).astype(np.float64)
    rows = []
    for s, top in zip(sigmas, tops):
        e = np.exp(-a * a / (2.0 * s * s))
        for n in range(top + 1):
            rows.append(e * (a / s) ** n / e.sum())
    return np.stack(rows).astype(np.float32)


def to_bf16(x):
    return x.astype(jnp.bfloat16.dtype)


def band_matrix():
    taps = tap_table()
    hi = to_bf16(taps).astype(np.float32)
    lo = to_bf16(taps - hi).astype(np.float32)
    full = []
    for part in (hi, lo):
        m = np.zeros((160, 11, TC), np.float32)
        for f in range(11):
            for x in range(TC):
                m[x : x + 23, f, x] = part[f]
        full.append(m.reshape(160, 11 * TC))
    h, l = full
    tail = np.zeros((TC, 11 * TC), np.float32)
    tail[0:32], tail[32:64], tail[64:96] = h[128:], h[128:], l[128:]
    return to_bf16(np.concatenate([h[:128], h[:128], l[:128], tail]))


def slot_of(row):
    return 16 + row if row < H else (row - H if row < H + ROWS else row)


def vertical_matrices():
    taps = to_bf16(tap_table()).astype(np.float32)
    first = np.zeros((ROWS, 16, 208), np.float32)
    second = np.zeros((ROWS, 16, 240), np.float32)
    slot = 0
    for i in range(5):
        for j in range(5 - i):
            for r in range(ROWS):
                for a in range(23):
                    first[r, slot, i * SLOTS + slot_of(r + a)] = taps[j, a]
            slot += 1
    first[:, ONES, 38] = 1.0
    slot = 0
    for g in range(2):
        for i in range(3):
            for j in range(3 - i):
                for r in range(ROWS):
                    for a in range(23):
                        second[r, slot, (3 * g + i) * SLOTS + slot_of(r + a)] = taps[5 + 3 * g + j, a]
                slot += 1
    return to_bf16(first.reshape(256, 208)), to_bf16(second.reshape(256, 240))


def column_powers():
    u = 2.0 * (np.arange(COLS).astype(np.float32) + np.float32(0.5)) / np.float32(COLS) - np.float32(1.0)
    u = u.astype(np.float32)
    return u


def column_rows():
    return np.stack([column_powers()] * 8)


def column_factors():
    u = column_powers()
    return to_bf16(np.concatenate([np.stack([u ** (k + 1)] * 16) for k in range(2)]))


def pack_rows(x):
    pairs = x.reshape(x.shape[0] // 2, 2, 16, TC)
    a, b = pairs[:, 0], pairs[:, 1]
    row = lax.broadcasted_iota(jnp.int32, (1, 8, TC), 1)
    mid = jnp.where(row < 3, a[:, 8:], pltpu.roll(b[:, :8], 3, 1))
    return jnp.concatenate([a[:, :8], mid, pltpu.roll(b, H, 1)[:, :8]], axis=1)


def unpack_rows(x):
    row = lax.broadcasted_iota(jnp.int32, (1, 8, TC), 1)
    end = pltpu.roll(x[:, 16:], 5, 1)
    b = jnp.concatenate([jnp.where(row < 5, pltpu.roll(x[:, 8:16], 5, 1), end), end], axis=1)
    pairs = jnp.concatenate([x[:, None, :16], b[:, None]], axis=1)
    return pairs.reshape(2 * x.shape[0], 16, TC)


def window_rows(shift, x, rolled, hs, band):
    count, rows, _ = x.shape
    start = CM + shift - H
    tile = lax.shift_right_logical(start, 7)
    rem = lax.bitwise_and(start, 127)
    rolled[0:count, 0:rows] = pltpu.roll(x, lax.bitwise_and(128 - rem, 127), 2)
    rolled[count : count + 1, 0:rows] = jnp.zeros((1, rows, TC), F32)
    lane3 = lax.broadcasted_iota(jnp.int32, (1, rows, TC), 2)
    w = jnp.where(
        lane3 < 128 - rem, rolled[pl.ds(tile, 17), 0:rows], rolled[pl.ds(tile + 1, 17), 0:rows]
    ).reshape(17 * rows, TC)
    main = w[: 16 * rows]
    nxt = w[rows:]
    hi = main.astype(BF16)
    lo = (main - hi.astype(F32)).astype(BF16)
    nhi = nxt.astype(BF16).astype(F32)
    nlo = nxt - nhi
    lane = lax.broadcasted_iota(jnp.int32, (1, TC), 1)
    tail = jnp.where(
        lane < 32,
        nhi,
        jnp.where(lane < 64, pltpu.roll(nlo, 32, 1), jnp.where(lane < 96, pltpu.roll(nhi, 64, 1), 0.0)),
    ).astype(BF16)
    lhs = jnp.concatenate([hi, lo, hi, tail], axis=1)
    for c in range(6):
        n = 256 if c < 5 else 128
        res = jnp.dot(lhs, band[:, 256 * c : 256 * c + n], preferred_element_type=F32)
        for f in range(2 * c, 2 * c + n // TC):
            o = (f - 2 * c) * TC
            for j in range(16):
                hs[f * SLOTS : f * SLOTS + rows, j * TC : (j + 1) * TC] = res[
                    j * rows : (j + 1) * rows, o : o + TC
                ]


def fit_stage(shift, first_row, own, above, below, sci, band, va, vb, powers, e_out, mom_out, rolled, hs, acc, last):
    row16 = lax.broadcasted_iota(jnp.int32, (1, 16, TC), 1)
    row8 = lax.broadcasted_iota(jnp.int32, (1, 8, TC), 1)
    lane = lax.broadcasted_iota(jnp.int32, (1, TC), 1)
    b = pltpu.roll(below, H, 1)
    mid = jnp.where(row16 < H, above, b)
    end = jnp.where(row8 < 6, b[:, :8], jnp.where(row8 == 6, 1.0, 0.0))
    window_rows(shift, jnp.concatenate([own, mid, end], axis=1), rolled, hs, band)
    sub8 = lax.broadcasted_iota(jnp.int32, (8, 1), 0)
    for c in range(8):
        cols = slice(256 * c, 256 * c + 256)
        oa = jnp.dot(va[...], hs[0:208, cols].astype(BF16), preferred_element_type=F32)
        ob = jnp.dot(vb[...], hs[200:440, cols].astype(BF16), preferred_element_type=F32)
        pieces = []
        for r in range(ROWS):
            pieces += [
                oa[16 * r : 16 * r + 16],
                ob[16 * r : 16 * r + 8],
                jnp.where(sub8 == TARGET - 24, sci[r : r + 1, cols], ob[16 * r + 8 : 16 * r + 16]),
            ]
        e_out[:, cols] = jnp.concatenate(pieces, axis=0).astype(BF16)
    acc[...] = jnp.zeros_like(acc)

    def row_step(r, carry):
        e = e_out[pl.ds(pl.multiple_of(r * 32, 32), 32), :]
        rows = [e]
        for k in range(2):
            p = powers[16 * k : 16 * k + 16, :]
            rows += [e[0:16] * p, e[16:32] * p]
        g = lax.dot_general(
            jnp.concatenate([e] + rows[3:], axis=0),
            jnp.concatenate(rows, axis=0),
            (((1,), (1,)), ((), ())),
            preferred_element_type=F32,
        )
        v = (first_row + r).astype(F32) * (2.0 / 256.0) + (1.0 / 256.0 - 1.0)
        low = g[32:64]
        g = g[0:32]
        last[0, :, 0:96] += low
        last[1, :, 0:96] += low * v
        scale = v
        acc[0, :, 0:96] += g
        for m in range(1, 5):
            acc[m, :, 0:96] += g * scale
            scale = scale * v
        return carry

    last[...] = jnp.zeros_like(last)
    lax.fori_loop(0, ROWS, row_step, 0, unroll=8)
    units = (
        jnp.where(lane < 96, acc[0], pltpu.roll(last[0], 64, 1)),
        jnp.where(lane < 96, acc[1], pltpu.roll(last[1], 64, 1)),
        jnp.where(lane < 96, acc[2], pltpu.roll(last[0], 32, 1)),
        jnp.where(lane < 64, acc[3], pltpu.roll(acc[4], 64, 1)),
    )
    for i, unit in enumerate(units):
        for j in range(4):
            mom_out[4 * i + j] = unit[8 * j : 8 * j + 8]


def unit_of(k, m):
    if m < 2 and k < 4:
        return m, k
    if m == 2:
        return 2, k
    return {(4, 0): (2, 3), (0, 3): (3, 0), (1, 3): (3, 1), (0, 4): (3, 2)}[(k, m)]


def inverse2(m):
    (a, b), (c, d) = m
    r = 1.0 / (a * d - b * c)
    return (d * r, -b * r), (-c * r, a * r)


def times2(x, y):
    return tuple(tuple(x[i][0] * y[0][j] + x[i][1] * y[1][j] for j in range(2)) for i in range(2))


def plus2(x, y, sign):
    return tuple(tuple(x[i][j] + sign * y[i][j] for j in range(2)) for i in range(2))


def factor4(p):
    part = lambda i, j: tuple(tuple(p[2 * i + a][2 * j + b] for b in range(2)) for a in range(2))
    head = inverse2(part(0, 0))
    x = times2(head, part(0, 1))
    low = part(1, 0)
    return head, x, low, inverse2(plus2(part(1, 1), times2(low, x), -1.0))


def solve4(parts, r):
    head, x, low, tail = parts
    y = [head[i][0] * r[0] + head[i][1] * r[1] for i in range(2)]
    z = [r[2 + i] - (low[i][0] * y[0] + low[i][1] * y[1]) for i in range(2)]
    u = [tail[i][0] * z[0] + tail[i][1] * z[1] for i in range(2)]
    return [y[i] - (x[i][0] * u[0] + x[i][1] * u[1]) for i in range(2)] + u


def sweep_panel(mat, zero, q, lane):
    t = q // 4
    top = 32 * q
    base = 32 * (q % 4)
    sub = lax.broadcasted_iota(jnp.int32, (8, TC), 0)
    tiles = [[mat[top + 8 * i : top + 8 * i + 8, TC * h : TC * h + TC] for h in range(2)] for i in range(4)]
    for k in range(0, 28, 4):
        i0, s0, l0 = k // 8, k % 8, base + k
        cols = [
            [jnp.broadcast_to(tiles[i][t][:, l0 + j : l0 + j + 1], (8, TC)) for j in range(4)]
            for i in range(4)
        ]
        whole_cols = [cols[i0][j] + zero for j in range(4)]
        p = [
            [jnp.broadcast_to(whole_cols[j][s0 + i : s0 + i + 1], (8, TC)) for j in range(4)]
            for i in range(4)
        ]
        parts = factor4(p)
        in_lane = (lane >= l0) & (lane < l0 + 4)
        in_row = (sub >= s0) & (sub < s0 + 4)
        rows = []
        for h in range(2):
            r = [jnp.broadcast_to(tiles[i0][h][s0 + j : s0 + j + 1], (8, TC)) for j in range(4)]
            if h == t:
                r = [jnp.where(in_lane, jnp.where(lane == l0 + j, 1.0, 0.0), r[j]) for j in range(4)]
            rows.append(solve4(parts, r))
        for i in range(4):
            c = cols[i]
            if i == i0:
                c = [jnp.where(in_row, jnp.where(sub == s0 + j, -1.0, 0.0), c[j]) for j in range(4)]
            for h in range(2):
                old = tiles[i][h]
                if h == t:
                    old = jnp.where(in_lane, 0.0, old)
                if i == i0:
                    old = jnp.where(in_row, 0.0, old)
                u = rows[h]
                tiles[i][h] = old - ((c[0] * u[0] + c[1] * u[1]) + (c[2] * u[2] + c[3] * u[3]))
    inside = (lane >= base) & (lane < base + 28)
    swept = [[], []]
    for i in range(4):
        for h in range(2):
            f = tiles[i][h]
            if h == t:
                f = jnp.where(inside, -f, f)
            if i == 3:
                f = jnp.where(sub < 4, f, 0.0)
            swept[h].append(f)
    f = jnp.concatenate([jnp.concatenate(swept[h], axis=0) for h in range(2)], axis=1)
    f_hi = f.astype(BF16)
    f = f - f_hi.astype(F32)
    f_mid = f.astype(BF16)
    f_lo = (f - f_mid.astype(F32)).astype(BF16)
    right = jnp.concatenate(
        [f_hi, f_mid, f_hi, f_lo, f_hi, f_mid, jnp.zeros((64, 2 * TC), BF16)], axis=0
    )
    z = jnp.where(inside, mat[top + 32 : 200, TC * t : TC * t + TC], 0.0)
    if base:
        z = pltpu.roll(z, 128 - base, 1)
    z = z + pltpu.roll(z, 32, 1)
    z = z + pltpu.roll(z, 64, 1)
    z_hi = z.astype(BF16).astype(F32)
    z = z - z_hi
    z_mid = z.astype(BF16).astype(F32)
    z_lo = z - z_mid
    slot = lax.shift_right_logical(lane, 5)
    left = jnp.concatenate(
        [
            jnp.where(slot == 2, z_mid, z_hi),
            jnp.where(slot == 0, z_lo, jnp.where(slot == 1, z_mid, 0.0)),
        ],
        axis=1,
    ).astype(BF16)
    change = jnp.dot(left, right, preferred_element_type=F32)
    for h in range(2):
        old = mat[top + 32 : 200, TC * h : TC * h + TC]
        if h == t:
            old = jnp.where(inside, 0.0, old)
        mat[top + 32 : 200, TC * h : TC * h + TC] = old - change[:, TC * h : TC * h + TC]


def apply_stage(order, first_row, moms, e_ref, sci, upow, out, mat, fx):
    units = [jnp.concatenate([moms[4 * i + j] for j in range(4)], axis=0) for i in range(4)]
    lane = lax.broadcasted_iota(jnp.int32, (1, TC), 1)
    row = lax.broadcasted_iota(jnp.int32, (32, 1), 0)
    degree = lambda q: 0 if q == 0 else (1 if q < 3 else 2)

    def col_active(t):
        q = lax.shift_right_logical(lane, 5) + 4 * t
        deg = jnp.where(q >= 1, 1, 0) + jnp.where(q >= 3, 1, 0)
        return (deg <= order) | (lax.bitwise_and(lane, 31) == ONES)

    for q in range(6):
        row_on = (degree(q) <= order) | (row == ONES)
        for t in range(2):
            block = jnp.zeros((32, TC), F32)
            for s in range(4 if t == 0 else 2):
                p = 4 * t + s
                i, k = unit_of(mono[q][0] + mono[p][0], mono[q][1] + mono[p][1])
                piece = units[i]
                if s != k:
                    piece = pltpu.roll(piece, (32 * (s - k)) % 128, 1)
                block = jnp.where(lax.shift_right_logical(lane, 5) == s, piece, block)
            both = row_on & col_active(t)
            block = jnp.where(both, block, 0.0)
            if t == q // 4:
                diag = lane == row + 32 * (q % 4)
                block = jnp.where(diag, jnp.where(both, block, 1.0) * (1.0 + ridge), block)
            mat[32 * q : 32 * q + 32, TC * t : TC * t + TC] = block
            if q == 0:
                mat[192:200, TC * t : TC * t + TC] = jnp.where(col_active(t), block[24:32], 0.0)
    fx[...] = jnp.zeros_like(fx)
    zero = fx[...]
    for q in range(6):
        sweep_panel(mat, zero, q, lane)
    coef = []
    for q in range(6):
        z = mat[192:200, TC * (q // 4) : TC * (q // 4) + TC]
        z = jnp.broadcast_to(z[TARGET - 24 : TARGET - 23], (8, TC))
        if q % 4:
            z = pltpu.roll(z, 128 - 32 * (q % 4), 1)
        z = jnp.where(lane < 28, z, 0.0)
        z = z + pltpu.roll(z, 32, 1)
        z = z + pltpu.roll(z, 64, 1)
        coef.append(jnp.concatenate([z, z], axis=0))
    row16 = lax.broadcasted_iota(jnp.int32, (16, 1), 0)
    v = (first_row + row16).astype(F32) * (2.0 / 256.0) + (1.0 / 256.0 - 1.0)
    parts = (coef[0] + v * (coef[2] + v * coef[5]), coef[1] + v * coef[4], coef[3])
    his, los = [], []
    for p in parts:
        wide_p = jnp.concatenate(
            [jnp.where(row16 == 4 * n + lax.shift_right_logical(lane, 5), p, 0.0) for n in range(4)],
            axis=1,
        )
        h = wide_p.astype(BF16)
        his.append(h)
        los.append((wide_p - h.astype(F32)).astype(BF16))
    res = jnp.dot(jnp.concatenate(his + los, axis=0), e_ref[...], preferred_element_type=F32)
    t0, t1, t2 = (res[16 * i : 16 * i + 16] + res[48 + 16 * i : 64 + 16 * i] for i in range(3))
    u = jnp.concatenate([upow[...]] * 2, axis=0)
    out[...] = sci[...] - (t0 + u * (t1 + u * t2))


MESH = pl.DeviceIdType.MESH


def whole_kernel(
    ccds, strips, shift_h, order_h, source_h, slot_h, store_h, sci_h, band_h, va_h, vb_h, upow_h, powers_h, out,
    sent, got, sent2, got2, sci, band, va, vb, upow, powers, e, rolled, hs, acc, last, mom, parts, part, totals, mat, fx,
    shift, order, source, slot, store, local, send, recv, send2, recv2, s1, r1, s2, r2,
):
    ccd = lax.axis_index("ccd")
    strip = lax.axis_index("strip")
    count = ccds * strips
    me = ccd * strips + strip
    barrier = pltpu.get_barrier_semaphore()
    loads = [
        pltpu.make_async_copy(h, v, local.at[i])
        for i, (h, v) in enumerate(
            ((source_h, source), (slot_h, slot), (store_h, store), (shift_h, shift), (order_h, order),
             (band_h, band), (va_h, va), (vb_h, vb), (upow_h, upow), (powers_h, powers), (sci_h, sci))
        )
    ]

    hops = (0, 1, 2, 1)
    turn = lambda i, k: lax.rem(i + k, 4)
    shifts = [(y, c, z, x) for y in range(4) for c in range(2) for z in range(4) for x in range(4)]
    shifts.sort(key=lambda o: -(hops[o[0]] + hops[o[2]] + hops[o[3]] + 0.5 * o[1]))
    rows = [[turn(ccd // 2, y) * 2 + lax.rem(ccd + c, 2) for c in range(2)] for y in range(4)]
    cells = [[turn(strip // 4, z) * 4 + turn(lax.rem(strip, 4), x) for x in range(4)] for z in range(4)]

    def each_peer(act):
        for y, c, z, x in shifts[:-1]:
            act(rows[y][c], cells[z][x])

    each_peer(
        lambda c, k: pl.semaphore_signal(barrier, inc=1, device_id=(c, k), device_id_type=MESH)
    )
    for load in loads:
        load.start()
    for load in loads[:3]:
        load.wait()

    tiles = source.shape[0]
    flat = tiles * ROWS
    sheet = jnp.concatenate([store[...].reshape(flat, TC), jnp.zeros((-flat % TC, TC), F32)], axis=0)
    near = sheet.shape[0] // TC
    for i in range(near):
        sent[pl.ds(i, count, stride=near), :] = jnp.transpose(sheet[TC * i : TC * i + TC])
    for i in range(near):
        got[pl.ds(near * me + i, 1), :] = sent[pl.ds(near * me + i, 1), :]
    pl.semaphore_wait(barrier, count - 1)

    def send_all(src, dst, size, done, arrived):
        each_peer(
            lambda c, k: pltpu.make_async_remote_copy(
                src_ref=src.at[pl.ds(size * (c * strips + k), size)],
                dst_ref=dst.at[pl.ds(size * me, size)],
                send_sem=done,
                recv_sem=arrived,
                device_id=(c, k),
                device_id_type=MESH,
            ).start()
        )

    send_all(sent, got, near, send, recv)
    rest = got.at[pl.ds(0, near * (count - 1))]
    pltpu.make_async_copy(rest, rest, recv).wait()
    sheet = jnp.concatenate(
        [jnp.transpose(got[pl.ds(i, count, stride=near), :]) for i in range(near)], axis=0
    )
    found = []
    for t in range(tiles):
        owner = jnp.broadcast_to(source[t : t + 1, :], (8, count))
        place = jnp.broadcast_to(slot[t : t + 1, :], (8, count))
        for h in range(0, ROWS, 8):
            tile = jnp.zeros((8, count), F32)
            for p in range(tiles):
                tile = jnp.where(
                    place == p,
                    jnp.take_along_axis(
                        sheet[ROWS * p + h : ROWS * p + h + 8], owner, axis=1, mode="promise_in_bounds"
                    ),
                    tile,
                )
            found.append(tile)
    mine = jnp.concatenate(found, axis=0)
    up = pack_rows(pltpu.roll(pltpu.roll(mine, 1, 1).reshape(tiles, ROWS, count), 16 - 5, 1))
    down = pack_rows(pltpu.roll(mine, count - 1, 1).reshape(tiles, ROWS, count))
    half = tiles // 2 * 24
    sheet = jnp.concatenate(
        [
            mine,
            up.reshape(half, count),
            down.reshape(half, count),
            jnp.zeros((-(flat + 2 * half) % TC, count), F32),
        ],
        axis=0,
    )
    far = sheet.shape[0] // TC
    for i in range(far):
        sent2[pl.ds(i, count, stride=far), :] = jnp.transpose(sheet[TC * i : TC * i + TC])
    send_all(sent2, got2, far, send2, recv2)
    for i in range(far):
        got2[pl.ds(far * me + i, 1), :] = sent2[pl.ds(far * me + i, 1), :]
    for load in loads[3:]:
        load.wait()
    rest2 = got2.at[pl.ds(0, far * (count - 1))]
    pltpu.make_async_copy(rest2, rest2, recv2).wait()
    sheet = jnp.concatenate(
        [jnp.transpose(got2[pl.ds(i, count, stride=far), :]) for i in range(far)], axis=0
    )
    own = sheet[:flat].reshape(tiles, ROWS, TC)
    above = unpack_rows(sheet[flat : flat + half].reshape(tiles // 2, 24, TC))
    below = unpack_rows(sheet[flat + half : flat + 2 * half].reshape(tiles // 2, 24, TC))
    above = jnp.where(strip > 0, above, 0.0)
    below = jnp.where(strip < strips - 1, below, 0.0)
    first_row = strip * ROWS
    fit_stage(shift[0], first_row, own, above, below, sci, band, va, vb, powers, e, mom, rolled, hs, acc, last)
    peers = [(ccd, cells[z][x]) for y, c, z, x in shifts[:-1] if y == 0 and c == 0]
    for to in peers:
        pltpu.make_async_remote_copy(
            src_ref=mom.at[to[1]],
            dst_ref=parts.at[strip],
            send_sem=s1,
            recv_sem=r1,
            device_id=to,
            device_id_type=MESH,
        ).start()
    parts[strip] = mom[strip]
    few = parts.at[pl.ds(0, strips - 1)]
    pltpu.make_async_copy(few, few, r1).wait()
    total = parts[0]
    for i in range(1, strips):
        total = total + parts[i]
    part[...] = total
    for to in peers:
        pltpu.make_async_remote_copy(
            src_ref=part,
            dst_ref=totals.at[strip],
            send_sem=s2,
            recv_sem=r2,
            device_id=to,
            device_id_type=MESH,
        ).start()
    totals[strip] = total
    pltpu.make_async_copy(few, few, r2).wait()
    apply_stage(order[0], first_row, totals, e, sci, upow, out, mat, fx)
    pltpu.make_async_copy(rest, rest, send).wait()
    pltpu.make_async_copy(rest2, rest2, send2).wait()
    pltpu.make_async_copy(few, few, s1).wait()
    pltpu.make_async_copy(few, few, s2).wait()


VM = pl.BlockSpec(memory_space=pltpu.VMEM)
SM = pl.BlockSpec(memory_space=pltpu.SMEM)
ANY = pl.BlockSpec(memory_space=pl.ANY)
LIMIT = 60 * 1024 * 1024


def whole(shift, order, source, slot, store, sci, ccds, strips):
    count = ccds * strips
    tiles = source.shape[0]
    near = -(-tiles * ROWS // TC)
    far = -(-(tiles * ROWS + tiles * 24) // TC)
    tables = [band_matrix(), *vertical_matrices(), column_rows(), column_factors()]
    blocks = pltpu.VMEM((strips, 128 // strips, TC), F32)
    dma = pltpu.SemaphoreType.DMA
    return pl.pallas_call(
        lambda *refs: whole_kernel(ccds, strips, *refs),
        out_shape=pltpu.VMEM((ROWS, COLS), F32),
        in_specs=[ANY] * 11,
        out_specs=VM,
        scratch_shapes=[
            pltpu.VMEM((near * count, TC), F32),
            pltpu.VMEM((near * count, TC), F32),
            pltpu.VMEM((far * count, TC), F32),
            pltpu.VMEM((far * count, TC), F32),
            pltpu.VMEM((ROWS, COLS), F32),
            *[pltpu.VMEM(x.shape, x.dtype) for x in tables],
            pltpu.VMEM((ROWS * 32, COLS), BF16),
            pltpu.VMEM((tiles + 1, SLOTS, TC), F32),
            pltpu.VMEM((440, COLS), F32),
            pltpu.VMEM((5, 32, TC), F32),
            pltpu.VMEM((2, 32, TC), F32),
            blocks,
            blocks,
            pltpu.VMEM((128 // strips, TC), F32),
            blocks,
            pltpu.VMEM((200, 2 * TC), F32),
            pltpu.VMEM((8, TC), F32),
            pltpu.SMEM((1,), jnp.int32),
            pltpu.SMEM((1,), jnp.int32),
            pltpu.VMEM(source.shape, jnp.int32),
            pltpu.VMEM(source.shape, jnp.int32),
            pltpu.VMEM(store.shape, F32),
            dma((11,)),
            dma,
            dma,
            dma,
            dma,
            dma,
            dma,
            dma,
            dma,
        ],
        compiler_params=pltpu.CompilerParams(
            collective_id=0, has_side_effects=True, vmem_limit_bytes=LIMIT
        ),
        name="whole",
    )(shift, order, source, slot, store, sci, *[jnp.asarray(x) for x in tables])


def body(tile_store, tile_source, tile_slot, shift_cols, spatial_order, science):
    strips = lax.axis_size("strip")
    return whole(
        shift_cols, spatial_order, tile_source.T, tile_slot.T, tile_store, science,
        lax.axis_size("ccd"), strips,
    )


def solution(mesh):
    placed = (
        P(("ccd", "strip"), None, None),
        P(),
        P(),
        P("ccd"),
        P("ccd"),
        P(("ccd", "strip"), None),
    )
    return jax.shard_map(
        body, mesh=mesh, in_specs=placed, out_specs=P(("ccd", "strip"), None), check_vma=False
    )
```
